256 devices in a mesh: dp: 32 (over y, x, core), tsp: 8 (over z).
Axes of the slice: x: 4, y: 4, z: 8, core: 2. Of those that a mesh axis runs over, the one named last changes fastest.
Arguments:
- tokens: bfloat16 [65536, 8192], P('dp', 'tsp'), may hold values from -6 to 6
- cotangent: bfloat16 [65536, 1024], P('dp', 'tsp'), may hold values from -6 to 6
- frozen_key_weight: bfloat16 [8192, 1024], P('tsp'), may hold values from -0.1875 to 0.1875
- adapter_down_weight: bfloat16 [64, 64, 8192], P('dp', None, 'tsp'), may hold values from -0.0625 to 0.0625
- adapter_up_weight: bfloat16 [64, 64, 1024], P('dp', None, 'tsp'), may hold values from -0.1875 to 0.1875
- adapter_place_table: int32 [64], replicated, may hold values from 0 to 63, as said below
- segment_adapter: int32 [512], P('dp'), may hold values from 0 to 63, as said below
- segment_live_count: int32 [512], P('dp'), may hold values from 1 to 128, as said below
Outputs:
- token_gradient: bfloat16 [65536, 8192], P('dp', 'tsp')
- down_grad: float32 [64, 64, 8192], P('dp', None, 'tsp')
- up_grad: float32 [64, 64, 1024], P('dp', None, 'tsp')
The draws below stay inside these ranges and needn't reach their ends.
Inputs may be any that keep to these rules, and one draw needn't show every extreme that they name: A permutation: adapter a is held at place adapter_place_table[a], that is by the dp index adapter_place_table[a] // 2 as its entry adapter_place_table[a] % 2; the adapters' arrays and gradients are indexed by place. `segment_adapter`: the 16 segments of one dp index name at most one adapter held by any one dp index; an adapter may be named by several of them. `segment_live_count`: the live rows stand at the start of each segment; on every dp index some segment is full.
All inputs are finite; a program needn't handle non-finite values.
Results may differ from the reference program's by a relative error of at most 0.0034.
Values may be sent and summed in bfloat16 or wider, within the bound.
A program may use at most 128 MiB of HBM per device.

```python
import jax
import jax.numpy as jnp
from jax import lax

MODEL_WIDTH = 8192
KEY_WIDTH = 1024
ADAPTER_RANKS = 64
SEGMENT_ROWS = 128
ADAPT_DEV = 2
SEG_DEV = 16
ADAPTER_TOTAL = 64
TOKENS = 65536
N_DP = 32


def storage_order(key):
    return jax.random.permutation(jax.random.fold_in(key, 11), ADAPTER_TOTAL).astype(jnp.int32)


def draw_adapter_place_table(key, part):
    return storage_order(key)


def draw_segment_adapter(key, part):
    order = storage_order(key)
    inverse = jnp.argsort(order, stable=True).astype(jnp.int32)
    distinct = min(N_DP, SEG_DEV - SEG_DEV // 8)
    scores = jax.random.randint(jax.random.fold_in(key, 21), (N_DP, N_DP), 0, 1 << 20) * N_DP + jnp.arange(N_DP, dtype=jnp.int32)[None, :]
    owners = jnp.argsort(scores, axis=1, stable=True)[:, :distinct].astype(jnp.int32)
    entries = jax.random.randint(jax.random.fold_in(key, 22), (N_DP, distinct), 0, ADAPT_DEV)
    chosen = owners * ADAPT_DEV + entries
    extra = jax.random.randint(jax.random.fold_in(key, 23), (N_DP, SEG_DEV - distinct), 0, distinct)
    firsts = jnp.broadcast_to(jnp.arange(distinct, dtype=jnp.int32)[None, :], (N_DP, distinct))
    picks = jnp.concatenate([firsts, extra.astype(jnp.int32)], axis=1)
    positions = jnp.take_along_axis(chosen, picks, axis=1)
    shuffle = jax.random.randint(jax.random.fold_in(key, 24), (N_DP, SEG_DEV), 0, 1 << 20) * SEG_DEV + jnp.arange(SEG_DEV, dtype=jnp.int32)[None, :]
    reorder = jnp.argsort(shuffle, axis=1, stable=True)
    positions = jnp.take_along_axis(positions, reorder, axis=1)
    return inverse[positions.reshape(-1)].astype(jnp.int32)


def draw_segment_live_count(key, part):
    counts = jax.random.randint(jax.random.fold_in(key, 31), (N_DP, SEG_DEV), 1, SEGMENT_ROWS + 1)
    full_at = jax.random.randint(jax.random.fold_in(key, 32), (N_DP, 1), 0, SEG_DEV)
    counts = jnp.where(jnp.arange(SEG_DEV, dtype=jnp.int32)[None, :] == full_at, SEGMENT_ROWS, counts)
    return counts.reshape(-1).astype(jnp.int32)


def levels(stream_key, shape, shards, smallest, high):
    factor_of = 1.0
    for dim, shards_of in shards:
        heights = jax.random.uniform(jax.random.fold_in(jax.random.fold_in(stream_key, 6), dim), (shards_of,), jnp.float32, smallest / len(shards), high / len(shards))
        factor_of = factor_of * jnp.repeat(jnp.exp(heights), shape[dim] // shards_of).reshape((-1,) + (1,) * (len(shape) - 1 - dim))
    return factor_of


def centred(stream_key, dims, spread, most, pieces=(), kind=jnp.bfloat16):
    result = jax.random.normal(stream_key, dims, jnp.float32) * spread
    if len(pieces) > 0:
        result = levels(stream_key, dims, pieces, -0.22, 0.18) * result
    return jnp.clip(result, min=-most, max=most).astype(kind)


def setup_inputs(seed: int = 0) -> dict:
    key_list = jax.random.split(jax.random.key(seed), 9)
    tokens = centred(key_list[0], (TOKENS, MODEL_WIDTH), 1.0, 6.0, ((0, 32), (1, 8)))
    cotangent = centred(key_list[1], (TOKENS, KEY_WIDTH), 1.0, 6.0, ((0, 32), (1, 8)))
    frozen_key_weight = centred(key_list[2], (MODEL_WIDTH, KEY_WIDTH), KEY_WIDTH ** -0.5, 0.1875, ((0, 8),))
    adapter_down_weight = centred(key_list[3], (ADAPTER_TOTAL, ADAPTER_RANKS, MODEL_WIDTH), MODEL_WIDTH ** -0.5, 0.0625, ((0, 32), (2, 8)))
    adapter_up_weight = centred(key_list[4], (ADAPTER_TOTAL, ADAPTER_RANKS, KEY_WIDTH), KEY_WIDTH ** -0.5, 0.1875, ((0, 32), (2, 8)))
    adapter_place_table = draw_adapter_place_table(jax.random.fold_in(key_list[8], 71), 0)
    segment_adapter = draw_segment_adapter(jax.random.fold_in(key_list[8], 71), 0)
    segment_live_count = draw_segment_live_count(jax.random.fold_in(key_list[8], 71), 0)
    return dict(tokens=tokens, cotangent=cotangent, frozen_key_weight=frozen_key_weight, adapter_down_weight=adapter_down_weight, adapter_up_weight=adapter_up_weight, adapter_place_table=adapter_place_table, segment_adapter=segment_adapter, segment_live_count=segment_live_count)


ADAPTER_SCALE = 2.0


def reference(tokens, cotangent, frozen_key_weight, adapter_down_weight, adapter_up_weight, adapter_place_table, segment_adapter, segment_live_count):
    tok_block = SEGMENT_ROWS * SEG_DEV

    def one_block(carry, block):
        down_total, up_total = carry
        first = (block * tok_block).astype(jnp.int32)
        rows_x = lax.dynamic_slice_in_dim(tokens, first, tok_block, 0)
        rows_dy = lax.dynamic_slice_in_dim(cotangent, first, tok_block, 0)
        seg_first = (block * SEG_DEV).astype(jnp.int32)
        idents = lax.dynamic_slice_in_dim(segment_adapter, seg_first, SEG_DEV, 0)
        counts = lax.dynamic_slice_in_dim(segment_live_count, seg_first, SEG_DEV, 0)
        adapter_places = adapter_place_table[idents].astype(jnp.int32)
        segment_down_weight = adapter_down_weight[adapter_places].astype(jnp.float32)
        segment_up_weight = adapter_up_weight[adapter_places].astype(jnp.float32)
        live_mask = (jnp.arange(SEGMENT_ROWS, dtype=jnp.int32)[None, :] < counts[:, None]).astype(jnp.float32)
        input_rows = rows_x.reshape(SEG_DEV, SEGMENT_ROWS, MODEL_WIDTH).astype(jnp.float32)
        incoming_gradient = rows_dy.reshape(SEG_DEV, SEGMENT_ROWS, KEY_WIDTH).astype(jnp.float32)
        reduced_rows = (jnp.einsum("gtd,grd->gtr", input_rows, segment_down_weight) * live_mask[:, :, None]).astype(jnp.bfloat16)
        gathered_weights = (jnp.einsum("gtk,grk->gtr", incoming_gradient, segment_up_weight) * live_mask[:, :, None]).astype(jnp.bfloat16)
        frozen_output = jnp.dot(rows_dy, frozen_key_weight.T, preferred_element_type=jnp.float32).reshape(SEG_DEV, SEGMENT_ROWS, MODEL_WIDTH)
        adapter_output = jnp.einsum("wks,wsx->wkx", gathered_weights.astype(jnp.float32), segment_down_weight)
        token_gradient = ((frozen_output + ADAPTER_SCALE * adapter_output) * live_mask[:, :, None]).astype(jnp.bfloat16)
        segment_down_gradient = jnp.einsum("upf,upb->ufb", gathered_weights.astype(jnp.float32), input_rows) * (ADAPTER_SCALE / SEGMENT_ROWS)
        segment_up_gradient = jnp.einsum("ija,ijn->ian", reduced_rows.astype(jnp.float32), incoming_gradient) * (ADAPTER_SCALE / SEGMENT_ROWS)
        down_total = down_total.at[adapter_places].add(segment_down_gradient)
        up_total = up_total.at[adapter_places].add(segment_up_gradient)
        return (down_total, up_total), token_gradient.reshape(tok_block, MODEL_WIDTH)

    start = (jnp.zeros((ADAPTER_TOTAL, ADAPTER_RANKS, MODEL_WIDTH), jnp.float32), jnp.zeros((ADAPTER_TOTAL, ADAPTER_RANKS, KEY_WIDTH), jnp.float32))
    (down_grad, up_grad), blocks = lax.scan(one_block, start, jnp.arange(N_DP, dtype=jnp.int32))
    return blocks.reshape(TOKENS, MODEL_WIDTH), down_grad, up_grad
```

```python
import jax
import jax.numpy as jnp
from jax import lax
from jax.experimental import pallas as pl
from jax.experimental.pallas import tpu as pltpu
from jax.sharding import PartitionSpec as P

ADAPTER_SCALE = 2.0
MESH = pl.DeviceIdType.MESH
SIDE = 4
RING = 8
HALF = 32
VMEM_LIMIT = 60 * 1024 * 1024


def lookup(idents, mapping):
    matches = idents[:, None] == jnp.arange(mapping.shape[0], dtype=jnp.int32)[None, :]
    return jnp.sum(jnp.where(matches, mapping[None, :], 0), axis=1)


def place_in_plane():
    me = lax.axis_index("dp")
    core = lax.rem(me, 2)
    chip = lax.div(me, 2)
    return me, core, lax.div(chip, SIDE), lax.rem(chip, SIDE)


def side(v):
    return lax.rem(v + 2 * SIDE, SIDE)


def device_of(y, x, core):
    return (side(y) * SIDE + side(x)) * 2 + core


def greet(devices):
    barrier = pltpu.get_barrier_semaphore()
    for device in devices:
        pl.semaphore_signal(barrier, inc=1, device_id=device, device_id_type=MESH)
    pl.semaphore_wait(barrier, len(devices))


def plane_neighbours():
    me, core, y, x = place_in_plane()
    z = lax.axis_index("tsp")
    return [
        (me + 1 - 2 * core, z),
        (device_of(y, x + 1, core), z),
        (device_of(y, x - 1, core), z),
        (device_of(y + 1, x, core), z),
        (device_of(y - 1, x, core), z),
    ]


def gather_kernel(mine, out, local_sem, send_sem, recv_sem):
    me, core, y, x = place_in_plane()
    z = lax.axis_index("tsp")
    peer = me + 1 - 2 * core
    greet(plane_neighbours())
    ids = {}
    sends = []

    def index_of(key):
        return ids.setdefault(key, len(ids))

    def send(ref, device, key):
        k = index_of(key)
        copy = pltpu.make_async_remote_copy(
            ref, ref, send_sem.at[k], recv_sem.at[k], (device, z), MESH
        )
        copy.start()
        sends.append(copy)

    def arrived(ref, key):
        k = index_of(key)
        pltpu.make_async_remote_copy(
            ref, ref, send_sem.at[k], recv_sem.at[k], (peer, z), MESH
        ).wait_recv()

    def owner(tau, di, dj):
        return device_of(y + dj, x + di, tau) if tau == 0 else device_of(y + di, x + dj, tau)

    def near(tau, di, dj):
        return device_of(y + dj, x + di, core) if tau == 0 else device_of(y + di, x + dj, core)

    def block(tau, di, dj, half):
        return out.at[pl.ds(2 * owner(tau, di, dj), 2), half]

    def unit(tau, di, dj, e):
        return out.at[2 * owner(tau, di, dj) + e, core]

    def swap(tau, di, dj):
        send(block(tau, di, dj, core), peer, ("swap", tau, di, dj))

    local = pltpu.make_async_copy(mine, out.at[pl.ds(2 * me, 2)], local_sem)
    local.start()
    k = index_of("own")
    own = pltpu.make_async_remote_copy(
        mine, out.at[pl.ds(2 * me, 2)], send_sem.at[k], recv_sem.at[k], (peer, z), MESH
    )
    own.start()
    sends.append(own)
    local.wait()
    pltpu.make_async_remote_copy(
        mine, out.at[pl.ds(2 * peer, 2)], send_sem.at[k], recv_sem.at[k], (peer, z), MESH
    ).wait_recv()
    for tau in (0, 1):
        for s in (1, -1):
            send(block(tau, 0, 0, core), near(tau, s, 0), ("one", tau, s))
    for tau in (0, 1):
        for s in (1, -1):
            send(block(tau, 0, 0, core), near(tau, 0, s), ("two", tau, 0, s))
    for tau in (0, 1):
        for s in (1, -1):
            arrived(block(tau, -s, 0, core), ("one", tau, s))
            send(unit(tau, -s, 0, 0 if s == 1 else 1), near(tau, s, 0), ("onward", tau, s))
    for tau in (0, 1):
        for s in (1, -1):
            for t in (1, -1):
                send(block(tau, -s, 0, core), near(tau, 0, t), ("two", tau, -s, t))
            swap(tau, -s, 0)
    for tau in (0, 1):
        arrived(unit(tau, 2, 0, 0), ("onward", tau, 1))
        arrived(unit(tau, 2, 0, 1), ("onward", tau, -1))
        for t in (1, -1):
            send(block(tau, 2, 0, core), near(tau, 0, t), ("two", tau, 2, t))
        swap(tau, 2, 0)
    for di in (0, -1, 1, 2):
        for tau in (0, 1):
            for t in (1, -1):
                arrived(block(tau, di, -t, core), ("two", tau, di, t))
                send(
                    unit(tau, di, -t, 0 if t == 1 else 1),
                    near(tau, 0, t),
                    ("last", tau, di, t),
                )
                swap(tau, di, -t)
    for di in (0, -1, 1, 2):
        for tau in (0, 1):
            arrived(unit(tau, di, 2, 0), ("last", tau, di, 1))
            arrived(unit(tau, di, 2, 1), ("last", tau, di, -1))
            swap(tau, di, 2)
    for copy in sends:
        copy.wait_send()
    for tau in (0, 1):
        for di in (0, -1, 1, 2):
            for dj in (0, -1, 1, 2):
                if di or dj:
                    arrived(block(tau, di, dj, 1 - core), ("swap", tau, di, dj))


def gather_maps(mine):
    places, width = 2 * lax.axis_size("dp"), mine.shape[-1]
    return pl.pallas_call(
        gather_kernel,
        out_shape=jax.ShapeDtypeStruct((places, 2, HALF, width), mine.dtype),
        in_specs=[pl.BlockSpec(memory_space=pltpu.VMEM)],
        out_specs=pl.BlockSpec(memory_space=pl.ANY),
        scratch_shapes=[
            pltpu.SemaphoreType.DMA,
            pltpu.SemaphoreType.DMA((71,)),
            pltpu.SemaphoreType.DMA((71,)),
        ],
        compiler_params=pltpu.CompilerParams(
            collective_id=0, has_side_effects=True, vmem_limit_bytes=8 * 1024 * 1024
        ),
        name="gather_maps",
    )(mine)


def project_kernel(places, live, tokens, cotangent, maps, out):
    g = pl.program_id(0)
    width = tokens.shape[1]
    both = maps[0]
    contract = (((1,), (1,)), ((), ()))
    lowered = lax.dot_general(
        tokens[...], both[:, :width], contract, preferred_element_type=jnp.float32
    )
    pulled = lax.dot_general(
        cotangent[...], both[:, width:], contract, preferred_element_type=jnp.float32
    )
    terms = jnp.concatenate([lowered, pulled], axis=1)
    row = lax.broadcasted_iota(jnp.int32, terms.shape, 0)
    out[0] = jnp.where(row < live[g], terms, 0.0)


def project(places, live, tokens, cotangent, maps):
    segments = places.shape[0]
    rows = tokens.shape[0] // segments
    width, key = tokens.shape[1], cotangent.shape[1]
    ranks = maps.shape[1]
    return pl.pallas_call(
        project_kernel,
        out_shape=jax.ShapeDtypeStruct((segments, rows, 2 * ranks), jnp.float32),
        grid_spec=pltpu.PrefetchScalarGridSpec(
            num_scalar_prefetch=2,
            grid=(segments,),
            in_specs=[
                pl.BlockSpec((rows, width), lambda g, p, n: (g, 0)),
                pl.BlockSpec((rows, key), lambda g, p, n: (g, 0)),
                pl.BlockSpec((1, ranks, width + key), lambda g, p, n: (p[g], 0, 0)),
            ],
            out_specs=pl.BlockSpec((1, rows, 2 * ranks), lambda g, p, n: (g, 0, 0)),
        ),
        name="project",
    )(places, live, tokens, cotangent, maps)


def sum_kernel(part, out, held, sent, send_sem, recv_sem, out_send_sem, out_recv_sem):
    i = lax.axis_index("tsp")
    dp = lax.axis_index("dp")

    def at(v):
        return lax.rem(v + 2 * RING, RING)

    greet([(dp, at(i + 1)), (dp, at(i - 1))])
    copies = []

    def send(src, d, step, u):
        copy = pltpu.make_async_remote_copy(
            src,
            held.at[d, step, u],
            send_sem.at[d, step, u],
            recv_sem.at[d, step, u],
            (dp, at(i + 1 - 2 * d)),
            MESH,
        )
        copy.start()
        copies.append(copy)

    def arrived(d, step, u):
        pltpu.make_async_remote_copy(
            held.at[d, step, u],
            held.at[d, step, u],
            send_sem.at[d, step, u],
            recv_sem.at[d, step, u],
            (dp, at(i + 1 - 2 * d)),
            MESH,
        ).wait_recv()

    for d in (0, 1):
        send(part.at[2 * at(i + 4) + d], d, 0, d)
    for d in (0, 1):
        s = 1 - 2 * d
        send(part.at[2 * at(i + 3 * s) + 1 - d], d, 1, 1 - d)
    for step in (1, 2, 3):
        for v in (0, 1):
            for d in (0, 1):
                u = v if d == 0 else 1 - v
                if step == 1 and v == 1:
                    continue
                s = 1 - 2 * d
                arrived(d, step - 1, u)
                sent[d, step, u] = held[d, step - 1, u] + part[2 * at(i + s * (4 - step)) + u]
                send(sent.at[d, step, u], d, step, u)
    for u in (0, 1):
        arrived(0, 3, u)
        arrived(1, 3, u)
        out[2 * i + u] = (part[2 * i + u] + held[0, 3, u] + held[1, 3, u]).astype(out.dtype)

    def pass_on(chunk, u, d, step):
        ref = out.at[pl.ds(2 * at(chunk), 2)] if u is None else out.at[2 * at(chunk) + u]
        copy = pltpu.make_async_remote_copy(
            ref,
            ref,
            out_send_sem.at[d, step],
            out_recv_sem.at[d, step],
            (dp, at(i + 1 - 2 * d)),
            MESH,
        )
        return copy

    for d in (0, 1):
        copy = pass_on(i, None, d, 0)
        copy.start()
        copies.append(copy)
    for step in (1, 2, 3):
        for d in (0, 1):
            s = 1 - 2 * d
            pass_on(i - step * s, None, d, step - 1).wait_recv()
            copy = pass_on(i - step * s, d if step == 3 else None, d, step)
            copy.start()
            copies.append(copy)
    for d in (0, 1):
        pass_on(i + 4, d, d, 3).wait_recv()
    for copy in copies:
        copy.wait_send()


def sum_over_features(part):
    segments, rows, terms = part.shape
    return pl.pallas_call(
        sum_kernel,
        out_shape=jax.ShapeDtypeStruct(part.shape, jnp.bfloat16),
        in_specs=[pl.BlockSpec(memory_space=pltpu.VMEM)],
        out_specs=pl.BlockSpec(memory_space=pltpu.VMEM),
        scratch_shapes=[
            pltpu.VMEM((2, 4, 2, rows, terms), jnp.float32),
            pltpu.VMEM((2, 4, 2, rows, terms), jnp.float32),
            pltpu.SemaphoreType.DMA((2, 4, 2)),
            pltpu.SemaphoreType.DMA((2, 4, 2)),
            pltpu.SemaphoreType.DMA((2, 4)),
            pltpu.SemaphoreType.DMA((2, 4)),
        ],
        compiler_params=pltpu.CompilerParams(collective_id=1, has_side_effects=True),
        name="sum_over_features",
    )(part)


def slots_kernel(owners, summed, tokens, cotangent, out, total):
    g = pl.program_id(0)
    width = tokens.shape[1]
    rows = tokens.shape[0]
    ranks = summed.shape[2] // 2

    @pl.when(g == 0)
    def _():
        total[...] = jnp.zeros_like(total)

    contract = (((0,), (0,)), ((), ()))
    both = summed[0]
    down = lax.dot_general(
        both[:, ranks:], tokens[...], contract, preferred_element_type=jnp.float32
    )
    up = lax.dot_general(
        both[:, :ranks], cotangent[...], contract, preferred_element_type=jnp.float32
    )
    slot = owners[g]
    total[slot, :, :width] += down
    total[slot, :, width:] += up

    @pl.when(g == pl.num_programs(0) - 1)
    def _():
        @pl.loop(0, total.shape[0])
        def _(o):
            out[o] = (total[o] * (ADAPTER_SCALE / rows)).astype(out.dtype)


def slot_gradients(owners, summed, tokens, cotangent):
    segments, rows, terms = summed.shape
    width, key = tokens.shape[1], cotangent.shape[1]
    shape = (lax.axis_size("dp"), terms // 2, width + key)
    return pl.pallas_call(
        slots_kernel,
        out_shape=jax.ShapeDtypeStruct(shape, jnp.bfloat16),
        grid_spec=pltpu.PrefetchScalarGridSpec(
            num_scalar_prefetch=1,
            grid=(segments,),
            in_specs=[
                pl.BlockSpec((1, rows, terms), lambda g, o: (g, 0, 0)),
                pl.BlockSpec((rows, width), lambda g, o: (g, 0)),
                pl.BlockSpec((rows, key), lambda g, o: (g, 0)),
            ],
            out_specs=pl.BlockSpec(shape, lambda g, o: (0, 0, 0)),
            scratch_shapes=[pltpu.VMEM(shape, jnp.float32)],
        ),
        name="slot_gradients",
    )(owners, summed, tokens, cotangent)


def scatter_kernel(
    slots, entry, out,
    peer_slots, peer_entry, s1, r1, s2, r2, acc, s3, r3, s4, r4, res,
    peer_send, peer_recv, send1, recv1, send2, recv2, send3, recv3, send4, recv4, end_send, end_recv,
):
    me, core, y, x = place_in_plane()
    z = lax.axis_index("tsp")
    peer = me + 1 - 2 * core
    width = slots.shape[-1]
    greet(plane_neighbours())
    waits = []

    def copy_of(src, dst, ss, rs, device):
        return pltpu.make_async_remote_copy(src, dst, ss, rs, (device, z), MESH)

    def go(copy):
        copy.start()
        waits.append(copy)

    def piece(tau, di):
        if tau == 0:
            return slots.at[side(y + di), :, 0, 1 - core], peer_slots.at[side(y + di), :, 0]
        return slots.at[:, side(x + di), 1, 1 - core], peer_slots.at[:, side(x + di), 1]

    def from_peer(tau, di):
        src, dst = piece(tau, di)
        k = di + 1
        return copy_of(src, dst, peer_send.at[tau, k], peer_recv.at[tau, k], peer)

    go(copy_of(entry, peer_entry, end_send.at[1], end_recv.at[1], peer))
    for di in (2, 1, -1, 0):
        for tau in (0, 1):
            go(from_peer(tau, di))
    copy_of(entry, peer_entry, end_send.at[1], end_recv.at[1], peer).wait_recv()

    def term(tau, di, j, e):
        yy, xx = (side(y + di), j) if tau == 0 else (j, side(x + di))
        o = (yy * SIDE + xx) * 2 + tau
        tile = [width // entry.shape[1]]
        mine = jnp.concatenate([entry[pl.ds(o, 1), :]] * tile[0], axis=1)
        theirs = jnp.concatenate([peer_entry[pl.ds(o, 1), :]] * tile[0], axis=1)
        a = slots[yy, xx, tau, core].astype(jnp.float32)
        b = peer_slots[yy, xx, tau].astype(jnp.float32)
        return jnp.where(mine == e, a, 0.0) + jnp.where(theirs == e, b, 0.0)

    def near(tau, axis, s):
        vertical = (tau == 0) == (axis == 0)
        return device_of(y + s, x, core) if vertical else device_of(y, x + s, core)

    def first(tau, d, j):
        return copy_of(
            s1.at[tau, d, j], r1.at[tau, d, j], send1.at[tau, d, j], recv1.at[tau, d, j],
            near(tau, 0, 1 - 2 * d),
        )

    def second(tau, d, j, e):
        return copy_of(
            s2.at[tau, d, j, e], r2.at[tau, d, j, e],
            send2.at[tau, d, j, e], recv2.at[tau, d, j, e], near(tau, 0, 1 - 2 * d),
        )

    for tau in (0, 1):
        from_peer(tau, 2).wait_recv()

        @pl.loop(0, SIDE)
        def _(j):
            for d in (0, 1):
                s1[tau, d, j] = term(tau, 2, j, d).astype(s1.dtype)
                first(tau, d, j).start()

    for tau in (0, 1):
        for d in (0, 1):
            from_peer(tau, 1 - 2 * d).wait_recv()

        @pl.loop(0, SIDE)
        def _(j):
            for d in (0, 1):
                s2[tau, d, j, 1 - d] = term(tau, 1 - 2 * d, j, 1 - d).astype(s2.dtype)
                second(tau, d, j, 1 - d).start()

    for tau in (0, 1):

        @pl.loop(0, SIDE)
        def _(j):
            for d in (0, 1):
                first(tau, d, j).wait_recv()
                passed = r1[tau, d, j].astype(jnp.float32)
                s2[tau, d, j, d] = (term(tau, 1 - 2 * d, j, d) + passed).astype(s2.dtype)
                second(tau, d, j, d).start()

    for tau in (0, 1):
        from_peer(tau, 0).wait_recv()

        @pl.loop(0, SIDE)
        def _(j):
            for e in (0, 1):
                acc[tau, j, e] = term(tau, 0, j, e)

    def spot(tau, dj):
        return side((x if tau == 0 else y) + dj)

    def third(tau, d):
        return copy_of(
            s3.at[tau, d], r3.at[tau, d], send3.at[tau, d], recv3.at[tau, d], near(tau, 1, 1 - 2 * d)
        )

    def fourth(tau, d, e):
        return copy_of(
            s4.at[tau, d, e], r4.at[tau, d, e], send4.at[tau, d, e], recv4.at[tau, d, e],
            near(tau, 1, 1 - 2 * d),
        )

    def total(tau, dj, e):
        j = spot(tau, dj)
        for d in (0, 1):
            second(tau, d, j, e).wait_recv()
        return (
            acc[tau, j, e]
            + r2[tau, 0, j, e].astype(jnp.float32)
            + r2[tau, 1, j, e].astype(jnp.float32)
        )

    for tau in (0, 1):
        for d in (0, 1):
            s3[tau, d] = total(tau, 2, d).astype(s3.dtype)
            go(third(tau, d))
    for tau in (0, 1):
        for d in (0, 1):
            s4[tau, d, 1 - d] = total(tau, 1 - 2 * d, 1 - d).astype(s4.dtype)
            go(fourth(tau, d, 1 - d))
    for tau in (0, 1):
        for d in (0, 1):
            value = total(tau, 1 - 2 * d, d)
            third(tau, d).wait_recv()
            s4[tau, d, d] = (value + r3[tau, d].astype(jnp.float32)).astype(s4.dtype)
            go(fourth(tau, d, d))
    for tau in (0, 1):
        for e in (0, 1):
            value = total(tau, 0, e)
            for d in (0, 1):
                fourth(tau, d, e).wait_recv()
                value += r4[tau, d, e].astype(jnp.float32)
            res[tau, e] = value
    last = copy_of(res.at[1 - core], out.at[:, core], end_send.at[0], end_recv.at[0], peer)
    last.start()
    out[:, core] = res[core]
    copy_of(res.at[1 - core], out.at[:, 1 - core], end_send.at[0], end_recv.at[0], peer).wait_recv()
    last.wait_send()
    for copy in waits:
        copy.wait_send()
    for tau in (0, 1):
        for d in (0, 1):

            @pl.loop(0, SIDE)
            def _(j):
                first(tau, d, j).wait_send()
                for e in (0, 1):
                    second(tau, d, j, e).wait_send()


def scatter_gradients(slots, entry):
    width = slots.shape[-1]
    unit = (HALF, width)
    bf16, f32 = jnp.bfloat16, jnp.float32
    dma = pltpu.SemaphoreType.DMA
    pair = lambda *dims: [dma(dims), dma(dims)]
    return pl.pallas_call(
        scatter_kernel,
        out_shape=jax.ShapeDtypeStruct((2, 2) + unit, f32),
        in_specs=[pl.BlockSpec(memory_space=pltpu.VMEM)] * 2,
        out_specs=pl.BlockSpec(memory_space=pltpu.VMEM),
        scratch_shapes=[
            pltpu.VMEM((SIDE, SIDE, 2) + unit, bf16),
            pltpu.VMEM(entry.shape, f32),
            pltpu.VMEM((2, 2, SIDE) + unit, bf16),
            pltpu.VMEM((2, 2, SIDE) + unit, bf16),
            pltpu.VMEM((2, 2, SIDE, 2) + unit, bf16),
            pltpu.VMEM((2, 2, SIDE, 2) + unit, bf16),
            pltpu.VMEM((2, SIDE, 2) + unit, f32),
            pltpu.VMEM((2, 2) + unit, bf16),
            pltpu.VMEM((2, 2) + unit, bf16),
            pltpu.VMEM((2, 2, 2) + unit, bf16),
            pltpu.VMEM((2, 2, 2) + unit, bf16),
            pltpu.VMEM((2, 2) + unit, f32),
        ]
        + pair(2, 4)
        + pair(2, 2, SIDE)
        + pair(2, 2, SIDE, 2)
        + pair(2, 2)
        + pair(2, 2, 2)
        + pair(2),
        compiler_params=pltpu.CompilerParams(
            collective_id=2, has_side_effects=True, vmem_limit_bytes=VMEM_LIMIT
        ),
        name="scatter_gradients",
    )(slots, entry)


def tokens_kernel(places, live, cotangent, frozen, summed, maps, out):
    g = pl.program_id(0)
    width = out.shape[1]
    ranks = summed.shape[2] // 2
    value = lax.dot_general(
        cotangent[...], frozen[...], (((1,), (1,)), ((), ())), preferred_element_type=jnp.float32
    )
    value += ADAPTER_SCALE * jnp.dot(
        summed[0][:, ranks:], maps[0][:, :width], preferred_element_type=jnp.float32
    )
    row = lax.broadcasted_iota(jnp.int32, value.shape, 0)
    out[...] = jnp.where(row < live[g], value, 0.0).astype(out.dtype)


def token_gradients(places, live, cotangent, frozen, summed, maps):
    segments, rows, terms = summed.shape
    width, keys = frozen.shape
    ranks = maps.shape[1]
    return pl.pallas_call(
        tokens_kernel,
        out_shape=jax.ShapeDtypeStruct((segments * rows, width), jnp.bfloat16),
        grid_spec=pltpu.PrefetchScalarGridSpec(
            num_scalar_prefetch=2,
            grid=(segments,),
            in_specs=[
                pl.BlockSpec((rows, keys), lambda g, p, n: (g, 0)),
                pl.BlockSpec((width, keys), lambda g, p, n: (0, 0)),
                pl.BlockSpec((1, rows, terms), lambda g, p, n: (g, 0, 0)),
                pl.BlockSpec((1, ranks, maps.shape[2]), lambda g, p, n: (p[g], 0, 0)),
            ],
            out_specs=pl.BlockSpec((rows, width), lambda g, p, n: (g, 0)),
        ),
        name="token_gradients",
    )(places, live, cotangent, frozen, summed, maps)


def on_device(
    tokens,
    cotangent,
    frozen_key_weight,
    adapter_down_weight,
    adapter_up_weight,
    adapter_place_table,
    segment_adapter,
    segment_live_count,
):
    dp_count = lax.axis_size("dp")
    held, ranks, width = adapter_down_weight.shape
    places = lookup(segment_adapter, adapter_place_table)
    owners = places // held
    owner_hit = owners[:, None] == jnp.arange(dp_count, dtype=jnp.int32)[None, :]
    wanted = jnp.max(jnp.where(owner_hit, (places % held)[:, None], -1), axis=0)
    entry = jnp.broadcast_to(wanted.astype(jnp.float32)[:, None], (dp_count, 128))
    all_cotangent = lax.all_gather(cotangent, "tsp", axis=1, tiled=True)
    mine = jnp.concatenate([adapter_down_weight, adapter_up_weight], axis=2)
    mine = mine.reshape(held, 2, HALF, mine.shape[2])
    maps = gather_maps(mine).reshape(dp_count * held, ranks, mine.shape[3])
    part = project(places, segment_live_count, tokens, cotangent, maps)
    summed = sum_over_features(part)
    slots = slot_gradients(owners, summed, tokens, cotangent)
    slots = slots.reshape(SIDE, SIDE, 2, 2, HALF, slots.shape[2])
    grads = scatter_gradients(slots, entry).reshape(held, ranks, slots.shape[-1])
    token_gradient = token_gradients(
        places, segment_live_count, all_cotangent, frozen_key_weight, summed, maps
    )
    return token_gradient, grads[:, :, :width], grads[:, :, width:]


def solution(mesh):
    placed = (
        P("dp", "tsp"),
        P("dp", "tsp"),
        P("tsp", None),
        P("dp", None, "tsp"),
        P("dp", None, "tsp"),
        P(),
        P("dp"),
        P("dp"),
    )
    return jax.shard_map(
        on_device,
        mesh=mesh,
        in_specs=placed,
        out_specs=(P("dp", "tsp"), P("dp", None, "tsp"), P("dp", None, "tsp")),
        check_vma=False,
    )
```

```python
import jax
import jax.numpy as jnp
from jax import lax
from jax.experimental import pallas as pl
from jax.experimental.pallas import tpu as pltpu
from jax.sharding import PartitionSpec as P

ADAPTER_SCALE = 2.0
MESH = pl.DeviceIdType.MESH
SIDE = 4
RING = 8
HALF = 32
MIB = 1024 * 1024


def lookup(idents, mapping):
    matches = idents[:, None] == jnp.arange(mapping.shape[0], dtype=jnp.int32)[None, :]
    return jnp.sum(jnp.where(matches, mapping[None, :], 0), axis=1)


def place_in_plane():
    me = lax.axis_index("dp")
    core = lax.rem(me, 2)
    chip = lax.div(me, 2)
    return me, core, lax.div(chip, SIDE), lax.rem(chip, SIDE)


def side(v):
    return lax.rem(v + 2 * SIDE, SIDE)


def device_of(y, x, core):
    return (side(y) * SIDE + side(x)) * 2 + core


def greet(devices):
    barrier = pltpu.get_barrier_semaphore()
    for device in devices:
        pl.semaphore_signal(barrier, inc=1, device_id=device, device_id_type=MESH)
    pl.semaphore_wait(barrier, len(devices))


def plane_neighbours():
    me, core, y, x = place_in_plane()
    z = lax.axis_index("tsp")
    return [
        (me + 1 - 2 * core, z),
        (device_of(y, x + 1, core), z),
        (device_of(y, x - 1, core), z),
        (device_of(y + 1, x, core), z),
        (device_of(y - 1, x, core), z),
    ]


def ring(v):
    return lax.rem(v + 2 * RING, RING)


def ring_neighbours():
    me, z = lax.axis_index("dp"), lax.axis_index("tsp")
    return [(me, ring(z + 1)), (me, ring(z - 1))]


def gather_kernel(mine, cotangent, out, beside, local_sem, send_sem, recv_sem, ring_send, ring_recv):
    me, core, y, x = place_in_plane()
    z = lax.axis_index("tsp")
    peer = me + 1 - 2 * core
    greet(plane_neighbours() + ring_neighbours())

    def hop(src, step, d):
        return pltpu.make_async_remote_copy(
            src, beside.at[2 * step + d], ring_send.at[step, d], ring_recv.at[step, d],
            (me, ring(z + 1 - 2 * d)), MESH,
        )

    ids = {}
    sends = []

    def index_of(key):
        return ids.setdefault(key, len(ids))

    def send(ref, device, key):
        k = index_of(key)
        copy = pltpu.make_async_remote_copy(
            ref, ref, send_sem.at[k], recv_sem.at[k], (device, z), MESH
        )
        copy.start()
        sends.append(copy)

    def arrived(ref, key):
        k = index_of(key)
        pltpu.make_async_remote_copy(
            ref, ref, send_sem.at[k], recv_sem.at[k], (peer, z), MESH
        ).wait_recv()

    def owner(tau, di, dj):
        return device_of(y + dj, x + di, tau) if tau == 0 else device_of(y + di, x + dj, tau)

    def near(tau, di, dj):
        return device_of(y + dj, x + di, core) if tau == 0 else device_of(y + di, x + dj, core)

    def block(tau, di, dj, half):
        return out.at[pl.ds(2 * owner(tau, di, dj), 2), half]

    def unit(tau, di, dj, e):
        return out.at[2 * owner(tau, di, dj) + e, core]

    def swap(tau, di, dj):
        send(block(tau, di, dj, core), peer, ("swap", tau, di, dj))

    local = pltpu.make_async_copy(mine, out.at[pl.ds(2 * me, 2)], local_sem)
    local.start()
    k = index_of("own")
    own = pltpu.make_async_remote_copy(
        mine, out.at[pl.ds(2 * me, 2)], send_sem.at[k], recv_sem.at[k], (peer, z), MESH
    )
    own.start()
    sends.append(own)
    local.wait()
    pltpu.make_async_remote_copy(
        mine, out.at[pl.ds(2 * peer, 2)], send_sem.at[k], recv_sem.at[k], (peer, z), MESH
    ).wait_recv()
    for tau in (0, 1):
        for s in (1, -1):
            send(block(tau, 0, 0, core), near(tau, s, 0), ("one", tau, s))
    for tau in (0, 1):
        for s in (1, -1):
            send(block(tau, 0, 0, core), near(tau, 0, s), ("two", tau, 0, s))
    for d in (0, 1):
        copy = hop(cotangent, 0, d)
        copy.start()
        sends.append(copy)
    for tau in (0, 1):
        for s in (1, -1):
            arrived(block(tau, -s, 0, core), ("one", tau, s))
            send(unit(tau, -s, 0, 0 if s == 1 else 1), near(tau, s, 0), ("onward", tau, s))
    for tau in (0, 1):
        for s in (1, -1):
            for t in (1, -1):
                send(block(tau, -s, 0, core), near(tau, 0, t), ("two", tau, -s, t))
            swap(tau, -s, 0)
    for tau in (0, 1):
        arrived(unit(tau, 2, 0, 0), ("onward", tau, 1))
        arrived(unit(tau, 2, 0, 1), ("onward", tau, -1))
        for t in (1, -1):
            send(block(tau, 2, 0, core), near(tau, 0, t), ("two", tau, 2, t))
        swap(tau, 2, 0)
    for di in (0, -1, 1, 2):
        if di == 1:
            for d in (0, 1):
                hop(cotangent, 0, d).wait_recv()
                copy = hop(beside.at[d], 1, d)
                copy.start()
                sends.append(copy)
        for tau in (0, 1):
            for t in (1, -1):
                arrived(block(tau, di, -t, core), ("two", tau, di, t))
                send(
                    unit(tau, di, -t, 0 if t == 1 else 1),
                    near(tau, 0, t),
                    ("last", tau, di, t),
                )
                swap(tau, di, -t)
    for di in (0, -1, 1, 2):
        for tau in (0, 1):
            arrived(unit(tau, di, 2, 0), ("last", tau, di, 1))
            arrived(unit(tau, di, 2, 1), ("last", tau, di, -1))
            swap(tau, di, 2)
    for copy in sends:
        copy.wait_send()
    for d in (0, 1):
        hop(beside.at[d], 1, d).wait_recv()
    for tau in (0, 1):
        for di in (0, -1, 1, 2):
            for dj in (0, -1, 1, 2):
                if di or dj:
                    arrived(block(tau, di, dj, 1 - core), ("swap", tau, di, dj))


def gather_maps(mine, cotangent):
    places, width = 2 * lax.axis_size("dp"), mine.shape[-1]
    anywhere = pl.BlockSpec(memory_space=pl.ANY)
    return pl.pallas_call(
        gather_kernel,
        out_shape=(
            jax.ShapeDtypeStruct((places, 2, HALF, width), mine.dtype),
            jax.ShapeDtypeStruct((4,) + cotangent.shape, cotangent.dtype),
        ),
        in_specs=[pl.BlockSpec(memory_space=pltpu.VMEM), anywhere],
        out_specs=(anywhere, anywhere),
        scratch_shapes=[
            pltpu.SemaphoreType.DMA,
            pltpu.SemaphoreType.DMA((71,)),
            pltpu.SemaphoreType.DMA((71,)),
            pltpu.SemaphoreType.DMA((2, 2)),
            pltpu.SemaphoreType.DMA((2, 2)),
        ],
        compiler_params=pltpu.CompilerParams(
            collective_id=0, has_side_effects=True, vmem_limit_bytes=4 * MIB
        ),
        cost_estimate=pl.CostEstimate(flops=0, transcendentals=0, bytes_accessed=60 * MIB),
        name="gather_maps",
    )(mine, cotangent)


def project_kernel(places, live, tokens, cotangent, maps, out):
    segments, rows, _ = out.shape
    width = tokens.shape[1]
    contract = (((1,), (1,)), ((), ()))
    row = lax.broadcasted_iota(jnp.int32, out.shape[1:], 0)
    for g in range(segments):
        p = places[g]
        here = pl.ds(g * rows, rows)
        lowered = lax.dot_general(
            tokens[here, :], maps[p, :, :width], contract, preferred_element_type=jnp.float32
        )
        pulled = lax.dot_general(
            cotangent[here, :], maps[p, :, width:], contract, preferred_element_type=jnp.float32
        )
        terms = jnp.concatenate([lowered, pulled], axis=1)
        out[g] = jnp.where(row < live[g], terms, 0.0)


def project(places, live, tokens, cotangent, maps):
    segments = places.shape[0]
    rows = tokens.shape[0] // segments
    scalars = pl.BlockSpec(memory_space=pltpu.SMEM)
    whole = pl.BlockSpec(memory_space=pltpu.VMEM)
    return pl.pallas_call(
        project_kernel,
        out_shape=jax.ShapeDtypeStruct((segments, rows, 2 * maps.shape[1]), jnp.float32),
        in_specs=[scalars, scalars, whole, whole, whole],
        out_specs=whole,
        compiler_params=pltpu.CompilerParams(vmem_limit_bytes=20 * MIB),
        name="project",
    )(places, live, tokens, cotangent, maps)


def sum_kernel(part, out, held, sent, send_sem, recv_sem, out_send_sem, out_recv_sem):
    i = lax.axis_index("tsp")
    dp = lax.axis_index("dp")

    def at(v):
        return lax.rem(v + 2 * RING, RING)

    greet([(dp, at(i + 1)), (dp, at(i - 1))])
    copies = []

    def send(src, d, step, u):
        copy = pltpu.make_async_remote_copy(
            src,
            held.at[d, step, u],
            send_sem.at[d, step, u],
            recv_sem.at[d, step, u],
            (dp, at(i + 1 - 2 * d)),
            MESH,
        )
        copy.start()
        copies.append(copy)

    def arrived(d, step, u):
        pltpu.make_async_remote_copy(
            held.at[d, step, u],
            held.at[d, step, u],
            send_sem.at[d, step, u],
            recv_sem.at[d, step, u],
            (dp, at(i + 1 - 2 * d)),
            MESH,
        ).wait_recv()

    for d in (0, 1):
        send(part.at[2 * at(i + 4) + d], d, 0, d)
    for d in (0, 1):
        s = 1 - 2 * d
        send(part.at[2 * at(i + 3 * s) + 1 - d], d, 1, 1 - d)
    for step in (1, 2, 3):
        for v in (0, 1):
            for d in (0, 1):
                u = v if d == 0 else 1 - v
                if step == 1 and v == 1:
                    continue
                s = 1 - 2 * d
                arrived(d, step - 1, u)
                sent[d, step, u] = held[d, step - 1, u] + part[2 * at(i + s * (4 - step)) + u]
                send(sent.at[d, step, u], d, step, u)
    for u in (0, 1):
        arrived(0, 3, u)
        arrived(1, 3, u)
        out[2 * i + u] = (part[2 * i + u] + held[0, 3, u] + held[1, 3, u]).astype(out.dtype)

    def pass_on(chunk, u, d, step):
        ref = out.at[pl.ds(2 * at(chunk), 2)] if u is None else out.at[2 * at(chunk) + u]
        copy = pltpu.make_async_remote_copy(
            ref,
            ref,
            out_send_sem.at[d, step],
            out_recv_sem.at[d, step],
            (dp, at(i + 1 - 2 * d)),
            MESH,
        )
        return copy

    for d in (0, 1):
        copy = pass_on(i, None, d, 0)
        copy.start()
        copies.append(copy)
    for step in (1, 2, 3):
        for d in (0, 1):
            s = 1 - 2 * d
            pass_on(i - step * s, None, d, step - 1).wait_recv()
            copy = pass_on(i - step * s, d if step == 3 else None, d, step)
            copy.start()
            copies.append(copy)
    for d in (0, 1):
        pass_on(i + 4, d, d, 3).wait_recv()
    for copy in copies:
        copy.wait_send()


def sum_over_features(part):
    segments, rows, terms = part.shape
    return pl.pallas_call(
        sum_kernel,
        out_shape=jax.ShapeDtypeStruct(part.shape, jnp.bfloat16),
        in_specs=[pl.BlockSpec(memory_space=pltpu.VMEM)],
        out_specs=pl.BlockSpec(memory_space=pltpu.VMEM),
        scratch_shapes=[
            pltpu.VMEM((2, 4, 2, rows, terms), jnp.float32),
            pltpu.VMEM((2, 4, 2, rows, terms), jnp.float32),
            pltpu.SemaphoreType.DMA((2, 4, 2)),
            pltpu.SemaphoreType.DMA((2, 4, 2)),
            pltpu.SemaphoreType.DMA((2, 4)),
            pltpu.SemaphoreType.DMA((2, 4)),
        ],
        compiler_params=pltpu.CompilerParams(
            collective_id=1, has_side_effects=True, vmem_limit_bytes=8 * MIB
        ),
        cost_estimate=pl.CostEstimate(flops=0, transcendentals=0, bytes_accessed=60 * MIB),
        name="sum_over_features",
    )(part)


def packed_kernel(heads, summed, tokens, cotangent, out, total):
    segments, rows, terms = summed.shape
    ranks, width = terms // 2, tokens.shape[1]
    contract = (((0,), (0,)), ((), ()))
    for g in range(segments):
        here = pl.ds(g * rows, rows)
        down = lax.dot_general(
            summed[g, :, ranks:], tokens[here, :], contract, preferred_element_type=jnp.float32
        )
        up = lax.dot_general(
            summed[g, :, :ranks], cotangent[here, :], contract, preferred_element_type=jnp.float32
        )
        value = jnp.concatenate([down, up], axis=1)
        h = heads[g]
        total[h] = jnp.where(h == g, value, total[h] + value)

    @pl.loop(0, segments)
    def _(g):
        out[g] = (total[g] * (ADAPTER_SCALE / rows)).astype(out.dtype)


def packed_gradients(heads, summed, tokens, cotangent):
    segments, rows, terms = summed.shape
    shape = (segments, terms // 2, tokens.shape[1] + cotangent.shape[1])
    whole = pl.BlockSpec(memory_space=pltpu.VMEM)
    return pl.pallas_call(
        packed_kernel,
        out_shape=jax.ShapeDtypeStruct(shape, jnp.bfloat16),
        in_specs=[pl.BlockSpec(memory_space=pltpu.SMEM), whole, whole, whole],
        out_specs=whole,
        scratch_shapes=[pltpu.VMEM(shape, jnp.float32)],
        compiler_params=pltpu.CompilerParams(vmem_limit_bytes=16 * MIB),
        name="packed_gradients",
    )(heads, summed, tokens, cotangent)


def scatter_kernel(
    index, packed, entry, beside, out_down, out_up, beyond,
    slots, peer_slots, peer_entry, s1, r1, s2, r2, acc, s3, r3, s4, r4, res_down, res_up,
    peer_send, peer_recv, send1, recv1, send2, recv2, send3, recv3, send4, recv4, end_send, end_recv,
    ring_send, ring_recv,
):
    me, core, y, x = place_in_plane()
    z = lax.axis_index("tsp")
    peer = me + 1 - 2 * core
    width = packed.shape[-1]
    split = out_down.shape[-1]
    greet(plane_neighbours() + ring_neighbours())
    waits = []
    half_rows = beside.shape[1] // 2

    def hop(step, d):
        half = pl.ds(d * half_rows, half_rows)
        src = beside.at[2 + d] if step == 0 else beyond.at[d, half]
        dst = beyond.at[d] if step == 0 else beyond.at[2, half]
        return pltpu.make_async_remote_copy(
            src, dst, ring_send.at[step, d], ring_recv.at[step, d],
            (me, ring(z + 1 - 2 * d)), MESH,
        )

    for d in (0, 1):
        copy = hop(0, d)
        copy.start()
        waits.append(copy)

    def copy_of(src, dst, ss, rs, device):
        return pltpu.make_async_remote_copy(src, dst, ss, rs, (device, z), MESH)

    def go(copy):
        copy.start()
        waits.append(copy)

    def piece(tau, di):
        if tau == 0:
            return slots.at[side(y + di), :, 0], peer_slots.at[side(y + di), :, 0]
        return slots.at[:, side(x + di), 1], peer_slots.at[:, side(x + di), 1]

    def from_peer(tau, di):
        src, dst = piece(tau, di)
        k = di + 1
        return copy_of(src, dst, peer_send.at[tau, k], peer_recv.at[tau, k], peer)

    go(copy_of(entry, peer_entry, end_send.at[1], end_recv.at[1], peer))
    for di in (2, 1, -1, 0):
        for tau in (0, 1):

            @pl.loop(0, SIDE)
            def _(j):
                yy, xx = (side(y + di), j) if tau == 0 else (j, side(x + di))
                slots[yy, xx, tau] = packed[index[(yy * SIDE + xx) * 2 + tau], 1 - core]

            go(from_peer(tau, di))
    copy_of(entry, peer_entry, end_send.at[1], end_recv.at[1], peer).wait_recv()

    def term(tau, di, j, e):
        yy, xx = (side(y + di), j) if tau == 0 else (j, side(x + di))
        o = (yy * SIDE + xx) * 2 + tau
        tile = [width // entry.shape[1]]
        mine = jnp.concatenate([entry[pl.ds(o, 1), :]] * tile[0], axis=1)
        theirs = jnp.concatenate([peer_entry[pl.ds(o, 1), :]] * tile[0], axis=1)
        a = packed[index[o], core].astype(jnp.float32)
        b = peer_slots[yy, xx, tau].astype(jnp.float32)
        return jnp.where(mine == e, a, 0.0) + jnp.where(theirs == e, b, 0.0)

    def near(tau, axis, s):
        vertical = (tau == 0) == (axis == 0)
        return device_of(y + s, x, core) if vertical else device_of(y, x + s, core)

    def first(tau, d, j):
        return copy_of(
            s1.at[tau, d, j], r1.at[tau, d, j], send1.at[tau, d, j], recv1.at[tau, d, j],
            near(tau, 0, 1 - 2 * d),
        )

    def second(tau, d, j, e):
        return copy_of(
            s2.at[tau, d, j, e], r2.at[tau, d, j, e],
            send2.at[tau, d, j, e], recv2.at[tau, d, j, e], near(tau, 0, 1 - 2 * d),
        )

    for tau in (0, 1):
        from_peer(tau, 2).wait_recv()

        @pl.loop(0, SIDE)
        def _(j):
            for d in (0, 1):
                s1[tau, d, j] = term(tau, 2, j, d).astype(s1.dtype)
                first(tau, d, j).start()

    for tau in (0, 1):
        for d in (0, 1):
            from_peer(tau, 1 - 2 * d).wait_recv()

        @pl.loop(0, SIDE)
        def _(j):
            for d in (0, 1):
                s2[tau, d, j, 1 - d] = term(tau, 1 - 2 * d, j, 1 - d).astype(s2.dtype)
                second(tau, d, j, 1 - d).start()

    for tau in (0, 1):

        @pl.loop(0, SIDE)
        def _(j):
            for d in (0, 1):
                first(tau, d, j).wait_recv()
                passed = r1[tau, d, j].astype(jnp.float32)
                s2[tau, d, j, d] = (term(tau, 1 - 2 * d, j, d) + passed).astype(s2.dtype)
                second(tau, d, j, d).start()

    for tau in (0, 1):
        from_peer(tau, 0).wait_recv()

        @pl.loop(0, SIDE)
        def _(j):
            for e in (0, 1):
                acc[tau, j, e] = term(tau, 0, j, e)

    for d in (0, 1):
        hop(0, d).wait_recv()
        copy = hop(1, d)
        copy.start()
        waits.append(copy)

    def spot(tau, dj):
        return side((x if tau == 0 else y) + dj)

    def third(tau, d):
        return copy_of(
            s3.at[tau, d], r3.at[tau, d], send3.at[tau, d], recv3.at[tau, d], near(tau, 1, 1 - 2 * d)
        )

    def fourth(tau, d, e):
        return copy_of(
            s4.at[tau, d, e], r4.at[tau, d, e], send4.at[tau, d, e], recv4.at[tau, d, e],
            near(tau, 1, 1 - 2 * d),
        )

    def total(tau, dj, e):
        j = spot(tau, dj)
        for d in (0, 1):
            second(tau, d, j, e).wait_recv()
        return (
            acc[tau, j, e]
            + r2[tau, 0, j, e].astype(jnp.float32)
            + r2[tau, 1, j, e].astype(jnp.float32)
        )

    for tau in (0, 1):
        for d in (0, 1):
            s3[tau, d] = total(tau, 2, d).astype(s3.dtype)
            go(third(tau, d))
    for tau in (0, 1):
        for d in (0, 1):
            s4[tau, d, 1 - d] = total(tau, 1 - 2 * d, 1 - d).astype(s4.dtype)
            go(fourth(tau, d, 1 - d))
    for tau in (0, 1):
        for d in (0, 1):
            value = total(tau, 1 - 2 * d, d)
            third(tau, d).wait_recv()
            s4[tau, d, d] = (value + r3[tau, d].astype(jnp.float32)).astype(s4.dtype)
            go(fourth(tau, d, d))
    for tau in (0, 1):
        for e in (0, 1):
            value = total(tau, 0, e)
            for d in (0, 1):
                fourth(tau, d, e).wait_recv()
                value += r4[tau, d, e].astype(jnp.float32)
            res_down[tau, e] = value[:, :split]
            res_up[tau, e] = value[:, split:]
    for k, (res, out) in enumerate(((res_down, out_down), (res_up, out_up))):
        go(copy_of(res.at[1 - core], out.at[:, core], end_send.at[2 * k], end_recv.at[2 * k], peer))
        out[:, core] = res[core]
    for k, (res, out) in enumerate(((res_down, out_down), (res_up, out_up))):
        copy_of(
            res.at[1 - core], out.at[:, 1 - core], end_send.at[2 * k], end_recv.at[2 * k], peer
        ).wait_recv()
    for d in (0, 1):
        hop(1, d).wait_recv()
    for copy in waits:
        copy.wait_send()
    for tau in (0, 1):
        for d in (0, 1):

            @pl.loop(0, SIDE)
            def _(j):
                first(tau, d, j).wait_send()
                for e in (0, 1):
                    second(tau, d, j, e).wait_send()


def scatter_gradients(index, packed, entry, beside, width):
    unit = packed.shape[2:]
    keys = unit[1] - width
    bf16, f32 = jnp.bfloat16, jnp.float32
    dma = pltpu.SemaphoreType.DMA
    pair = lambda *dims: [dma(dims), dma(dims)]
    whole = pl.BlockSpec(memory_space=pltpu.VMEM)
    anywhere = pl.BlockSpec(memory_space=pl.ANY)
    return pl.pallas_call(
        scatter_kernel,
        out_shape=(
            jax.ShapeDtypeStruct((2, 2, HALF, width), f32),
            jax.ShapeDtypeStruct((2, 2, HALF, keys), f32),
            jax.ShapeDtypeStruct((3,) + beside.shape[1:], bf16),
        ),
        in_specs=[pl.BlockSpec(memory_space=pltpu.SMEM), whole, whole, anywhere],
        out_specs=(whole, whole, anywhere),
        scratch_shapes=[
            pltpu.VMEM((SIDE, SIDE, 2) + unit, bf16),
            pltpu.VMEM((SIDE, SIDE, 2) + unit, bf16),
            pltpu.VMEM(entry.shape, f32),
            pltpu.VMEM((2, 2, SIDE) + unit, bf16),
            pltpu.VMEM((2, 2, SIDE) + unit, bf16),
            pltpu.VMEM((2, 2, SIDE, 2) + unit, bf16),
            pltpu.VMEM((2, 2, SIDE, 2) + unit, bf16),
            pltpu.VMEM((2, SIDE, 2) + unit, f32),
            pltpu.VMEM((2, 2) + unit, bf16),
            pltpu.VMEM((2, 2) + unit, bf16),
            pltpu.VMEM((2, 2, 2) + unit, bf16),
            pltpu.VMEM((2, 2, 2) + unit, bf16),
            pltpu.VMEM((2, 2, HALF, width), f32),
            pltpu.VMEM((2, 2, HALF, keys), f32),
        ]
        + pair(2, 4)
        + pair(2, 2, SIDE)
        + pair(2, 2, SIDE, 2)
        + pair(2, 2)
        + pair(2, 2, 2)
        + pair(3)
        + pair(2, 2),
        compiler_params=pltpu.CompilerParams(
            collective_id=2, has_side_effects=True, vmem_limit_bytes=24 * MIB
        ),
        cost_estimate=pl.CostEstimate(flops=0, transcendentals=0, bytes_accessed=100 * MIB),
        name="scatter_gradients",
    )(index, packed, entry, beside)


def tokens_kernel(
    places, live, cotangent, beside, beyond, frozen, summed, maps, out, tiles, sems
):
    segments, rows, terms = summed.shape
    ranks, width = terms // 2, out.shape[1]
    keys = cotangent.shape[1]
    z = lax.axis_index("tsp")
    block = tiles.shape[1]
    steps = out.shape[0] // block
    row = lax.broadcasted_iota(jnp.int32, (rows, width), 0)
    parts = (
        (cotangent, None, 0), (beside, 0, -1), (beside, 1, 1), (beside, 2, -2),
        (beside, 3, 2), (beyond, 0, -3), (beyond, 1, 3), (beyond, 2, 4),
    )
    weights = jnp.concatenate(
        [frozen[:, pl.ds(pl.multiple_of(ring(z + r) * keys, keys), keys)] for _, _, r in parts],
        axis=1,
    )

    def store(b):
        return pltpu.make_async_copy(
            tiles.at[lax.rem(b, 2)], out.at[pl.ds(b * block, block)], sems.at[lax.rem(b, 2)]
        )

    @pl.loop(0, steps)
    def _(b):
        @pl.when(b >= 2)
        def _():
            store(b - 2).wait()

        here = pl.ds(pl.multiple_of(b * block, block), block)
        left = jnp.concatenate(
            [ref[here, :] if k is None else ref[k, here, :] for ref, k, _ in parts], axis=1
        )
        value = lax.dot_general(
            left, weights, (((1,), (1,)), ((), ())), preferred_element_type=jnp.float32
        )
        for k in range(block // rows):
            g = b * (block // rows) + k
            extra = jnp.dot(
                summed[g, :, ranks:], maps[places[g], :, :width], preferred_element_type=jnp.float32
            )
            total = value[k * rows : (k + 1) * rows] + ADAPTER_SCALE * extra
            tiles[lax.rem(b, 2), k * rows : (k + 1) * rows] = jnp.where(
                row < live[g], total, 0.0
            ).astype(out.dtype)
        store(b).start()

    for b in (steps - 2, steps - 1):
        store(b).wait()


def token_gradients(places, live, cotangent, beside, beyond, frozen, summed, maps):
    segments, rows, terms = summed.shape
    width = frozen.shape[0]
    scalars = pl.BlockSpec(memory_space=pltpu.SMEM)
    whole = pl.BlockSpec(memory_space=pltpu.VMEM)
    return pl.pallas_call(
        tokens_kernel,
        out_shape=jax.ShapeDtypeStruct((segments * rows, width), jnp.bfloat16),
        in_specs=[scalars, scalars] + [whole] * 6,
        out_specs=pl.BlockSpec(memory_space=pl.ANY),
        scratch_shapes=[
            pltpu.VMEM((2, 2 * rows, width), jnp.bfloat16),
            pltpu.SemaphoreType.DMA((2,)),
        ],
        compiler_params=pltpu.CompilerParams(vmem_limit_bytes=28 * MIB),
        name="token_gradients",
    )(places, live, cotangent, beside, beyond, frozen, summed, maps)


def on_device(
    tokens,
    cotangent,
    frozen_key_weight,
    adapter_down_weight,
    adapter_up_weight,
    adapter_place_table,
    segment_adapter,
    segment_live_count,
):
    dp_count = lax.axis_size("dp")
    held, ranks, width = adapter_down_weight.shape
    places = lookup(segment_adapter, adapter_place_table)
    owners = places // held
    segment = jnp.arange(places.shape[0], dtype=jnp.int32)
    same = owners[:, None] == owners[None, :]
    heads = jnp.min(jnp.where(same, segment[None, :], places.shape[0]), axis=1)
    owner_hit = owners[:, None] == jnp.arange(dp_count, dtype=jnp.int32)[None, :]
    wanted = jnp.max(jnp.where(owner_hit, (places % held)[:, None], -1), axis=0)
    index = jnp.max(jnp.where(owner_hit, heads[:, None], 0), axis=0)
    entry = jnp.broadcast_to(wanted.astype(jnp.float32)[:, None], (dp_count, 128))
    mine = jnp.concatenate([adapter_down_weight, adapter_up_weight], axis=2)
    mine = mine.reshape(held, 2, HALF, mine.shape[2])
    maps, beside = gather_maps(mine, cotangent)
    maps = maps.reshape(dp_count * held, ranks, mine.shape[3])
    part = project(places, segment_live_count, tokens, cotangent, maps)
    summed = sum_over_features(part)
    packed = packed_gradients(heads, summed, tokens, cotangent)
    packed = packed.reshape(packed.shape[0], 2, HALF, packed.shape[2])
    down_grad, up_grad, beyond = scatter_gradients(index, packed, entry, beside, width)
    token_gradient = token_gradients(
        places, segment_live_count, cotangent, beside, beyond, frozen_key_weight, summed, maps
    )
    return (
        token_gradient,
        down_grad.reshape(held, ranks, width),
        up_grad.reshape(held, ranks, cotangent.shape[1]),
    )


def solution(mesh):
    placed = (
        P("dp", "tsp"),
        P("dp", "tsp"),
        P("tsp", None),
        P("dp", None, "tsp"),
        P("dp", None, "tsp"),
        P(),
        P("dp"),
        P("dp"),
    )
    return jax.shard_map(
        on_device,
        mesh=mesh,
        in_specs=placed,
        out_specs=(P("dp", "tsp"), P("dp", None, "tsp"), P("dp", None, "tsp")),
        check_vma=False,
    )
```

```python
import jax
import jax.numpy as jnp
from jax import lax
from jax.experimental import pallas as pl
from jax.experimental.pallas import tpu as pltpu
from jax.sharding import PartitionSpec as P

ADAPTER_SCALE = 2.0
MESH = pl.DeviceIdType.MESH
SIDE = 4
RING = 8
HALF = 32
MIB = 1024 * 1024
NEAR = (0, -1, 1, 2)


def lookup(idents, mapping):
    matches = idents[:, None] == jnp.arange(mapping.shape[0], dtype=jnp.int32)[None, :]
    return jnp.sum(jnp.where(matches, mapping[None, :], 0), axis=1)


def place_in_plane():
    me = lax.axis_index("dp")
    core = lax.rem(me, 2)
    chip = lax.div(me, 2)
    return me, core, lax.div(chip, SIDE), lax.rem(chip, SIDE)


def side(v):
    return lax.rem(v + 2 * SIDE, SIDE)


def ring(v):
    return lax.rem(v + 2 * RING, RING)


def device_of(y, x, core):
    return (side(y) * SIDE + side(x)) * 2 + core


def greet_neighbours():
    me, core, y, x = place_in_plane()
    z = lax.axis_index("tsp")
    devices = [
        (me + 1 - 2 * core, z),
        (device_of(y, x + 1, core), z),
        (device_of(y, x - 1, core), z),
        (device_of(y + 1, x, core), z),
        (device_of(y - 1, x, core), z),
        (me, ring(z + 1)),
        (me, ring(z - 1)),
    ]
    barrier = pltpu.get_barrier_semaphore()
    for device in devices:
        pl.semaphore_signal(barrier, inc=1, device_id=device, device_id_type=MESH)
    pl.semaphore_wait(barrier, len(devices))


def remote(src, dst, send, recv, device):
    return pltpu.make_async_remote_copy(src, dst, send, recv, device, MESH)


class PlaneGather:
    copies = 71

    def __init__(self, mine, out, local_sem, send_sem, recv_sem):
        self.me, self.core, self.y, self.x = place_in_plane()
        self.z = lax.axis_index("tsp")
        self.peer = self.me + 1 - 2 * self.core
        self.mine, self.out = mine, out
        self.local_sem, self.send_sem, self.recv_sem = local_sem, send_sem, recv_sem
        self.ids, self.sends = {}, []

    def make(self, src, dst, device, key):
        k = self.ids.setdefault(key, len(self.ids))
        return remote(src, dst, self.send_sem.at[k], self.recv_sem.at[k], (device, self.z))

    def send(self, ref, device, key):
        copy = self.make(ref, ref, device, key)
        copy.start()
        self.sends.append(copy)

    def arrived(self, ref, key):
        self.make(ref, ref, self.peer, key).wait_recv()

    def spot(self, tau, di, dj, core):
        if tau == 0:
            return device_of(self.y + dj, self.x + di, core)
        return device_of(self.y + di, self.x + dj, core)

    def near(self, tau, di, dj):
        return self.spot(tau, di, dj, self.core)

    def block(self, tau, di, dj, half):
        return self.out.at[pl.ds(2 * self.spot(tau, di, dj, tau), 2), half]

    def unit(self, tau, di, dj, e):
        return self.out.at[2 * self.spot(tau, di, dj, tau) + e, self.core]

    def swap(self, tau, di, dj):
        self.send(self.block(tau, di, dj, self.core), self.peer, ("swap", tau, di, dj))

    def own(self):
        here = self.out.at[pl.ds(2 * self.me, 2)]
        self.local = pltpu.make_async_copy(self.mine, here, self.local_sem)
        self.local.start()
        copy = self.make(self.mine, here, self.peer, "own")
        copy.start()
        self.sends.append(copy)

    def own_arrived(self):
        self.local.wait()
        self.make(self.mine, self.out.at[pl.ds(2 * self.peer, 2)], self.peer, "own").wait_recv()

    def one(self):
        for tau in (0, 1):
            for s in (1, -1):
                self.send(self.block(tau, 0, 0, self.core), self.near(tau, s, 0), ("one", tau, s))

    def two(self, *offsets):
        for di in offsets:
            for tau in (0, 1):
                for t in (1, -1):
                    self.send(
                        self.block(tau, di, 0, self.core), self.near(tau, 0, t), ("two", tau, di, t)
                    )

    def one_arrived(self):
        for tau in (0, 1):
            for s in (1, -1):
                self.arrived(self.block(tau, -s, 0, self.core), ("one", tau, s))
                e = 0 if s == 1 else 1
                self.send(self.unit(tau, -s, 0, e), self.near(tau, s, 0), ("onward", tau, s))
        self.two(-1, 1)
        for tau in (0, 1):
            for s in (1, -1):
                self.swap(tau, -s, 0)

    def onward_arrived(self):
        for tau in (0, 1):
            self.arrived(self.unit(tau, 2, 0, 0), ("onward", tau, 1))
            self.arrived(self.unit(tau, 2, 0, 1), ("onward", tau, -1))
        self.two(2)
        for tau in (0, 1):
            self.swap(tau, 2, 0)

    def two_arrived(self, di):
        for tau in (0, 1):
            for t in (1, -1):
                self.arrived(self.block(tau, di, -t, self.core), ("two", tau, di, t))
                e = 0 if t == 1 else 1
                self.send(
                    self.unit(tau, di, -t, e), self.near(tau, 0, t), ("last", tau, di, t)
                )
                self.swap(tau, di, -t)

    def last_arrived(self, di):
        for tau in (0, 1):
            self.arrived(self.unit(tau, di, 2, 0), ("last", tau, di, 1))
            self.arrived(self.unit(tau, di, 2, 1), ("last", tau, di, -1))
            self.swap(tau, di, 2)

    def swaps_arrived(self):
        for tau in (0, 1):
            for di in NEAR:
                for dj in NEAR:
                    if di or dj:
                        self.arrived(self.block(tau, di, dj, 1 - self.core), ("swap", tau, di, dj))

    def sent(self):
        for copy in self.sends:
            copy.wait_send()


class RingSum:
    def __init__(self, part, out, held, passed, send_sem, recv_sem, out_send, out_recv):
        self.me, self.i = lax.axis_index("dp"), lax.axis_index("tsp")
        self.part, self.out, self.held, self.passed = part, out, held, passed
        self.send_sem, self.recv_sem = send_sem, recv_sem
        self.out_send, self.out_recv = out_send, out_recv
        self.copies = []

    def copy(self, src, d, step, u):
        return remote(
            src, self.held.at[d, step, u], self.send_sem.at[d, step, u],
            self.recv_sem.at[d, step, u], (self.me, ring(self.i + 1 - 2 * d)),
        )

    def send(self, src, d, step, u):
        copy = self.copy(src, d, step, u)
        copy.start()
        self.copies.append(copy)

    def begin(self):
        for d in (0, 1):
            self.send(self.part.at[ring(self.i + 4), d], d, 0, d)
        for d in (0, 1):
            s = 1 - 2 * d
            self.send(self.part.at[ring(self.i + 3 * s), 1 - d], d, 1, 1 - d)

    def step(self, step):
        for v in (0, 1):
            for d in (0, 1):
                u = v if d == 0 else 1 - v
                if step == 1 and v == 1:
                    continue
                s = 1 - 2 * d
                self.copy(self.held.at[d, step - 1, u], d, step - 1, u).wait_recv()
                self.passed[d, step, u] = (
                    self.held[d, step - 1, u] + self.part[ring(self.i + s * (4 - step)), u]
                )
                self.send(self.passed.at[d, step, u], d, step, u)

    def pass_on(self, chunk, u, d, step):
        ref = self.out.at[ring(chunk)] if u is None else self.out.at[ring(chunk), u]
        return remote(
            ref, ref, self.out_send.at[d, step], self.out_recv.at[d, step],
            (self.me, ring(self.i + 1 - 2 * d)),
        )

    def total(self):
        for u in (0, 1):
            for d in (0, 1):
                self.copy(self.held.at[d, 3, u], d, 3, u).wait_recv()
            self.out[self.i, u] = (
                self.part[self.i, u] + self.held[0, 3, u] + self.held[1, 3, u]
            ).astype(self.out.dtype)
        for d in (0, 1):
            copy = self.pass_on(self.i, None, d, 0)
            copy.start()
            self.copies.append(copy)

    def onward(self, step):
        for d in (0, 1):
            s = 1 - 2 * d
            self.pass_on(self.i - step * s, None, d, step - 1).wait_recv()
            copy = self.pass_on(self.i - step * s, d if step == 3 else None, d, step)
            copy.start()
            self.copies.append(copy)

    def end(self):
        for d in (0, 1):
            self.pass_on(self.i + 4, d, d, 3).wait_recv()

    def sent(self):
        for copy in self.copies:
            copy.wait_send()


def ring_sum_scratch(part):
    dma = pltpu.SemaphoreType.DMA
    shape = (2, 4, 2) + part[2:]
    return [
        pltpu.VMEM(shape, jnp.float32), pltpu.VMEM(shape, jnp.float32),
        dma((2, 4, 2)), dma((2, 4, 2)), dma((2, 4)), dma((2, 4)),
    ]


class CotangentRing:
    def __init__(self, source, target, send_sem, recv_sem, rows):
        self.me, self.z = lax.axis_index("dp"), lax.axis_index("tsp")
        self.source, self.target = source, target
        self.send_sem, self.recv_sem = send_sem, recv_sem
        self.quarter = rows // 4
        self.copies = []

    def copy(self, step, d, q):
        here = pl.ds(q * self.quarter, self.quarter)
        src, dst = self.source(step, d), self.target(step, d)
        return remote(
            src.at[here], dst.at[here], self.send_sem.at[step, d, q],
            self.recv_sem.at[step, d, q], (self.me, ring(self.z + 1 - 2 * d)),
        )

    def launch(self, step, q, first=False):
        for d in (0, 1):
            if step == 3 and q // 2 != d:
                continue
            if not first:
                self.copy(step - 1, d, q).wait_recv()
            copy = self.copy(step, d, q)
            copy.start()
            self.copies.append(copy)

    def arrived(self, step, q):
        for d in (0, 1):
            if step == 3 and q // 2 != d:
                continue
            self.copy(step, d, q).wait_recv()

    def sent(self):
        for copy in self.copies:
            copy.wait_send()


def gather_kernel(
    places, live, down, up, tokens, cotangent,
    down_maps, pulled, tokens_here, cotangent_here, beside,
    up_maps, part, held, passed, send_sem, recv_sem, out_send, out_recv,
    local_sem, down_send, down_recv, up_send, up_recv, cot_send, cot_recv,
):
    greet_neighbours()
    downs = PlaneGather(down, down_maps, local_sem.at[0], down_send, down_recv)
    ups = PlaneGather(up, up_maps, local_sem.at[1], up_send, up_recv)
    sums = RingSum(part, pulled, held, passed, send_sem, recv_sem, out_send, out_recv)
    cots = CotangentRing(
        lambda step, d: cotangent if step == 0 else beside.at[2 * (step - 1) + d],
        lambda step, d: beside.at[2 * step + d],
        cot_send, cot_recv, cotangent.shape[0],
    )
    ups.own()
    downs.own()
    cotangent_copy = pltpu.make_async_copy(cotangent, cotangent_here, local_sem.at[2])
    cotangent_copy.start()
    tokens_copy = pltpu.make_async_copy(tokens, tokens_here, local_sem.at[3])
    tokens_copy.start()
    ups.own_arrived()
    ups.one()
    ups.two(0)
    downs.own_arrived()
    downs.one()
    for q in range(4):
        cots.launch(0, q, first=True)
    ups.one_arrived()
    downs.two(0)
    ups.onward_arrived()
    downs.one_arrived()
    for di in NEAR:
        ups.two_arrived(di)
    for di in NEAR:
        ups.last_arrived(di)
    downs.onward_arrived()
    ups.swaps_arrived()
    cotangent_copy.wait()

    segments = places.shape[0]
    rows = cotangent.shape[0] // segments
    ranks, keys = 2 * HALF, cotangent.shape[1]
    row = lax.broadcasted_iota(jnp.int32, (rows, ranks), 0)
    for j in range(segments // 2):
        pair = []
        for g in (2 * j, 2 * j + 1):
            term = lax.dot_general(
                cotangent_here[g * rows : (g + 1) * rows, :],
                up_maps[places[g]].reshape(ranks, keys),
                (((1,), (1,)), ((), ())),
                preferred_element_type=jnp.float32,
            )
            pair.append(jnp.where(row < live[g], term, 0.0))
        part[j] = jnp.concatenate(pair, axis=1).reshape(part.shape[1:])
    sums.begin()
    sums.step(1)
    downs.two_arrived(0)
    sums.step(2)
    downs.two_arrived(-1)
    sums.step(3)
    downs.two_arrived(1)
    sums.total()
    cots.launch(1, 0)
    downs.two_arrived(2)
    sums.onward(1)
    downs.last_arrived(0)
    cots.launch(1, 1)
    downs.last_arrived(-1)
    sums.onward(2)
    downs.last_arrived(1)
    downs.last_arrived(2)
    sums.onward(3)
    sums.end()
    downs.swaps_arrived()
    tokens_copy.wait()
    for q in (2, 3):
        cots.arrived(0, q)
    for q in (0, 1):
        cots.arrived(1, q)
    for each in (ups, downs, sums, cots):
        each.sent()


def gather_maps(places, live, down, up, tokens, cotangent):
    count = 2 * lax.axis_size("dp")
    rows = cotangent.shape[0] // places.shape[0]
    ranks = 2 * HALF
    part = (places.shape[0] // 2, 2, rows // 2, 2 * ranks)
    bf16 = jnp.bfloat16
    dma = pltpu.SemaphoreType.DMA
    scalars = pl.BlockSpec(memory_space=pltpu.SMEM)
    whole = pl.BlockSpec(memory_space=pltpu.VMEM)
    anywhere = pl.BlockSpec(memory_space=pl.ANY)
    far = pl.BlockSpec(memory_space=pltpu.HBM)
    return pl.pallas_call(
        gather_kernel,
        out_shape=(
            jax.ShapeDtypeStruct((count,) + down.shape[1:], bf16),
            jax.ShapeDtypeStruct(part, bf16),
            jax.ShapeDtypeStruct(tokens.shape, bf16),
            jax.ShapeDtypeStruct(cotangent.shape, bf16),
            jax.ShapeDtypeStruct((4,) + cotangent.shape, bf16),
        ),
        in_specs=[scalars, scalars, far, far, far, far],
        out_specs=(anywhere, whole, whole, whole, anywhere),
        scratch_shapes=[pltpu.VMEM((count,) + up.shape[1:], bf16), pltpu.VMEM(part, jnp.float32)]
        + ring_sum_scratch(part)
        + [dma((4,))]
        + [dma((PlaneGather.copies,)) for _ in range(4)]
        + [dma((2, 2, 4)), dma((2, 2, 4))],
        compiler_params=pltpu.CompilerParams(
            collective_id=0, has_side_effects=True, vmem_limit_bytes=12 * MIB
        ),
        name="gather_maps",
    )(places, live, down, up, tokens, cotangent)


def between_kernel(places, live, heads, tokens, maps, pulled, part, packed, total):
    segments = places.shape[0]
    rows, width = tokens.shape[0] // segments, tokens.shape[1]
    ranks = 2 * HALF
    row = lax.broadcasted_iota(jnp.int32, (rows, ranks), 0)
    for j in range(segments // 2):
        both = pulled[j].reshape(rows, 2 * ranks)
        pair = []
        for k in (0, 1):
            g = 2 * j + k
            here = slice(g * rows, (g + 1) * rows)
            term = lax.dot_general(
                tokens[here, :], maps[places[g]].reshape(ranks, width),
                (((1,), (1,)), ((), ())), preferred_element_type=jnp.float32,
            )
            pair.append(jnp.where(row < live[g], term, 0.0))
            value = lax.dot_general(
                both[:, k * ranks : (k + 1) * ranks], tokens[here, :],
                (((0,), (0,)), ((), ())), preferred_element_type=jnp.float32,
            )
            h = heads[g]
            total[h] = jnp.where(h == g, value, total[h] + value)
        part[j] = jnp.concatenate(pair, axis=1).reshape(part.shape[1:])

    @pl.loop(0, segments)
    def _(g):
        scaled = (total[g] * (ADAPTER_SCALE / rows)).astype(packed.dtype)
        packed[g] = scaled.reshape(packed.shape[1:])


def between(places, live, heads, tokens, maps, pulled):
    segments, width = places.shape[0], tokens.shape[1]
    scalars = pl.BlockSpec(memory_space=pltpu.SMEM)
    whole = pl.BlockSpec(memory_space=pltpu.VMEM)
    return pl.pallas_call(
        between_kernel,
        out_shape=(
            jax.ShapeDtypeStruct(pulled.shape, jnp.float32),
            jax.ShapeDtypeStruct((segments, 2, HALF, width), jnp.bfloat16),
        ),
        in_specs=[scalars] * 3 + [whole] * 3,
        out_specs=(whole, whole),
        scratch_shapes=[pltpu.VMEM((segments, 2 * HALF, width), jnp.float32)],
        compiler_params=pltpu.CompilerParams(vmem_limit_bytes=24 * MIB),
        name="between",
    )(places, live, heads, tokens, maps, pulled)


class PlaneReduce:
    def __init__(self, index, packed, entry, peer_entry, out, bufs, sems):
        self.me, self.core, self.y, self.x = place_in_plane()
        self.z = lax.axis_index("tsp")
        self.peer = self.me + 1 - 2 * self.core
        self.index, self.packed, self.entry, self.peer_entry = index, packed, entry, peer_entry
        self.out = out
        (
            self.slots, self.peer_slots, self.s1, self.r1, self.s2, self.r2,
            self.acc, self.s3, self.r3, self.s4, self.r4, self.res,
        ) = bufs
        self.sems = sems
        self.waits = []

    @staticmethod
    def scratch(unit):
        bf16, f32 = jnp.bfloat16, jnp.float32
        dma = pltpu.SemaphoreType.DMA
        bufs = [
            pltpu.VMEM((SIDE, SIDE, 2) + unit, bf16),
            pltpu.VMEM((SIDE, SIDE, 2) + unit, bf16),
            pltpu.VMEM((2, 2, SIDE) + unit, bf16),
            pltpu.VMEM((2, 2, SIDE) + unit, bf16),
            pltpu.VMEM((2, 2, SIDE, 2) + unit, bf16),
            pltpu.VMEM((2, 2, SIDE, 2) + unit, bf16),
            pltpu.VMEM((2, SIDE, 2) + unit, f32),
            pltpu.VMEM((2, 2) + unit, bf16),
            pltpu.VMEM((2, 2) + unit, bf16),
            pltpu.VMEM((2, 2, 2) + unit, bf16),
            pltpu.VMEM((2, 2, 2) + unit, bf16),
            pltpu.VMEM((2, 2) + unit, f32),
        ]
        sems = []
        for dims in ((2, 4), (2, 2, SIDE), (2, 2, SIDE, 2), (2, 2), (2, 2, 2), (1,)):
            sems += [dma(dims), dma(dims)]
        return bufs, sems

    def copy(self, src, dst, stage, at, device):
        send, recv = self.sems[2 * stage], self.sems[2 * stage + 1]
        return remote(src, dst, send.at[at], recv.at[at], (device, self.z))

    def go(self, copy):
        copy.start()
        self.waits.append(copy)

    def spot(self, tau, di, j):
        if tau == 0:
            return side(self.y + di), j
        return j, side(self.x + di)

    def near(self, tau, axis, d):
        s = 1 - 2 * d
        if (tau == 0) == (axis == 0):
            return device_of(self.y + s, self.x, self.core)
        return device_of(self.y, self.x + s, self.core)

    def from_peer(self, tau, di):
        if tau == 0:
            at = (side(self.y + di), slice(None), 0)
        else:
            at = (slice(None), side(self.x + di), 1)
        return self.copy(
            self.slots.at[at], self.peer_slots.at[at], 0, (tau, di + 1), self.peer
        )

    def share(self):
        for di in (2, 1, -1, 0):
            for tau in (0, 1):

                @pl.loop(0, SIDE)
                def _(j):
                    yy, xx = self.spot(tau, di, j)
                    o = (yy * SIDE + xx) * 2 + tau
                    self.slots[yy, xx, tau] = self.packed[self.index[o], 1 - self.core]

                self.go(self.from_peer(tau, di))

    def term(self, tau, di, j, e):
        yy, xx = self.spot(tau, di, j)
        o = (yy * SIDE + xx) * 2 + tau
        times = self.packed.shape[-1] // self.entry.shape[1]
        mine = jnp.concatenate([self.entry[pl.ds(o, 1), :]] * times, axis=1)
        theirs = jnp.concatenate([self.peer_entry[pl.ds(o, 1), :]] * times, axis=1)
        a = self.packed[self.index[o], self.core].astype(jnp.float32)
        b = self.peer_slots[yy, xx, tau].astype(jnp.float32)
        return jnp.where(mine == e, a, 0.0) + jnp.where(theirs == e, b, 0.0)

    def first(self, tau, d, j):
        at = (tau, d, j)
        return self.copy(self.s1.at[at], self.r1.at[at], 1, at, self.near(tau, 0, d))

    def second(self, tau, d, j, e):
        at = (tau, d, j, e)
        return self.copy(self.s2.at[at], self.r2.at[at], 2, at, self.near(tau, 0, d))

    def third(self, tau, d):
        at = (tau, d)
        return self.copy(self.s3.at[at], self.r3.at[at], 3, at, self.near(tau, 1, d))

    def fourth(self, tau, d, e):
        at = (tau, d, e)
        return self.copy(self.s4.at[at], self.r4.at[at], 4, at, self.near(tau, 1, d))

    def send_first(self):
        for tau in (0, 1):
            self.from_peer(tau, 2).wait_recv()

            @pl.loop(0, SIDE)
            def _(j):
                for d in (0, 1):
                    self.s1[tau, d, j] = self.term(tau, 2, j, d).astype(self.s1.dtype)
                    self.first(tau, d, j).start()

    def send_second_free(self):
        for tau in (0, 1):
            for d in (0, 1):
                self.from_peer(tau, 1 - 2 * d).wait_recv()

            @pl.loop(0, SIDE)
            def _(j):
                for d in (0, 1):
                    value = self.term(tau, 1 - 2 * d, j, 1 - d)
                    self.s2[tau, d, j, 1 - d] = value.astype(self.s2.dtype)
                    self.second(tau, d, j, 1 - d).start()

    def send_second(self, tau):
        @pl.loop(0, SIDE)
        def _(j):
            for d in (0, 1):
                self.first(tau, d, j).wait_recv()
                value = self.term(tau, 1 - 2 * d, j, d) + self.r1[tau, d, j].astype(jnp.float32)
                self.s2[tau, d, j, d] = value.astype(self.s2.dtype)
                self.second(tau, d, j, d).start()

    def keep(self):
        for tau in (0, 1):
            self.from_peer(tau, 0).wait_recv()

            @pl.loop(0, SIDE)
            def _(j):
                for e in (0, 1):
                    self.acc[tau, j, e] = self.term(tau, 0, j, e)

    def total(self, tau, dj, e):
        j = side((self.x if tau == 0 else self.y) + dj)
        for d in (0, 1):
            self.second(tau, d, j, e).wait_recv()
        return (
            self.acc[tau, j, e]
            + self.r2[tau, 0, j, e].astype(jnp.float32)
            + self.r2[tau, 1, j, e].astype(jnp.float32)
        )

    def send_third(self):
        for tau in (0, 1):
            for d in (0, 1):
                self.s3[tau, d] = self.total(tau, 2, d).astype(self.s3.dtype)
                self.go(self.third(tau, d))

    def send_fourth_free(self):
        for tau in (0, 1):
            for d in (0, 1):
                value = self.total(tau, 1 - 2 * d, 1 - d)
                self.s4[tau, d, 1 - d] = value.astype(self.s4.dtype)
                self.go(self.fourth(tau, d, 1 - d))

    def send_fourth(self):
        for tau in (0, 1):
            for d in (0, 1):
                value = self.total(tau, 1 - 2 * d, d)
                self.third(tau, d).wait_recv()
                value += self.r3[tau, d].astype(jnp.float32)
                self.s4[tau, d, d] = value.astype(self.s4.dtype)
                self.go(self.fourth(tau, d, d))

    def finish(self):
        for tau in (0, 1):
            for e in (0, 1):
                value = self.total(tau, 0, e)
                for d in (0, 1):
                    self.fourth(tau, d, e).wait_recv()
                    value += self.r4[tau, d, e].astype(jnp.float32)
                self.res[tau, e] = value
        self.go(self.copy(
            self.res.at[1 - self.core], self.out.at[:, self.core], 5, 0, self.peer
        ))
        self.out[:, self.core] = self.res[self.core]

    def finished(self):
        self.copy(
            self.res.at[1 - self.core], self.out.at[:, 1 - self.core], 5, 0, self.peer
        ).wait_recv()

    def sent(self):
        for copy in self.waits:
            copy.wait_send()
        for tau in (0, 1):
            for d in (0, 1):

                @pl.loop(0, SIDE)
                def _(j):
                    self.first(tau, d, j).wait_send()
                    for e in (0, 1):
                        self.second(tau, d, j, e).wait_send()


REDUCE_BUFS, REDUCE_SEMS, SUM_REFS = 12, 12, 6


def scatter_kernel(
    index, owners, packed, entry, part, cotangent, beside, out_down, out_up, beyond, *rest
):
    rest = list(rest)

    def take(n):
        taken = rest[:n]
        del rest[:n]
        return taken

    peer_entry, lowered, packed_up = take(3)
    sum_refs = take(SUM_REFS)
    down_bufs, down_sems = take(REDUCE_BUFS), take(REDUCE_SEMS)
    up_bufs, up_sems = take(REDUCE_BUFS), take(REDUCE_SEMS)
    entry_send, entry_recv, cot_send, cot_recv = rest
    greet_neighbours()
    downs = PlaneReduce(index, packed, entry, peer_entry, out_down, down_bufs, down_sems)
    ups = PlaneReduce(index, packed_up, entry, peer_entry, out_up, up_bufs, up_sems)
    sums = RingSum(part, lowered, *sum_refs)
    rows = cotangent.shape[0]
    cots = CotangentRing(
        lambda step, d: beside.at[d] if step == 1 else beyond.at[2 * (step - 2) + d],
        lambda step, d: beyond.at[4] if step == 3 else beyond.at[2 * (step - 1) + d],
        cot_send, cot_recv, rows,
    )

    def cot_from_before(q):
        for d in (0, 1):
            here = pl.ds(q * cots.quarter, cots.quarter)
            copy = remote(
                beside.at[2 + d].at[here], beyond.at[2 + d].at[here], cot_send.at[2, d, q],
                cot_recv.at[2, d, q], (cots.me, ring(cots.z + 1 - 2 * d)),
            )
            copy.start()
            cots.copies.append(copy)

    sums.begin()
    entries = remote(entry, peer_entry, entry_send, entry_recv, (downs.peer, downs.z))
    entries.start()
    downs.share()
    for q in (2, 3):
        cots.launch(1, q, first=True)
    entries.wait_recv()
    downs.send_first()
    sums.step(1)
    downs.send_second_free()
    sums.step(2)
    downs.send_second(0)
    sums.step(3)
    downs.send_second(1)
    sums.total()
    downs.keep()
    sums.onward(1)
    for q in (0, 1):
        cot_from_before(q)
    sums.onward(2)
    sums.onward(3)
    sums.end()
    for q in (2, 3):
        cots.launch(2, q)

    segments = owners.shape[0]
    seg_rows, keys = rows // segments, cotangent.shape[1]
    ranks = 2 * HALF
    values = []
    for g in range(segments):
        both = lowered[g // 2].reshape(seg_rows, 2 * ranks)
        values.append(lax.dot_general(
            both[:, (g % 2) * ranks : (g % 2 + 1) * ranks],
            cotangent[g * seg_rows : (g + 1) * seg_rows, :],
            (((0,), (0,)), ((), ())),
            preferred_element_type=jnp.float32,
        ))
    for g in range(segments):
        value = values[g]
        for h in range(segments):
            if h != g:
                value = value + jnp.where(owners[h] == owners[g], values[h], 0.0)
        scaled = (value * (ADAPTER_SCALE / seg_rows)).astype(packed_up.dtype)
        packed_up[g] = scaled.reshape(packed_up.shape[1:])

    ups.share()
    downs.send_third()
    ups.send_first()
    downs.send_fourth_free()
    ups.send_second_free()
    downs.send_fourth()
    for tau in (0, 1):
        ups.send_second(tau)
    for q in range(4):
        cots.launch(3, q)
    ups.keep()
    ups.send_third()
    downs.finish()
    ups.send_fourth_free()
    ups.send_fourth()
    ups.finish()
    downs.finished()
    ups.finished()
    for q in range(4):
        cots.arrived(3, q)
    for q in (2, 3):
        for d in (0, 1):
            if q // 2 != d:
                cots.copy(2, d, q).wait_recv()
    for q in (0, 1):
        for d in (0, 1):
            if q // 2 != d:
                cots.copy(2, d, q).wait_recv()
    entries.wait_send()
    for each in (downs, ups, sums, cots):
        each.sent()


def scatter_gradients(index, owners, packed, entry, part, cotangent, beside):
    down_unit = packed.shape[2:]
    up_unit = (HALF, cotangent.shape[1])
    bf16, f32 = jnp.bfloat16, jnp.float32
    dma = pltpu.SemaphoreType.DMA
    scalars = pl.BlockSpec(memory_space=pltpu.SMEM)
    whole = pl.BlockSpec(memory_space=pltpu.VMEM)
    anywhere = pl.BlockSpec(memory_space=pl.ANY)
    down_bufs, down_sems = PlaneReduce.scratch(down_unit)
    up_bufs, up_sems = PlaneReduce.scratch(up_unit)
    return pl.pallas_call(
        scatter_kernel,
        out_shape=(
            jax.ShapeDtypeStruct((2, 2) + down_unit, f32),
            jax.ShapeDtypeStruct((2, 2) + up_unit, f32),
            jax.ShapeDtypeStruct((5,) + beside.shape[1:], bf16),
        ),
        in_specs=[scalars, scalars, whole, whole, whole, whole, anywhere],
        out_specs=(whole, whole, anywhere),
        scratch_shapes=[
            pltpu.VMEM(entry.shape, f32),
            pltpu.VMEM(part.shape, bf16),
            pltpu.VMEM((packed.shape[0], 2) + up_unit, bf16),
        ]
        + ring_sum_scratch(part.shape)
        + down_bufs + down_sems + up_bufs + up_sems
        + [dma(()), dma(()), dma((4, 2, 4)), dma((4, 2, 4))],
        compiler_params=pltpu.CompilerParams(
            collective_id=1, has_side_effects=True, vmem_limit_bytes=30 * MIB
        ),
        name="scatter_gradients",
    )(index, owners, packed, entry, part, cotangent, beside)


def tokens_kernel(
    places, live, cotangent, beside, beyond, frozen, pulled, maps, out, tiles, sems
):
    segments = places.shape[0]
    width, keys = out.shape[1], cotangent.shape[1]
    rows = out.shape[0] // segments
    ranks = 2 * HALF
    z = lax.axis_index("tsp")
    block = tiles.shape[1]
    steps = out.shape[0] // block
    row = lax.broadcasted_iota(jnp.int32, (rows, width), 0)
    offsets = (0, -1, 1, -2, 2, -3, 3, 4)
    weights = jnp.concatenate(
        [frozen[:, pl.ds(pl.multiple_of(ring(z + r) * keys, keys), keys)] for r in offsets],
        axis=1,
    )

    def store(b):
        return pltpu.make_async_copy(
            tiles.at[lax.rem(b, 2)], out.at[pl.ds(b * block, block)], sems.at[lax.rem(b, 2)]
        )

    for half in (0, 1):
        second = (beside, 2) if half == 0 else (beyond, 0)
        third = (beside, 3) if half == 0 else (beyond, 1)
        parts = (
            (beside, 0), (beside, 1), second, third, (beyond, 2), (beyond, 3), (beyond, 4)
        )

        @pl.loop(half * steps // 2, (half + 1) * steps // 2)
        def _(b):
            @pl.when(b >= 2)
            def _():
                store(b - 2).wait()

            here = pl.ds(pl.multiple_of(b * block, block), block)
            left = jnp.concatenate(
                [cotangent[here, :]] + [ref[k, here, :] for ref, k in parts], axis=1
            )
            value = lax.dot_general(
                left, weights, (((1,), (1,)), ((), ())), preferred_element_type=jnp.float32
            )
            for k in range(2):
                g = 2 * b + k
                both = pulled[b].reshape(rows, 2 * ranks)
                extra = jnp.dot(
                    both[:, k * ranks : (k + 1) * ranks], maps[places[g]].reshape(ranks, width),
                    preferred_element_type=jnp.float32,
                )
                total = value[k * rows : (k + 1) * rows] + ADAPTER_SCALE * extra
                tiles[lax.rem(b, 2), k * rows : (k + 1) * rows] = jnp.where(
                    row < live[g], total, 0.0
                ).astype(out.dtype)
            store(b).start()

    for b in (steps - 2, steps - 1):
        store(b).wait()


def token_gradients(places, live, cotangent, beside, beyond, frozen, pulled, maps):
    segments = places.shape[0]
    rows, width = cotangent.shape[0] // segments, frozen.shape[0]
    scalars = pl.BlockSpec(memory_space=pltpu.SMEM)
    whole = pl.BlockSpec(memory_space=pltpu.VMEM)
    return pl.pallas_call(
        tokens_kernel,
        out_shape=jax.ShapeDtypeStruct((segments * rows, width), jnp.bfloat16),
        in_specs=[scalars, scalars] + [whole] * 6,
        out_specs=pl.BlockSpec(memory_space=pl.ANY),
        scratch_shapes=[
            pltpu.VMEM((2, 2 * rows, width), jnp.bfloat16),
            pltpu.SemaphoreType.DMA((2,)),
        ],
        compiler_params=pltpu.CompilerParams(vmem_limit_bytes=28 * MIB),
        name="token_gradients",
    )(places, live, cotangent, beside, beyond, frozen, pulled, maps)


def on_device(
    tokens,
    cotangent,
    frozen_key_weight,
    adapter_down_weight,
    adapter_up_weight,
    adapter_place_table,
    segment_adapter,
    segment_live_count,
):
    dp_count = lax.axis_size("dp")
    held, ranks, width = adapter_down_weight.shape
    keys = cotangent.shape[1]
    live = segment_live_count
    places = lookup(segment_adapter, adapter_place_table)
    owners = places // held
    segment = jnp.arange(places.shape[0], dtype=jnp.int32)
    same = owners[:, None] == owners[None, :]
    heads = jnp.min(jnp.where(same, segment[None, :], places.shape[0]), axis=1)
    owner_hit = owners[:, None] == jnp.arange(dp_count, dtype=jnp.int32)[None, :]
    wanted = jnp.max(jnp.where(owner_hit, (places % held)[:, None], -1), axis=0)
    index = jnp.max(jnp.where(owner_hit, heads[:, None], 0), axis=0)
    entry = jnp.broadcast_to(wanted.astype(jnp.float32)[:, None], (dp_count, 128))
    far = lambda array: pltpu.with_memory_space_constraint(array, pltpu.HBM)
    maps, pulled, tokens_here, cotangent_here, beside = gather_maps(
        places, live,
        far(adapter_down_weight.reshape(held, 2, HALF, width)),
        far(adapter_up_weight.reshape(held, 2, HALF, keys)),
        far(tokens), far(cotangent),
    )
    part, packed = between(places, live, heads, tokens_here, maps, pulled)
    down_grad, up_grad, beyond = scatter_gradients(
        index, owners, packed, entry, part, cotangent_here, beside
    )
    token_gradient = token_gradients(
        places, live, cotangent_here, beside, beyond, frozen_key_weight, pulled, maps
    )
    return (
        token_gradient,
        down_grad.reshape(held, ranks, width),
        up_grad.reshape(held, ranks, keys),
    )


def solution(mesh):
    placed = (
        P("dp", "tsp"),
        P("dp", "tsp"),
        P("tsp", None),
        P("dp", None, "tsp"),
        P("dp", None, "tsp"),
        P(),
        P("dp"),
        P("dp"),
    )
    return jax.shard_map(
        on_device,
        mesh=mesh,
        in_specs=placed,
        out_specs=(P("dp", "tsp"), P("dp", None, "tsp"), P("dp", None, "tsp")),
        check_vma=False,
    )
```

```python
import jax
import jax.numpy as jnp
from jax import lax
from jax.experimental import pallas as pl
from jax.experimental.pallas import tpu as pltpu
from jax.sharding import PartitionSpec as P

ADAPTER_SCALE = 2.0
MESH = pl.DeviceIdType.MESH
SIDE = 4
RING = 8
HALF = 32
MIB = 1024 * 1024
NEAR = (0, -1, 1, 2)


def lookup(idents, mapping):
    matches = idents[:, None] == jnp.arange(mapping.shape[0], dtype=jnp.int32)[None, :]
    return jnp.sum(jnp.where(matches, mapping[None, :], 0), axis=1)


def place_in_plane():
    me = lax.axis_index("dp")
    core = lax.rem(me, 2)
    chip = lax.div(me, 2)
    return me, core, lax.div(chip, SIDE), lax.rem(chip, SIDE)


def side(v):
    return lax.rem(v + 2 * SIDE, SIDE)


def ring(v):
    return lax.rem(v + 2 * RING, RING)


def device_of(y, x, core):
    return (side(y) * SIDE + side(x)) * 2 + core


def greet_neighbours():
    me, core, y, x = place_in_plane()
    z = lax.axis_index("tsp")
    devices = [
        (me + 1 - 2 * core, z),
        (device_of(y, x + 1, core), z),
        (device_of(y, x - 1, core), z),
        (device_of(y + 1, x, core), z),
        (device_of(y - 1, x, core), z),
        (me, ring(z + 1)),
        (me, ring(z - 1)),
    ]
    barrier = pltpu.get_barrier_semaphore()
    for device in devices:
        pl.semaphore_signal(barrier, inc=1, device_id=device, device_id_type=MESH)
    pl.semaphore_wait(barrier, len(devices))


def remote(src, dst, send, recv, device):
    return pltpu.make_async_remote_copy(src, dst, send, recv, device, MESH)


class PlaneGather:
    copies = 71

    def __init__(self, mine, out, local_sem, send_sem, recv_sem):
        self.me, self.core, self.y, self.x = place_in_plane()
        self.z = lax.axis_index("tsp")
        self.peer = self.me + 1 - 2 * self.core
        self.mine, self.out = mine, out
        self.local_sem, self.send_sem, self.recv_sem = local_sem, send_sem, recv_sem
        self.ids, self.sends = {}, []

    def make(self, src, dst, device, key):
        k = self.ids.setdefault(key, len(self.ids))
        return remote(src, dst, self.send_sem.at[k], self.recv_sem.at[k], (device, self.z))

    def send(self, ref, device, key):
        copy = self.make(ref, ref, device, key)
        copy.start()
        self.sends.append(copy)

    def arrived(self, ref, key):
        self.make(ref, ref, self.peer, key).wait_recv()

    def spot(self, tau, di, dj, core):
        if tau == 0:
            return device_of(self.y + dj, self.x + di, core)
        return device_of(self.y + di, self.x + dj, core)

    def near(self, tau, di, dj):
        return self.spot(tau, di, dj, self.core)

    def block(self, tau, di, dj, half):
        return self.out.at[pl.ds(2 * self.spot(tau, di, dj, tau), 2), half]

    def unit(self, tau, di, dj, e):
        return self.out.at[2 * self.spot(tau, di, dj, tau) + e, self.core]

    def swap(self, tau, di, dj):
        self.send(self.block(tau, di, dj, self.core), self.peer, ("swap", tau, di, dj))

    def own(self):
        here = self.out.at[pl.ds(2 * self.me, 2)]
        self.local = pltpu.make_async_copy(self.mine, here, self.local_sem)
        self.local.start()
        copy = self.make(self.mine, here, self.peer, "own")
        copy.start()
        self.sends.append(copy)

    def own_arrived(self):
        self.local.wait()
        self.make(self.mine, self.out.at[pl.ds(2 * self.peer, 2)], self.peer, "own").wait_recv()

    def one(self):
        for tau in (0, 1):
            for s in (1, -1):
                self.send(self.block(tau, 0, 0, self.core), self.near(tau, s, 0), ("one", tau, s))

    def two(self, *offsets):
        for di in offsets:
            for tau in (0, 1):
                for t in (1, -1):
                    self.send(
                        self.block(tau, di, 0, self.core), self.near(tau, 0, t), ("two", tau, di, t)
                    )

    def one_arrived(self):
        for tau in (0, 1):
            for s in (1, -1):
                self.arrived(self.block(tau, -s, 0, self.core), ("one", tau, s))
                e = 0 if s == 1 else 1
                self.send(self.unit(tau, -s, 0, e), self.near(tau, s, 0), ("onward", tau, s))
        self.two(-1, 1)
        for tau in (0, 1):
            for s in (1, -1):
                self.swap(tau, -s, 0)

    def onward_arrived(self):
        for tau in (0, 1):
            self.arrived(self.unit(tau, 2, 0, 0), ("onward", tau, 1))
            self.arrived(self.unit(tau, 2, 0, 1), ("onward", tau, -1))
        self.two(2)
        for tau in (0, 1):
            self.swap(tau, 2, 0)

    def two_arrived(self, di):
        for tau in (0, 1):
            for t in (1, -1):
                self.arrived(self.block(tau, di, -t, self.core), ("two", tau, di, t))
                e = 0 if t == 1 else 1
                self.send(
                    self.unit(tau, di, -t, e), self.near(tau, 0, t), ("last", tau, di, t)
                )
                self.swap(tau, di, -t)

    def last_arrived(self, di):
        for tau in (0, 1):
            self.arrived(self.unit(tau, di, 2, 0), ("last", tau, di, 1))
            self.arrived(self.unit(tau, di, 2, 1), ("last", tau, di, -1))
            self.swap(tau, di, 2)

    def swaps_arrived(self):
        for tau in (0, 1):
            for di in NEAR:
                for dj in NEAR:
                    if di or dj:
                        self.arrived(self.block(tau, di, dj, 1 - self.core), ("swap", tau, di, dj))

    def sent(self):
        for copy in self.sends:
            copy.wait_send()


class RingSum:
    def __init__(self, part, out, held, passed, send_sem, recv_sem, out_send, out_recv):
        self.me, self.i = lax.axis_index("dp"), lax.axis_index("tsp")
        self.part, self.out, self.held, self.passed = part, out, held, passed
        self.send_sem, self.recv_sem = send_sem, recv_sem
        self.out_send, self.out_recv = out_send, out_recv
        self.copies = []

    def copy(self, src, d, step, u):
        return remote(
            src, self.held.at[d, step, u], self.send_sem.at[d, step, u],
            self.recv_sem.at[d, step, u], (self.me, ring(self.i + 1 - 2 * d)),
        )

    def send(self, src, d, step, u):
        copy = self.copy(src, d, step, u)
        copy.start()
        self.copies.append(copy)

    def begin(self):
        for d in (0, 1):
            self.send(self.part.at[ring(self.i + 4), d], d, 0, d)
        for d in (0, 1):
            s = 1 - 2 * d
            self.send(self.part.at[ring(self.i + 3 * s), 1 - d], d, 1, 1 - d)

    def step(self, step):
        for v in (0, 1):
            for d in (0, 1):
                u = v if d == 0 else 1 - v
                if step == 1 and v == 1:
                    continue
                s = 1 - 2 * d
                self.copy(self.held.at[d, step - 1, u], d, step - 1, u).wait_recv()
                self.passed[d, step, u] = (
                    self.held[d, step - 1, u] + self.part[ring(self.i + s * (4 - step)), u]
                )
                self.send(self.passed.at[d, step, u], d, step, u)

    def pass_on(self, chunk, u, d, step):
        ref = self.out.at[ring(chunk)] if u is None else self.out.at[ring(chunk), u]
        return remote(
            ref, ref, self.out_send.at[d, step], self.out_recv.at[d, step],
            (self.me, ring(self.i + 1 - 2 * d)),
        )

    def total(self):
        for u in (0, 1):
            for d in (0, 1):
                self.copy(self.held.at[d, 3, u], d, 3, u).wait_recv()
            self.out[self.i, u] = (
                self.part[self.i, u] + self.held[0, 3, u] + self.held[1, 3, u]
            ).astype(self.out.dtype)
        for d in (0, 1):
            copy = self.pass_on(self.i, None, d, 0)
            copy.start()
            self.copies.append(copy)

    def onward(self, step):
        for d in (0, 1):
            s = 1 - 2 * d
            self.pass_on(self.i - step * s, None, d, step - 1).wait_recv()
            copy = self.pass_on(self.i - step * s, d if step == 3 else None, d, step)
            copy.start()
            self.copies.append(copy)

    def end(self):
        for d in (0, 1):
            self.pass_on(self.i + 4, d, d, 3).wait_recv()

    def sent(self):
        for copy in self.copies:
            copy.wait_send()


def ring_sum_scratch(part):
    dma = pltpu.SemaphoreType.DMA
    shape = (2, 4, 2) + part[2:]
    return [
        pltpu.VMEM(shape, jnp.float32), pltpu.VMEM(shape, jnp.float32),
        dma((2, 4, 2)), dma((2, 4, 2)), dma((2, 4)), dma((2, 4)),
    ]


class CotangentRing:
    eighths = 8

    def __init__(self, source, target, send_sem, recv_sem, rows, steps):
        self.me, self.z = lax.axis_index("dp"), lax.axis_index("tsp")
        self.source, self.target = source, target
        self.send_sem, self.recv_sem = send_sem, recv_sem
        self.size = rows // self.eighths
        self.copies = []
        self.origin = steps[0]
        self.queue, self.waited = [], set()
        for step in steps:
            for k in range(self.eighths if step < 3 else self.eighths // 2):
                pieces = [(step, 0, k), (step, 1, k if step < 3 else k + self.eighths // 2)]
                self.queue.append(pieces)

    def copy(self, step, d, q):
        here = pl.ds(q * self.size, self.size)
        src, dst = self.source(step, d), self.target(step, d)
        at = (step - self.origin, d, q)
        return remote(
            src.at[here], dst.at[here], self.send_sem.at[at], self.recv_sem.at[at],
            (self.me, ring(self.z + 1 - 2 * d)),
        )

    def wait(self, step, d, q):
        if step >= self.origin and (step, d, q) not in self.waited:
            self.waited.add((step, d, q))
            self.copy(step, d, q).wait_recv()

    def launch(self, count=1):
        for pieces in self.queue[:count]:
            for step, d, q in pieces:
                self.wait(step - 1, d, q)
                copy = self.copy(step, d, q)
                copy.start()
                self.copies.append((copy, (step, d, q)))
        self.queue = self.queue[count:]

    def arrived(self):
        for _, piece in self.copies:
            self.wait(*piece)

    def sent(self):
        for copy, _ in self.copies:
            copy.wait_send()


def gather_kernel(
    places, live, down, up, tokens, cotangent,
    down_maps, pulled, tokens_here, cotangent_here, beside,
    up_maps, part, held, passed, send_sem, recv_sem, out_send, out_recv,
    local_sem, down_send, down_recv, up_send, up_recv, cot_send, cot_recv,
):
    greet_neighbours()
    downs = PlaneGather(down, down_maps, local_sem.at[0], down_send, down_recv)
    ups = PlaneGather(up, up_maps, local_sem.at[1], up_send, up_recv)
    sums = RingSum(part, pulled, held, passed, send_sem, recv_sem, out_send, out_recv)
    cots = CotangentRing(
        lambda step, d: cotangent if step == 0 else beside.at[d],
        lambda step, d: beside.at[2 * step + d],
        cot_send, cot_recv, cotangent.shape[0], (0, 1),
    )
    ups.own()
    downs.own()
    cotangent_copy = pltpu.make_async_copy(cotangent, cotangent_here, local_sem.at[2])
    cotangent_copy.start()
    tokens_copy = pltpu.make_async_copy(tokens, tokens_here, local_sem.at[3])
    tokens_copy.start()
    cots.launch(6)
    ups.own_arrived()
    ups.one()
    ups.two(0)
    ups.one_arrived()
    downs.own_arrived()
    downs.one()
    ups.onward_arrived()
    for di in NEAR:
        ups.two_arrived(di)
    downs.two(0)
    for di in NEAR:
        ups.last_arrived(di)
    ups.swaps_arrived()
    cotangent_copy.wait()

    segments = places.shape[0]
    rows = cotangent.shape[0] // segments
    ranks, keys = 2 * HALF, cotangent.shape[1]
    row = lax.broadcasted_iota(jnp.int32, (rows, ranks), 0)
    for j in range(segments // 2):
        pair = []
        for g in (2 * j, 2 * j + 1):
            term = lax.dot_general(
                cotangent_here[g * rows : (g + 1) * rows, :],
                up_maps[places[g]].reshape(ranks, keys),
                (((1,), (1,)), ((), ())),
                preferred_element_type=jnp.float32,
            )
            pair.append(jnp.where(row < live[g], term, 0.0))
        part[j] = jnp.concatenate(pair, axis=1).reshape(part.shape[1:])
    sums.begin()
    cots.launch()
    downs.one_arrived()
    sums.step(1)
    cots.launch()
    downs.two_arrived(0)
    downs.onward_arrived()
    sums.step(2)
    cots.launch()
    sums.step(3)
    cots.launch()
    downs.two_arrived(-1)
    sums.total()
    cots.launch()
    downs.two_arrived(1)
    sums.onward(1)
    cots.launch()
    downs.two_arrived(2)
    sums.onward(2)
    cots.launch()
    downs.last_arrived(0)
    downs.last_arrived(-1)
    sums.onward(3)
    cots.launch(3)
    downs.last_arrived(1)
    downs.last_arrived(2)
    sums.end()
    downs.swaps_arrived()
    tokens_copy.wait()
    cots.arrived()
    for each in (ups, downs, sums, cots):
        each.sent()


def gather_maps(places, live, down, up, tokens, cotangent):
    count = 2 * lax.axis_size("dp")
    rows = cotangent.shape[0] // places.shape[0]
    ranks = 2 * HALF
    part = (places.shape[0] // 2, 2, rows // 2, 2 * ranks)
    bf16 = jnp.bfloat16
    dma = pltpu.SemaphoreType.DMA
    scalars = pl.BlockSpec(memory_space=pltpu.SMEM)
    whole = pl.BlockSpec(memory_space=pltpu.VMEM)
    anywhere = pl.BlockSpec(memory_space=pl.ANY)
    far = pl.BlockSpec(memory_space=pltpu.HBM)
    return pl.pallas_call(
        gather_kernel,
        out_shape=(
            jax.ShapeDtypeStruct((count,) + down.shape[1:], bf16),
            jax.ShapeDtypeStruct(part, bf16),
            jax.ShapeDtypeStruct(tokens.shape, bf16),
            jax.ShapeDtypeStruct(cotangent.shape, bf16),
            jax.ShapeDtypeStruct((4,) + cotangent.shape, bf16),
        ),
        in_specs=[scalars, scalars, far, far, far, far],
        out_specs=(anywhere, whole, whole, whole, anywhere),
        scratch_shapes=[pltpu.VMEM((count,) + up.shape[1:], bf16), pltpu.VMEM(part, jnp.float32)]
        + ring_sum_scratch(part)
        + [dma((4,))]
        + [dma((PlaneGather.copies,)) for _ in range(4)]
        + [dma((2, 2, CotangentRing.eighths)), dma((2, 2, CotangentRing.eighths))],
        compiler_params=pltpu.CompilerParams(
            collective_id=0, has_side_effects=True, vmem_limit_bytes=12 * MIB
        ),
        name="gather_maps",
    )(places, live, down, up, tokens, cotangent)


def between_kernel(places, live, heads, tokens, maps, pulled, part, packed, total):
    segments = places.shape[0]
    rows, width = tokens.shape[0] // segments, tokens.shape[1]
    ranks = 2 * HALF
    row = lax.broadcasted_iota(jnp.int32, (rows, ranks), 0)
    for j in range(segments // 2):
        both = pulled[j].reshape(rows, 2 * ranks)
        pair = []
        for k in (0, 1):
            g = 2 * j + k
            here = slice(g * rows, (g + 1) * rows)
            term = lax.dot_general(
                tokens[here, :], maps[places[g]].reshape(ranks, width),
                (((1,), (1,)), ((), ())), preferred_element_type=jnp.float32,
            )
            pair.append(jnp.where(row < live[g], term, 0.0))
            value = lax.dot_general(
                both[:, k * ranks : (k + 1) * ranks], tokens[here, :],
                (((0,), (0,)), ((), ())), preferred_element_type=jnp.float32,
            )
            h = heads[g]
            total[h] = jnp.where(h == g, value, total[h] + value)
        part[j] = jnp.concatenate(pair, axis=1).reshape(part.shape[1:])

    @pl.loop(0, segments)
    def _(g):
        scaled = (total[g] * (ADAPTER_SCALE / rows)).astype(packed.dtype)
        packed[g] = scaled.reshape(packed.shape[1:])


def between(places, live, heads, tokens, maps, pulled):
    segments, width = places.shape[0], tokens.shape[1]
    scalars = pl.BlockSpec(memory_space=pltpu.SMEM)
    whole = pl.BlockSpec(memory_space=pltpu.VMEM)
    return pl.pallas_call(
        between_kernel,
        out_shape=(
            jax.ShapeDtypeStruct(pulled.shape, jnp.float32),
            jax.ShapeDtypeStruct((segments, 2, HALF, width), jnp.bfloat16),
        ),
        in_specs=[scalars] * 3 + [whole] * 3,
        out_specs=(whole, whole),
        scratch_shapes=[pltpu.VMEM((segments, 2 * HALF, width), jnp.float32)],
        compiler_params=pltpu.CompilerParams(vmem_limit_bytes=24 * MIB),
        name="between",
    )(places, live, heads, tokens, maps, pulled)


class PlaneReduce:
    def __init__(self, index, packed, entry, peer_entry, out, bufs, sems):
        self.me, self.core, self.y, self.x = place_in_plane()
        self.z = lax.axis_index("tsp")
        self.peer = self.me + 1 - 2 * self.core
        self.index, self.packed, self.entry, self.peer_entry = index, packed, entry, peer_entry
        self.out = out
        (
            self.slots, self.peer_slots, self.s1, self.r1, self.s2, self.r2,
            self.acc, self.s3, self.r3, self.s4, self.r4, self.res,
        ) = bufs
        self.sems = sems
        self.waits = []

    @staticmethod
    def scratch(unit):
        bf16, f32 = jnp.bfloat16, jnp.float32
        dma = pltpu.SemaphoreType.DMA
        bufs = [
            pltpu.VMEM((SIDE, SIDE, 2) + unit, bf16),
            pltpu.VMEM((SIDE, SIDE, 2) + unit, bf16),
            pltpu.VMEM((2, 2, SIDE) + unit, bf16),
            pltpu.VMEM((2, 2, SIDE) + unit, bf16),
            pltpu.VMEM((2, 2, SIDE, 2) + unit, bf16),
            pltpu.VMEM((2, 2, SIDE, 2) + unit, bf16),
            pltpu.VMEM((2, SIDE, 2) + unit, f32),
            pltpu.VMEM((2, 2) + unit, bf16),
            pltpu.VMEM((2, 2) + unit, bf16),
            pltpu.VMEM((2, 2, 2) + unit, bf16),
            pltpu.VMEM((2, 2, 2) + unit, bf16),
            pltpu.VMEM((2, 2) + unit, f32),
        ]
        sems = []
        for dims in ((2, 4), (2, 2, SIDE), (2, 2, SIDE, 2), (2, 2), (2, 2, 2), (1,)):
            sems += [dma(dims), dma(dims)]
        return bufs, sems

    def copy(self, src, dst, stage, at, device):
        send, recv = self.sems[2 * stage], self.sems[2 * stage + 1]
        return remote(src, dst, send.at[at], recv.at[at], (device, self.z))

    def go(self, copy):
        copy.start()
        self.waits.append(copy)

    def spot(self, tau, di, j):
        if tau == 0:
            return side(self.y + di), j
        return j, side(self.x + di)

    def near(self, tau, axis, d):
        s = 1 - 2 * d
        if (tau == 0) == (axis == 0):
            return device_of(self.y + s, self.x, self.core)
        return device_of(self.y, self.x + s, self.core)

    def from_peer(self, tau, di):
        if tau == 0:
            at = (side(self.y + di), slice(None), 0)
        else:
            at = (slice(None), side(self.x + di), 1)
        return self.copy(
            self.slots.at[at], self.peer_slots.at[at], 0, (tau, di + 1), self.peer
        )

    def share(self):
        for di in (2, 1, -1, 0):
            for tau in (0, 1):

                @pl.loop(0, SIDE)
                def _(j):
                    yy, xx = self.spot(tau, di, j)
                    o = (yy * SIDE + xx) * 2 + tau
                    self.slots[yy, xx, tau] = self.packed[self.index[o], 1 - self.core]

                self.go(self.from_peer(tau, di))

    def term(self, tau, di, j, e):
        yy, xx = self.spot(tau, di, j)
        o = (yy * SIDE + xx) * 2 + tau
        times = self.packed.shape[-1] // self.entry.shape[1]
        mine = jnp.concatenate([self.entry[pl.ds(o, 1), :]] * times, axis=1)
        theirs = jnp.concatenate([self.peer_entry[pl.ds(o, 1), :]] * times, axis=1)
        a = self.packed[self.index[o], self.core].astype(jnp.float32)
        b = self.peer_slots[yy, xx, tau].astype(jnp.float32)
        return jnp.where(mine == e, a, 0.0) + jnp.where(theirs == e, b, 0.0)

    def first(self, tau, d, j):
        at = (tau, d, j)
        return self.copy(self.s1.at[at], self.r1.at[at], 1, at, self.near(tau, 0, d))

    def second(self, tau, d, j, e):
        at = (tau, d, j, e)
        return self.copy(self.s2.at[at], self.r2.at[at], 2, at, self.near(tau, 0, d))

    def third(self, tau, d):
        at = (tau, d)
        return self.copy(self.s3.at[at], self.r3.at[at], 3, at, self.near(tau, 1, d))

    def fourth(self, tau, d, e):
        at = (tau, d, e)
        return self.copy(self.s4.at[at], self.r4.at[at], 4, at, self.near(tau, 1, d))

    def send_first(self):
        for tau in (0, 1):
            self.from_peer(tau, 2).wait_recv()

            @pl.loop(0, SIDE)
            def _(j):
                for d in (0, 1):
                    self.s1[tau, d, j] = self.term(tau, 2, j, d).astype(self.s1.dtype)
                    self.first(tau, d, j).start()

    def send_second_free(self):
        for tau in (0, 1):
            for d in (0, 1):
                self.from_peer(tau, 1 - 2 * d).wait_recv()

            @pl.loop(0, SIDE)
            def _(j):
                for d in (0, 1):
                    value = self.term(tau, 1 - 2 * d, j, 1 - d)
                    self.s2[tau, d, j, 1 - d] = value.astype(self.s2.dtype)
                    self.second(tau, d, j, 1 - d).start()

    def send_second(self, tau):
        @pl.loop(0, SIDE)
        def _(j):
            for d in (0, 1):
                self.first(tau, d, j).wait_recv()
                value = self.term(tau, 1 - 2 * d, j, d) + self.r1[tau, d, j].astype(jnp.float32)
                self.s2[tau, d, j, d] = value.astype(self.s2.dtype)
                self.second(tau, d, j, d).start()

    def keep(self):
        for tau in (0, 1):
            self.from_peer(tau, 0).wait_recv()

            @pl.loop(0, SIDE)
            def _(j):
                for e in (0, 1):
                    self.acc[tau, j, e] = self.term(tau, 0, j, e)

    def total(self, tau, dj, e):
        j = side((self.x if tau == 0 else self.y) + dj)
        for d in (0, 1):
            self.second(tau, d, j, e).wait_recv()
        return (
            self.acc[tau, j, e]
            + self.r2[tau, 0, j, e].astype(jnp.float32)
            + self.r2[tau, 1, j, e].astype(jnp.float32)
        )

    def send_third(self):
        for tau in (0, 1):
            for d in (0, 1):
                self.s3[tau, d] = self.total(tau, 2, d).astype(self.s3.dtype)
                self.go(self.third(tau, d))

    def send_fourth_free(self):
        for tau in (0, 1):
            for d in (0, 1):
                value = self.total(tau, 1 - 2 * d, 1 - d)
                self.s4[tau, d, 1 - d] = value.astype(self.s4.dtype)
                self.go(self.fourth(tau, d, 1 - d))

    def send_fourth(self):
        for tau in (0, 1):
            for d in (0, 1):
                value = self.total(tau, 1 - 2 * d, d)
                self.third(tau, d).wait_recv()
                value += self.r3[tau, d].astype(jnp.float32)
                self.s4[tau, d, d] = value.astype(self.s4.dtype)
                self.go(self.fourth(tau, d, d))

    def finish(self):
        for tau in (0, 1):
            for e in (0, 1):
                value = self.total(tau, 0, e)
                for d in (0, 1):
                    self.fourth(tau, d, e).wait_recv()
                    value += self.r4[tau, d, e].astype(jnp.float32)
                self.res[tau, e] = value
        self.go(self.copy(
            self.res.at[1 - self.core], self.out.at[:, self.core], 5, 0, self.peer
        ))
        self.out[:, self.core] = self.res[self.core]

    def finished(self):
        self.copy(
            self.res.at[1 - self.core], self.out.at[:, 1 - self.core], 5, 0, self.peer
        ).wait_recv()

    def sent(self):
        for copy in self.waits:
            copy.wait_send()
        for tau in (0, 1):
            for d in (0, 1):

                @pl.loop(0, SIDE)
                def _(j):
                    self.first(tau, d, j).wait_send()
                    for e in (0, 1):
                        self.second(tau, d, j, e).wait_send()


REDUCE_BUFS, REDUCE_SEMS, SUM_REFS = 12, 12, 6


def scatter_kernel(
    index, owners, packed, entry, part, cotangent, beside, out_down, out_up, beyond, *rest
):
    rest = list(rest)

    def take(n):
        taken = rest[:n]
        del rest[:n]
        return taken

    peer_entry, lowered, packed_up = take(3)
    sum_refs = take(SUM_REFS)
    down_bufs, down_sems = take(REDUCE_BUFS), take(REDUCE_SEMS)
    up_bufs, up_sems = take(REDUCE_BUFS), take(REDUCE_SEMS)
    entry_send, entry_recv, cot_send, cot_recv = rest
    greet_neighbours()
    downs = PlaneReduce(index, packed, entry, peer_entry, out_down, down_bufs, down_sems)
    ups = PlaneReduce(index, packed_up, entry, peer_entry, out_up, up_bufs, up_sems)
    sums = RingSum(part, lowered, *sum_refs)
    rows = cotangent.shape[0]
    cots = CotangentRing(
        lambda step, d: beside.at[2 + d] if step == 2 else beyond.at[d],
        lambda step, d: beyond.at[d if step == 2 else 2],
        cot_send, cot_recv, rows, (2, 3),
    )
    sums.begin()
    entries = remote(entry, peer_entry, entry_send, entry_recv, (downs.peer, downs.z))
    entries.start()
    cots.launch()
    downs.share()
    sums.step(1)
    cots.launch()
    entries.wait_recv()
    downs.send_first()
    sums.step(2)
    cots.launch()
    downs.send_second_free()
    sums.step(3)
    cots.launch()
    sums.total()
    cots.launch()
    downs.send_second(0)
    sums.onward(1)
    cots.launch()
    downs.send_second(1)
    sums.onward(2)
    cots.launch()
    downs.keep()
    sums.onward(3)
    cots.launch()
    sums.end()

    segments = owners.shape[0]
    seg_rows, keys = rows // segments, cotangent.shape[1]
    ranks = 2 * HALF
    values = []
    for g in range(segments):
        both = lowered[g // 2].reshape(seg_rows, 2 * ranks)
        values.append(lax.dot_general(
            both[:, (g % 2) * ranks : (g % 2 + 1) * ranks],
            cotangent[g * seg_rows : (g + 1) * seg_rows, :],
            (((0,), (0,)), ((), ())),
            preferred_element_type=jnp.float32,
        ))
    for g in range(segments):
        value = values[g]
        for h in range(segments):
            if h != g:
                value = value + jnp.where(owners[h] == owners[g], values[h], 0.0)
        scaled = (value * (ADAPTER_SCALE / seg_rows)).astype(packed_up.dtype)
        packed_up[g] = scaled.reshape(packed_up.shape[1:])

    ups.share()
    ups.send_first()
    ups.send_second_free()
    cots.launch(4)
    ups.keep()
    for tau in (0, 1):
        ups.send_second(tau)
    downs.send_third()
    ups.send_third()
    ups.send_fourth_free()
    downs.send_fourth_free()
    ups.send_fourth()
    downs.send_fourth()
    ups.finish()
    downs.finish()
    ups.finished()
    downs.finished()
    cots.arrived()
    entries.wait_send()
    for each in (downs, ups, sums, cots):
        each.sent()


def scatter_gradients(index, owners, packed, entry, part, cotangent, beside):
    down_unit = packed.shape[2:]
    up_unit = (HALF, cotangent.shape[1])
    bf16, f32 = jnp.bfloat16, jnp.float32
    dma = pltpu.SemaphoreType.DMA
    scalars = pl.BlockSpec(memory_space=pltpu.SMEM)
    whole = pl.BlockSpec(memory_space=pltpu.VMEM)
    anywhere = pl.BlockSpec(memory_space=pl.ANY)
    down_bufs, down_sems = PlaneReduce.scratch(down_unit)
    up_bufs, up_sems = PlaneReduce.scratch(up_unit)
    return pl.pallas_call(
        scatter_kernel,
        out_shape=(
            jax.ShapeDtypeStruct((2, 2) + down_unit, f32),
            jax.ShapeDtypeStruct((2, 2) + up_unit, f32),
            jax.ShapeDtypeStruct((3,) + beside.shape[1:], bf16),
        ),
        in_specs=[scalars, scalars, whole, whole, whole, whole, anywhere],
        out_specs=(whole, whole, anywhere),
        scratch_shapes=[
            pltpu.VMEM(entry.shape, f32),
            pltpu.VMEM(part.shape, bf16),
            pltpu.VMEM((packed.shape[0], 2) + up_unit, bf16),
        ]
        + ring_sum_scratch(part.shape)
        + down_bufs + down_sems + up_bufs + up_sems
        + [dma(()), dma(()), dma((2, 2, CotangentRing.eighths)), dma((2, 2, CotangentRing.eighths))],
        compiler_params=pltpu.CompilerParams(
            collective_id=1, has_side_effects=True, vmem_limit_bytes=30 * MIB
        ),
        name="scatter_gradients",
    )(index, owners, packed, entry, part, cotangent, beside)


def tokens_kernel(
    places, live, cotangent, beside, beyond, frozen, pulled, maps, out, tiles, sems
):
    segments = places.shape[0]
    width, keys = out.shape[1], cotangent.shape[1]
    rows = out.shape[0] // segments
    ranks = 2 * HALF
    z = lax.axis_index("tsp")
    block = tiles.shape[1]
    steps = out.shape[0] // block
    row = lax.broadcasted_iota(jnp.int32, (rows, width), 0)
    offsets = (0, -1, 1, -2, 2, -3, 3, 4)
    weights = jnp.concatenate(
        [frozen[:, pl.ds(pl.multiple_of(ring(z + r) * keys, keys), keys)] for r in offsets],
        axis=1,
    )

    def store(b):
        return pltpu.make_async_copy(
            tiles.at[lax.rem(b, 2)], out.at[pl.ds(b * block, block)], sems.at[lax.rem(b, 2)]
        )

    parts = (
        (beside, 0), (beside, 1), (beside, 2), (beside, 3), (beyond, 0), (beyond, 1), (beyond, 2)
    )

    @pl.loop(0, steps)
    def _(b):
        @pl.when(b >= 2)
        def _():
            store(b - 2).wait()

        here = pl.ds(pl.multiple_of(b * block, block), block)
        left = jnp.concatenate(
            [cotangent[here, :]] + [ref[k, here, :] for ref, k in parts], axis=1
        )
        value = lax.dot_general(
            left, weights, (((1,), (1,)), ((), ())), preferred_element_type=jnp.float32
        )
        for k in range(2):
            g = 2 * b + k
            both = pulled[b].reshape(rows, 2 * ranks)
            extra = jnp.dot(
                both[:, k * ranks : (k + 1) * ranks], maps[places[g]].reshape(ranks, width),
                preferred_element_type=jnp.float32,
            )
            total = value[k * rows : (k + 1) * rows] + ADAPTER_SCALE * extra
            tiles[lax.rem(b, 2), k * rows : (k + 1) * rows] = jnp.where(
                row < live[g], total, 0.0
            ).astype(out.dtype)
        store(b).start()

    for b in (steps - 2, steps - 1):
        store(b).wait()


def token_gradients(places, live, cotangent, beside, beyond, frozen, pulled, maps):
    segments = places.shape[0]
    rows, width = cotangent.shape[0] // segments, frozen.shape[0]
    scalars = pl.BlockSpec(memory_space=pltpu.SMEM)
    whole = pl.BlockSpec(memory_space=pltpu.VMEM)
    return pl.pallas_call(
        tokens_kernel,
        out_shape=jax.ShapeDtypeStruct((segments * rows, width), jnp.bfloat16),
        in_specs=[scalars, scalars] + [whole] * 6,
        out_specs=pl.BlockSpec(memory_space=pl.ANY),
        scratch_shapes=[
            pltpu.VMEM((2, 2 * rows, width), jnp.bfloat16),
            pltpu.SemaphoreType.DMA((2,)),
        ],
        compiler_params=pltpu.CompilerParams(vmem_limit_bytes=28 * MIB),
        name="token_gradients",
    )(places, live, cotangent, beside, beyond, frozen, pulled, maps)


def on_device(
    tokens,
    cotangent,
    frozen_key_weight,
    adapter_down_weight,
    adapter_up_weight,
    adapter_place_table,
    segment_adapter,
    segment_live_count,
):
    dp_count = lax.axis_size("dp")
    held, ranks, width = adapter_down_weight.shape
    keys = cotangent.shape[1]
    live = segment_live_count
    places = lookup(segment_adapter, adapter_place_table)
    owners = places // held
    segment = jnp.arange(places.shape[0], dtype=jnp.int32)
    same = owners[:, None] == owners[None, :]
    heads = jnp.min(jnp.where(same, segment[None, :], places.shape[0]), axis=1)
    owner_hit = owners[:, None] == jnp.arange(dp_count, dtype=jnp.int32)[None, :]
    wanted = jnp.max(jnp.where(owner_hit, (places % held)[:, None], -1), axis=0)
    index = jnp.max(jnp.where(owner_hit, heads[:, None], 0), axis=0)
    entry = jnp.broadcast_to(wanted.astype(jnp.float32)[:, None], (dp_count, 128))
    far = lambda array: pltpu.with_memory_space_constraint(array, pltpu.HBM)
    maps, pulled, tokens_here, cotangent_here, beside = gather_maps(
        places, live,
        far(adapter_down_weight.reshape(held, 2, HALF, width)),
        far(adapter_up_weight.reshape(held, 2, HALF, keys)),
        far(tokens), far(cotangent),
    )
    part, packed = between(places, live, heads, tokens_here, maps, pulled)
    down_grad, up_grad, beyond = scatter_gradients(
        index, owners, packed, entry, part, cotangent_here, beside
    )
    token_gradient = token_gradients(
        places, live, cotangent_here, beside, beyond, frozen_key_weight, pulled, maps
    )
    return (
        token_gradient,
        down_grad.reshape(held, ranks, width),
        up_grad.reshape(held, ranks, keys),
    )


def solution(mesh):
    placed = (
        P("dp", "tsp"),
        P("dp", "tsp"),
        P("tsp", None),
        P("dp", None, "tsp"),
        P("dp", None, "tsp"),
        P(),
        P("dp"),
        P("dp"),
    )
    return jax.shard_map(
        on_device,
        mesh=mesh,
        in_specs=placed,
        out_specs=(P("dp", "tsp"), P("dp", None, "tsp"), P("dp", None, "tsp")),
        check_vma=False,
    )
```

```python
import jax
import jax.numpy as jnp
from jax import lax
from jax.experimental import pallas as pl
from jax.experimental.pallas import tpu as pltpu
from jax.sharding import PartitionSpec as P

ADAPTER_SCALE = 2.0
MESH = pl.DeviceIdType.MESH
SIDE = 4
RING = 8
HALF = 32
MIB = 1024 * 1024
NEAR = (0, -1, 1, 2)
CHIPS = sorted(
    ((dy, dx) for dy in NEAR for dx in NEAR if dy or dx), key=lambda at: -abs(at[0]) - abs(at[1])
)


def lookup(idents, mapping):
    matches = idents[:, None] == jnp.arange(mapping.shape[0], dtype=jnp.int32)[None, :]
    return jnp.sum(jnp.where(matches, mapping[None, :], 0), axis=1)


def place_in_plane():
    me = lax.axis_index("dp")
    core = lax.rem(me, 2)
    chip = lax.div(me, 2)
    return me, core, lax.div(chip, SIDE), lax.rem(chip, SIDE)


def side(v):
    return lax.rem(v + 2 * SIDE, SIDE)


def ring(v):
    return lax.rem(v + 2 * RING, RING)


def device_of(y, x, core):
    return (side(y) * SIDE + side(x)) * 2 + core


def greet_neighbours():
    me, core, y, x = place_in_plane()
    z = lax.axis_index("tsp")
    devices = [(me + 1 - 2 * core, z), (me, ring(z + 1)), (me, ring(z - 1))]
    devices += [(device_of(y + dy, x + dx, core), z) for dy, dx in CHIPS]
    barrier = pltpu.get_barrier_semaphore()
    for device in devices:
        pl.semaphore_signal(barrier, inc=1, device_id=device, device_id_type=MESH)
    pl.semaphore_wait(barrier, len(devices))


def remote(src, dst, send, recv, device):
    return pltpu.make_async_remote_copy(src, dst, send, recv, device, MESH)


class PlaneGather:
    copies = 71

    def __init__(self, mine, out, local_sem, send_sem, recv_sem):
        self.me, self.core, self.y, self.x = place_in_plane()
        self.z = lax.axis_index("tsp")
        self.peer = self.me + 1 - 2 * self.core
        self.mine, self.out = mine, out
        self.local_sem, self.send_sem, self.recv_sem = local_sem, send_sem, recv_sem
        self.ids, self.sends = {}, []

    def make(self, src, dst, device, key):
        k = self.ids.setdefault(key, len(self.ids))
        return remote(src, dst, self.send_sem.at[k], self.recv_sem.at[k], (device, self.z))

    def send(self, ref, device, key):
        copy = self.make(ref, ref, device, key)
        copy.start()
        self.sends.append(copy)

    def arrived(self, ref, key):
        self.make(ref, ref, self.peer, key).wait_recv()

    def spot(self, tau, di, dj, core):
        if tau == 0:
            return device_of(self.y + dj, self.x + di, core)
        return device_of(self.y + di, self.x + dj, core)

    def near(self, tau, di, dj):
        return self.spot(tau, di, dj, self.core)

    def block(self, tau, di, dj, half):
        return self.out.at[pl.ds(2 * self.spot(tau, di, dj, tau), 2), half]

    def unit(self, tau, di, dj, e):
        return self.out.at[2 * self.spot(tau, di, dj, tau) + e, self.core]

    def swap(self, tau, di, dj):
        self.send(self.block(tau, di, dj, self.core), self.peer, ("swap", tau, di, dj))

    def own(self):
        here = self.out.at[pl.ds(2 * self.me, 2)]
        self.local = pltpu.make_async_copy(self.mine, here, self.local_sem)
        self.local.start()
        copy = self.make(self.mine, here, self.peer, "own")
        copy.start()
        self.sends.append(copy)

    def own_arrived(self):
        self.local.wait()
        self.make(self.mine, self.out.at[pl.ds(2 * self.peer, 2)], self.peer, "own").wait_recv()

    def one(self):
        for tau in (0, 1):
            for s in (1, -1):
                self.send(self.block(tau, 0, 0, self.core), self.near(tau, s, 0), ("one", tau, s))

    def two(self, *offsets):
        for di in offsets:
            for tau in (0, 1):
                for t in (1, -1):
                    self.send(
                        self.block(tau, di, 0, self.core), self.near(tau, 0, t), ("two", tau, di, t)
                    )

    def one_arrived(self):
        for tau in (0, 1):
            for s in (1, -1):
                self.arrived(self.block(tau, -s, 0, self.core), ("one", tau, s))
                e = 0 if s == 1 else 1
                self.send(self.unit(tau, -s, 0, e), self.near(tau, s, 0), ("onward", tau, s))
        self.two(-1, 1)
        for tau in (0, 1):
            for s in (1, -1):
                self.swap(tau, -s, 0)

    def onward_arrived(self):
        for tau in (0, 1):
            self.arrived(self.unit(tau, 2, 0, 0), ("onward", tau, 1))
            self.arrived(self.unit(tau, 2, 0, 1), ("onward", tau, -1))
        self.two(2)
        for tau in (0, 1):
            self.swap(tau, 2, 0)

    def two_arrived(self, di):
        for tau in (0, 1):
            for t in (1, -1):
                self.arrived(self.block(tau, di, -t, self.core), ("two", tau, di, t))
                e = 0 if t == 1 else 1
                self.send(
                    self.unit(tau, di, -t, e), self.near(tau, 0, t), ("last", tau, di, t)
                )
                self.swap(tau, di, -t)

    def last_arrived(self, di):
        for tau in (0, 1):
            self.arrived(self.unit(tau, di, 2, 0), ("last", tau, di, 1))
            self.arrived(self.unit(tau, di, 2, 1), ("last", tau, di, -1))
            self.swap(tau, di, 2)

    def swaps_arrived(self):
        for tau in (0, 1):
            for di in NEAR:
                for dj in NEAR:
                    if di or dj:
                        self.arrived(self.block(tau, di, dj, 1 - self.core), ("swap", tau, di, dj))

    def sent(self):
        for copy in self.sends:
            copy.wait_send()


class DirectGather:
    copies = 2 * len(CHIPS) + 1

    def __init__(self, mine, out, local_sem, send_sem, recv_sem):
        self.me, self.core, self.y, self.x = place_in_plane()
        self.z = lax.axis_index("tsp")
        self.peer = self.me + 1 - 2 * self.core
        self.mine, self.out = mine, out
        self.local_sem, self.send_sem, self.recv_sem = local_sem, send_sem, recv_sem
        self.sends = []

    def block(self, device):
        return self.out.at[pl.ds(2 * device, 2)]

    def copy(self, src, dst, device, k):
        return remote(src, dst, self.send_sem.at[k], self.recv_sem.at[k], (device, self.z))

    def send(self, src, dst, device, k):
        copy = self.copy(src, dst, device, k)
        copy.start()
        self.sends.append(copy)

    def own(self):
        here = self.block(self.me)
        for k, (dy, dx) in enumerate(CHIPS):
            self.send(self.mine, here, device_of(self.y + dy, self.x + dx, self.core), k)
        self.send(self.mine, here, self.peer, 2 * len(CHIPS))
        self.local = pltpu.make_async_copy(self.mine, here, self.local_sem)
        self.local.start()

    def pass_across(self):
        for k, (dy, dx) in reversed(list(enumerate(CHIPS))):
            block = self.block(device_of(self.y - dy, self.x - dx, self.core))
            self.copy(block, block, self.peer, k).wait_recv()
            self.send(block, block, self.peer, len(CHIPS) + k)

    def arrived(self):
        self.local.wait()
        block = self.block(self.peer)
        self.copy(block, block, self.peer, 2 * len(CHIPS)).wait_recv()
        for k, (dy, dx) in reversed(list(enumerate(CHIPS))):
            block = self.block(device_of(self.y - dy, self.x - dx, 1 - self.core))
            self.copy(block, block, self.peer, len(CHIPS) + k).wait_recv()

    def sent(self):
        for copy in self.sends:
            copy.wait_send()


class RingSum:
    def __init__(self, part, out, held, passed, send_sem, recv_sem, out_send, out_recv):
        self.me, self.i = lax.axis_index("dp"), lax.axis_index("tsp")
        self.part, self.out, self.held, self.passed = part, out, held, passed
        self.send_sem, self.recv_sem = send_sem, recv_sem
        self.out_send, self.out_recv = out_send, out_recv
        self.copies = []

    def copy(self, src, d, step, u):
        return remote(
            src, self.held.at[d, step, u], self.send_sem.at[d, step, u],
            self.recv_sem.at[d, step, u], (self.me, ring(self.i + 1 - 2 * d)),
        )

    def send(self, src, d, step, u):
        copy = self.copy(src, d, step, u)
        copy.start()
        self.copies.append(copy)

    def begin(self):
        for d in (0, 1):
            self.send(self.part.at[ring(self.i + 4), d], d, 0, d)
        for d in (0, 1):
            s = 1 - 2 * d
            self.send(self.part.at[ring(self.i + 3 * s), 1 - d], d, 1, 1 - d)

    def step(self, step):
        for v in (0, 1):
            for d in (0, 1):
                u = v if d == 0 else 1 - v
                if step == 1 and v == 1:
                    continue
                s = 1 - 2 * d
                self.copy(self.held.at[d, step - 1, u], d, step - 1, u).wait_recv()
                self.passed[d, step, u] = (
                    self.held[d, step - 1, u] + self.part[ring(self.i + s * (4 - step)), u]
                )
                self.send(self.passed.at[d, step, u], d, step, u)

    def pass_on(self, chunk, u, d, step):
        ref = self.out.at[ring(chunk)] if u is None else self.out.at[ring(chunk), u]
        return remote(
            ref, ref, self.out_send.at[d, step], self.out_recv.at[d, step],
            (self.me, ring(self.i + 1 - 2 * d)),
        )

    def total(self):
        for u in (0, 1):
            for d in (0, 1):
                self.copy(self.held.at[d, 3, u], d, 3, u).wait_recv()
            self.out[self.i, u] = (
                self.part[self.i, u] + self.held[0, 3, u] + self.held[1, 3, u]
            ).astype(self.out.dtype)
        for d in (0, 1):
            copy = self.pass_on(self.i, None, d, 0)
            copy.start()
            self.copies.append(copy)

    def onward(self, step):
        for d in (0, 1):
            s = 1 - 2 * d
            self.pass_on(self.i - step * s, None, d, step - 1).wait_recv()
            copy = self.pass_on(self.i - step * s, d if step == 3 else None, d, step)
            copy.start()
            self.copies.append(copy)

    def end(self):
        for d in (0, 1):
            self.pass_on(self.i + 4, d, d, 3).wait_recv()

    def sent(self):
        for copy in self.copies:
            copy.wait_send()


def ring_sum_scratch(part):
    dma = pltpu.SemaphoreType.DMA
    shape = (2, 4, 2) + part[2:]
    return [
        pltpu.VMEM(shape, jnp.float32), pltpu.VMEM(shape, jnp.float32),
        dma((2, 4, 2)), dma((2, 4, 2)), dma((2, 4)), dma((2, 4)),
    ]


class CotangentRing:
    eighths = 8

    def __init__(self, source, target, send_sem, recv_sem, rows, steps):
        self.me, self.z = lax.axis_index("dp"), lax.axis_index("tsp")
        self.source, self.target = source, target
        self.send_sem, self.recv_sem = send_sem, recv_sem
        self.size = rows // self.eighths
        self.copies = []
        self.origin = steps[0]
        self.queue, self.waited = [], set()
        for step in steps:
            for k in range(self.eighths if step < 3 else self.eighths // 2):
                pieces = [(step, 0, k), (step, 1, k if step < 3 else k + self.eighths // 2)]
                self.queue.append(pieces)

    def copy(self, step, d, q):
        here = pl.ds(q * self.size, self.size)
        src, dst = self.source(step, d), self.target(step, d)
        at = (step - self.origin, d, q)
        return remote(
            src.at[here], dst.at[here], self.send_sem.at[at], self.recv_sem.at[at],
            (self.me, ring(self.z + 1 - 2 * d)),
        )

    def wait(self, step, d, q):
        if step >= self.origin and (step, d, q) not in self.waited:
            self.waited.add((step, d, q))
            self.copy(step, d, q).wait_recv()

    def launch(self, count=1):
        for pieces in self.queue[:count]:
            for step, d, q in pieces:
                self.wait(step - 1, d, q)
                copy = self.copy(step, d, q)
                copy.start()
                self.copies.append((copy, (step, d, q)))
        self.queue = self.queue[count:]

    def arrived(self):
        for _, piece in self.copies:
            self.wait(*piece)

    def sent(self):
        for copy, _ in self.copies:
            copy.wait_send()


def gather_kernel(
    places, live, down, up, tokens, cotangent,
    down_maps, pulled, tokens_here, cotangent_here, beside,
    up_maps, part, held, passed, send_sem, recv_sem, out_send, out_recv,
    local_sem, down_send, down_recv, up_send, up_recv, cot_send, cot_recv,
):
    greet_neighbours()
    downs = PlaneGather(down, down_maps, local_sem.at[0], down_send, down_recv)
    ups = DirectGather(up, up_maps, local_sem.at[1], up_send, up_recv)
    sums = RingSum(part, pulled, held, passed, send_sem, recv_sem, out_send, out_recv)
    cots = CotangentRing(
        lambda step, d: cotangent if step == 0 else beside.at[d],
        lambda step, d: beside.at[2 * step + d],
        cot_send, cot_recv, cotangent.shape[0], (0, 1),
    )
    ups.own()
    downs.own()
    cotangent_copy = pltpu.make_async_copy(cotangent, cotangent_here, local_sem.at[2])
    cotangent_copy.start()
    tokens_copy = pltpu.make_async_copy(tokens, tokens_here, local_sem.at[3])
    tokens_copy.start()
    cots.launch(6)
    downs.own_arrived()
    downs.one()
    downs.two(0)
    ups.pass_across()
    ups.arrived()
    cotangent_copy.wait()

    segments = places.shape[0]
    rows = cotangent.shape[0] // segments
    ranks, keys = 2 * HALF, cotangent.shape[1]
    row = lax.broadcasted_iota(jnp.int32, (rows, ranks), 0)
    for j in range(segments // 2):
        pair = []
        for g in (2 * j, 2 * j + 1):
            term = lax.dot_general(
                cotangent_here[g * rows : (g + 1) * rows, :],
                up_maps[places[g]].reshape(ranks, keys),
                (((1,), (1,)), ((), ())),
                preferred_element_type=jnp.float32,
            )
            pair.append(jnp.where(row < live[g], term, 0.0))
        part[j] = jnp.concatenate(pair, axis=1).reshape(part.shape[1:])
    sums.begin()
    cots.launch()
    downs.one_arrived()
    sums.step(1)
    cots.launch()
    downs.two_arrived(0)
    sums.step(2)
    cots.launch()
    downs.onward_arrived()
    sums.step(3)
    cots.launch()
    downs.two_arrived(-1)
    sums.total()
    cots.launch()
    downs.two_arrived(1)
    sums.onward(1)
    cots.launch()
    downs.two_arrived(2)
    sums.onward(2)
    cots.launch()
    downs.last_arrived(0)
    downs.last_arrived(-1)
    sums.onward(3)
    cots.launch(3)
    downs.last_arrived(1)
    downs.last_arrived(2)
    sums.end()
    downs.swaps_arrived()
    tokens_copy.wait()
    cots.arrived()
    for each in (ups, downs, sums, cots):
        each.sent()


def gather_maps(places, live, down, up, tokens, cotangent):
    count = 2 * lax.axis_size("dp")
    rows = cotangent.shape[0] // places.shape[0]
    ranks = 2 * HALF
    part = (places.shape[0] // 2, 2, rows // 2, 2 * ranks)
    bf16 = jnp.bfloat16
    dma = pltpu.SemaphoreType.DMA
    scalars = pl.BlockSpec(memory_space=pltpu.SMEM)
    whole = pl.BlockSpec(memory_space=pltpu.VMEM)
    anywhere = pl.BlockSpec(memory_space=pl.ANY)
    far = pl.BlockSpec(memory_space=pltpu.HBM)
    return pl.pallas_call(
        gather_kernel,
        out_shape=(
            jax.ShapeDtypeStruct((count,) + down.shape[1:], bf16),
            jax.ShapeDtypeStruct(part, bf16),
            jax.ShapeDtypeStruct(tokens.shape, bf16),
            jax.ShapeDtypeStruct(cotangent.shape, bf16),
            jax.ShapeDtypeStruct((4,) + cotangent.shape, bf16),
        ),
        in_specs=[scalars, scalars, far, far, far, far],
        out_specs=(anywhere, whole, whole, whole, anywhere),
        scratch_shapes=[pltpu.VMEM((count,) + up.shape[1:], bf16), pltpu.VMEM(part, jnp.float32)]
        + ring_sum_scratch(part)
        + [dma((4,))]
        + [dma((PlaneGather.copies,)) for _ in range(2)]
        + [dma((DirectGather.copies,)) for _ in range(2)]
        + [dma((2, 2, CotangentRing.eighths)), dma((2, 2, CotangentRing.eighths))],
        compiler_params=pltpu.CompilerParams(
            collective_id=0, has_side_effects=True, vmem_limit_bytes=12 * MIB
        ),
        name="gather_maps",
    )(places, live, down, up, tokens, cotangent)


def between_kernel(places, live, heads, tokens, maps, pulled, part, packed, total):
    segments = places.shape[0]
    rows, width = tokens.shape[0] // segments, tokens.shape[1]
    ranks = 2 * HALF
    row = lax.broadcasted_iota(jnp.int32, (rows, ranks), 0)
    for j in range(segments // 2):
        both = pulled[j].reshape(rows, 2 * ranks)
        pair = []
        for k in (0, 1):
            g = 2 * j + k
            here = slice(g * rows, (g + 1) * rows)
            term = lax.dot_general(
                tokens[here, :], maps[places[g]].reshape(ranks, width),
                (((1,), (1,)), ((), ())), preferred_element_type=jnp.float32,
            )
            pair.append(jnp.where(row < live[g], term, 0.0))
            value = lax.dot_general(
                both[:, k * ranks : (k + 1) * ranks], tokens[here, :],
                (((0,), (0,)), ((), ())), preferred_element_type=jnp.float32,
            )
            h = heads[g]
            total[h] = jnp.where(h == g, value, total[h] + value)
        part[j] = jnp.concatenate(pair, axis=1).reshape(part.shape[1:])

    @pl.loop(0, segments)
    def _(g):
        scaled = (total[g] * (ADAPTER_SCALE / rows)).astype(packed.dtype)
        packed[g] = scaled.reshape(packed.shape[1:])


def between(places, live, heads, tokens, maps, pulled):
    segments, width = places.shape[0], tokens.shape[1]
    scalars = pl.BlockSpec(memory_space=pltpu.SMEM)
    whole = pl.BlockSpec(memory_space=pltpu.VMEM)
    return pl.pallas_call(
        between_kernel,
        out_shape=(
            jax.ShapeDtypeStruct(pulled.shape, jnp.float32),
            jax.ShapeDtypeStruct((segments, 2, HALF, width), jnp.bfloat16),
        ),
        in_specs=[scalars] * 3 + [whole] * 3,
        out_specs=(whole, whole),
        scratch_shapes=[pltpu.VMEM((segments, 2 * HALF, width), jnp.float32)],
        compiler_params=pltpu.CompilerParams(vmem_limit_bytes=24 * MIB),
        name="between",
    )(places, live, heads, tokens, maps, pulled)


class PlaneReduce:
    def __init__(self, index, packed, entry, peer_entry, out, bufs, sems):
        self.me, self.core, self.y, self.x = place_in_plane()
        self.z = lax.axis_index("tsp")
        self.peer = self.me + 1 - 2 * self.core
        self.index, self.packed, self.entry, self.peer_entry = index, packed, entry, peer_entry
        self.out = out
        (
            self.slots, self.peer_slots, self.s1, self.r1, self.s2, self.r2,
            self.acc, self.s3, self.r3, self.s4, self.r4, self.res,
        ) = bufs
        self.sems = sems
        self.waits = []

    @staticmethod
    def scratch(unit):
        bf16, f32 = jnp.bfloat16, jnp.float32
        dma = pltpu.SemaphoreType.DMA
        bufs = [
            pltpu.VMEM((SIDE, SIDE, 2) + unit, bf16),
            pltpu.VMEM((SIDE, SIDE, 2) + unit, bf16),
            pltpu.VMEM((2, 2, SIDE) + unit, bf16),
            pltpu.VMEM((2, 2, SIDE) + unit, bf16),
            pltpu.VMEM((2, 2, SIDE, 2) + unit, bf16),
            pltpu.VMEM((2, 2, SIDE, 2) + unit, bf16),
            pltpu.VMEM((2, SIDE, 2) + unit, f32),
            pltpu.VMEM((2, 2) + unit, bf16),
            pltpu.VMEM((2, 2) + unit, bf16),
            pltpu.VMEM((2, 2, 2) + unit, bf16),
            pltpu.VMEM((2, 2, 2) + unit, bf16),
            pltpu.VMEM((2, 2) + unit, f32),
        ]
        sems = []
        for dims in ((2, 4), (2, 2, SIDE), (2, 2, SIDE, 2), (2, 2), (2, 2, 2), (1,)):
            sems += [dma(dims), dma(dims)]
        return bufs, sems

    def copy(self, src, dst, stage, at, device):
        send, recv = self.sems[2 * stage], self.sems[2 * stage + 1]
        return remote(src, dst, send.at[at], recv.at[at], (device, self.z))

    def go(self, copy):
        copy.start()
        self.waits.append(copy)

    def spot(self, tau, di, j):
        if tau == 0:
            return side(self.y + di), j
        return j, side(self.x + di)

    def near(self, tau, axis, d):
        s = 1 - 2 * d
        if (tau == 0) == (axis == 0):
            return device_of(self.y + s, self.x, self.core)
        return device_of(self.y, self.x + s, self.core)

    def from_peer(self, tau, di):
        if tau == 0:
            at = (side(self.y + di), slice(None), 0)
        else:
            at = (slice(None), side(self.x + di), 1)
        return self.copy(
            self.slots.at[at], self.peer_slots.at[at], 0, (tau, di + 1), self.peer
        )

    def share(self):
        for di in (2, 1, -1, 0):
            for tau in (0, 1):

                @pl.loop(0, SIDE)
                def _(j):
                    yy, xx = self.spot(tau, di, j)
                    o = (yy * SIDE + xx) * 2 + tau
                    self.slots[yy, xx, tau] = self.packed[self.index[o], 1 - self.core]

                self.go(self.from_peer(tau, di))

    def term(self, tau, di, j, e):
        yy, xx = self.spot(tau, di, j)
        o = (yy * SIDE + xx) * 2 + tau
        times = self.packed.shape[-1] // self.entry.shape[1]
        mine = jnp.concatenate([self.entry[pl.ds(o, 1), :]] * times, axis=1)
        theirs = jnp.concatenate([self.peer_entry[pl.ds(o, 1), :]] * times, axis=1)
        a = self.packed[self.index[o], self.core].astype(jnp.float32)
        b = self.peer_slots[yy, xx, tau].astype(jnp.float32)
        return jnp.where(mine == e, a, 0.0) + jnp.where(theirs == e, b, 0.0)

    def first(self, tau, d, j):
        at = (tau, d, j)
        return self.copy(self.s1.at[at], self.r1.at[at], 1, at, self.near(tau, 0, d))

    def second(self, tau, d, j, e):
        at = (tau, d, j, e)
        return self.copy(self.s2.at[at], self.r2.at[at], 2, at, self.near(tau, 0, d))

    def third(self, tau, d):
        at = (tau, d)
        return self.copy(self.s3.at[at], self.r3.at[at], 3, at, self.near(tau, 1, d))

    def fourth(self, tau, d, e):
        at = (tau, d, e)
        return self.copy(self.s4.at[at], self.r4.at[at], 4, at, self.near(tau, 1, d))

    def send_first(self):
        for tau in (0, 1):
            self.from_peer(tau, 2).wait_recv()

            @pl.loop(0, SIDE)
            def _(j):
                for d in (0, 1):
                    self.s1[tau, d, j] = self.term(tau, 2, j, d).astype(self.s1.dtype)
                    self.first(tau, d, j).start()

    def send_second_free(self):
        for tau in (0, 1):
            for d in (0, 1):
                self.from_peer(tau, 1 - 2 * d).wait_recv()

            @pl.loop(0, SIDE)
            def _(j):
                for d in (0, 1):
                    value = self.term(tau, 1 - 2 * d, j, 1 - d)
                    self.s2[tau, d, j, 1 - d] = value.astype(self.s2.dtype)
                    self.second(tau, d, j, 1 - d).start()

    def send_second(self, tau):
        @pl.loop(0, SIDE)
        def _(j):
            for d in (0, 1):
                self.first(tau, d, j).wait_recv()
                value = self.term(tau, 1 - 2 * d, j, d) + self.r1[tau, d, j].astype(jnp.float32)
                self.s2[tau, d, j, d] = value.astype(self.s2.dtype)
                self.second(tau, d, j, d).start()

    def keep(self):
        for tau in (0, 1):
            self.from_peer(tau, 0).wait_recv()

            @pl.loop(0, SIDE)
            def _(j):
                for e in (0, 1):
                    self.acc[tau, j, e] = self.term(tau, 0, j, e)

    def total(self, tau, dj, e):
        j = side((self.x if tau == 0 else self.y) + dj)
        for d in (0, 1):
            self.second(tau, d, j, e).wait_recv()
        return (
            self.acc[tau, j, e]
            + self.r2[tau, 0, j, e].astype(jnp.float32)
            + self.r2[tau, 1, j, e].astype(jnp.float32)
        )

    def send_third(self):
        for tau in (0, 1):
            for d in (0, 1):
                self.s3[tau, d] = self.total(tau, 2, d).astype(self.s3.dtype)
                self.go(self.third(tau, d))

    def send_fourth_free(self):
        for tau in (0, 1):
            for d in (0, 1):
                value = self.total(tau, 1 - 2 * d, 1 - d)
                self.s4[tau, d, 1 - d] = value.astype(self.s4.dtype)
                self.go(self.fourth(tau, d, 1 - d))

    def send_fourth(self):
        for tau in (0, 1):
            for d in (0, 1):
                value = self.total(tau, 1 - 2 * d, d)
                self.third(tau, d).wait_recv()
                value += self.r3[tau, d].astype(jnp.float32)
                self.s4[tau, d, d] = value.astype(self.s4.dtype)
                self.go(self.fourth(tau, d, d))

    def finish(self):
        for tau in (0, 1):
            for e in (0, 1):
                value = self.total(tau, 0, e)
                for d in (0, 1):
                    self.fourth(tau, d, e).wait_recv()
                    value += self.r4[tau, d, e].astype(jnp.float32)
                self.res[tau, e] = value
        self.go(self.copy(
            self.res.at[1 - self.core], self.out.at[:, self.core], 5, 0, self.peer
        ))
        self.out[:, self.core] = self.res[self.core]

    def finished(self):
        self.copy(
            self.res.at[1 - self.core], self.out.at[:, 1 - self.core], 5, 0, self.peer
        ).wait_recv()

    def sent(self):
        for copy in self.waits:
            copy.wait_send()
        for tau in (0, 1):
            for d in (0, 1):

                @pl.loop(0, SIDE)
                def _(j):
                    self.first(tau, d, j).wait_send()
                    for e in (0, 1):
                        self.second(tau, d, j, e).wait_send()


class DirectReduce:
    def __init__(self, index, packed, entry, peer_entry, out, bufs, sems):
        self.me, self.core, self.y, self.x = place_in_plane()
        self.z = lax.axis_index("tsp")
        self.peer = self.me + 1 - 2 * self.core
        self.index, self.packed, self.entry, self.peer_entry = index, packed, entry, peer_entry
        self.out = out
        self.slots, self.peer_slots, self.terms, self.landed, self.res = bufs
        self.send_sem, self.recv_sem = sems
        self.waits = []

    @staticmethod
    def scratch(unit):
        bf16 = jnp.bfloat16
        dma = pltpu.SemaphoreType.DMA
        chips = SIDE * SIDE
        bufs = [
            pltpu.VMEM((chips, 2) + unit, bf16),
            pltpu.VMEM((chips, 2) + unit, bf16),
            pltpu.VMEM((chips, 2, 2) + unit, bf16),
            pltpu.VMEM((len(CHIPS), 2, 2) + unit, bf16),
            pltpu.VMEM((2, 2) + unit, jnp.float32),
        ]
        return bufs, [dma((len(CHIPS) + 2,)), dma((len(CHIPS) + 2,))]

    def copy(self, src, dst, device, k):
        return remote(src, dst, self.send_sem.at[k], self.recv_sem.at[k], (device, self.z))

    def go(self, copy):
        copy.start()
        self.waits.append(copy)

    def share(self):
        @pl.loop(0, SIDE * SIDE)
        def _(q):
            for tau in (0, 1):
                self.slots[q, tau] = self.packed[self.index[2 * q + tau], 1 - self.core]

        self.go(self.copy(self.slots, self.peer_slots, self.peer, len(CHIPS)))

    def term(self, q, tau, e):
        o = 2 * q + tau
        a = self.packed[self.index[o], self.core].astype(jnp.float32)
        b = self.peer_slots[q, tau].astype(jnp.float32)
        return jnp.where(self.entry[pl.ds(o, 1), :] == e, a, 0.0) + jnp.where(
            self.peer_entry[pl.ds(o, 1), :] == e, b, 0.0
        )

    def send_all(self):
        self.copy(self.slots, self.peer_slots, self.peer, len(CHIPS)).wait_recv()

        @pl.loop(0, SIDE * SIDE)
        def _(q):
            for tau in (0, 1):
                for e in (0, 1):
                    self.terms[q, tau, e] = self.term(q, tau, e).astype(self.terms.dtype)

        for k, (dy, dx) in enumerate(CHIPS):
            device = device_of(self.y + dy, self.x + dx, self.core)
            self.go(self.copy(
                self.terms.at[lax.div(device, 2)], self.landed.at[k], device, k
            ))

    def finish(self):
        for k in range(len(CHIPS)):
            self.copy(self.landed.at[k], self.landed.at[k], self.peer, k).wait_recv()
        for tau in (0, 1):
            for e in (0, 1):
                value = self.term(lax.div(self.me, 2), tau, e)
                for k in range(len(CHIPS)):
                    value += self.landed[k, tau, e].astype(jnp.float32)
                self.res[tau, e] = value
        self.go(self.copy(
            self.res.at[1 - self.core], self.out.at[:, self.core], self.peer, len(CHIPS) + 1
        ))
        self.out[:, self.core] = self.res[self.core]

    def finished(self):
        self.copy(
            self.res.at[1 - self.core], self.out.at[:, 1 - self.core], self.peer, len(CHIPS) + 1
        ).wait_recv()

    def sent(self):
        for copy in self.waits:
            copy.wait_send()


REDUCE_BUFS, REDUCE_SEMS, SUM_REFS = 12, 12, 6


def scatter_kernel(
    index, owners, packed, entry, part, cotangent, beside, out_down, out_up, beyond, *rest
):
    rest = list(rest)

    def take(n):
        taken = rest[:n]
        del rest[:n]
        return taken

    peer_entry, lowered, packed_up = take(3)
    sum_refs = take(SUM_REFS)
    down_bufs, down_sems = take(REDUCE_BUFS), take(REDUCE_SEMS)
    up_bufs, up_sems = take(5), take(2)
    entry_send, entry_recv, cot_send, cot_recv = rest
    greet_neighbours()
    downs = PlaneReduce(index, packed, entry, peer_entry, out_down, down_bufs, down_sems)
    ups = DirectReduce(index, packed_up, entry, peer_entry, out_up, up_bufs, up_sems)
    sums = RingSum(part, lowered, *sum_refs)
    rows = cotangent.shape[0]
    cots = CotangentRing(
        lambda step, d: beside.at[2 + d] if step == 2 else beyond.at[d],
        lambda step, d: beyond.at[d if step == 2 else 2],
        cot_send, cot_recv, rows, (2, 3),
    )
    sums.begin()
    entries = remote(entry, peer_entry, entry_send, entry_recv, (downs.peer, downs.z))
    entries.start()
    cots.launch()
    downs.share()
    sums.step(1)
    cots.launch()
    entries.wait_recv()
    downs.send_first()
    sums.step(2)
    cots.launch()
    downs.send_second_free()
    sums.step(3)
    cots.launch()
    sums.total()
    cots.launch()
    downs.send_second(0)
    sums.onward(1)
    cots.launch()
    downs.send_second(1)
    sums.onward(2)
    cots.launch()
    downs.keep()
    sums.onward(3)
    cots.launch()
    sums.end()

    segments = owners.shape[0]
    seg_rows, keys = rows // segments, cotangent.shape[1]
    ranks = 2 * HALF
    values = []
    for g in range(segments):
        both = lowered[g // 2].reshape(seg_rows, 2 * ranks)
        values.append(lax.dot_general(
            both[:, (g % 2) * ranks : (g % 2 + 1) * ranks],
            cotangent[g * seg_rows : (g + 1) * seg_rows, :],
            (((0,), (0,)), ((), ())),
            preferred_element_type=jnp.float32,
        ))
    for g in range(segments):
        value = values[g]
        for h in range(segments):
            if h != g:
                value = value + jnp.where(owners[h] == owners[g], values[h], 0.0)
        scaled = (value * (ADAPTER_SCALE / seg_rows)).astype(packed_up.dtype)
        packed_up[g] = scaled.reshape(packed_up.shape[1:])

    ups.share()
    downs.send_third()
    ups.send_all()
    cots.launch(4)
    downs.send_fourth_free()
    downs.send_fourth()
    downs.finish()
    ups.finish()
    downs.finished()
    ups.finished()
    cots.arrived()
    entries.wait_send()
    for each in (downs, ups, sums, cots):
        each.sent()


def scatter_gradients(index, owners, packed, entry, part, cotangent, beside):
    down_unit = packed.shape[2:]
    up_unit = (HALF, cotangent.shape[1])
    bf16, f32 = jnp.bfloat16, jnp.float32
    dma = pltpu.SemaphoreType.DMA
    scalars = pl.BlockSpec(memory_space=pltpu.SMEM)
    whole = pl.BlockSpec(memory_space=pltpu.VMEM)
    anywhere = pl.BlockSpec(memory_space=pl.ANY)
    down_bufs, down_sems = PlaneReduce.scratch(down_unit)
    up_bufs, up_sems = DirectReduce.scratch(up_unit)
    return pl.pallas_call(
        scatter_kernel,
        out_shape=(
            jax.ShapeDtypeStruct((2, 2) + down_unit, f32),
            jax.ShapeDtypeStruct((2, 2) + up_unit, f32),
            jax.ShapeDtypeStruct((3,) + beside.shape[1:], bf16),
        ),
        in_specs=[scalars, scalars, whole, whole, whole, whole, anywhere],
        out_specs=(whole, whole, anywhere),
        scratch_shapes=[
            pltpu.VMEM(entry.shape, f32),
            pltpu.VMEM(part.shape, bf16),
            pltpu.VMEM((packed.shape[0], 2) + up_unit, bf16),
        ]
        + ring_sum_scratch(part.shape)
        + down_bufs + down_sems + up_bufs + up_sems
        + [dma(()), dma(()), dma((2, 2, CotangentRing.eighths)), dma((2, 2, CotangentRing.eighths))],
        compiler_params=pltpu.CompilerParams(
            collective_id=1, has_side_effects=True, vmem_limit_bytes=30 * MIB
        ),
        name="scatter_gradients",
    )(index, owners, packed, entry, part, cotangent, beside)


def tokens_kernel(
    places, live, cotangent, beside, beyond, frozen, pulled, maps, out, tiles, sems
):
    segments = places.shape[0]
    width, keys = out.shape[1], cotangent.shape[1]
    rows = out.shape[0] // segments
    ranks = 2 * HALF
    z = lax.axis_index("tsp")
    block = tiles.shape[1]
    steps = out.shape[0] // block
    row = lax.broadcasted_iota(jnp.int32, (rows, width), 0)
    offsets = (0, -1, 1, -2, 2, -3, 3, 4)
    weights = jnp.concatenate(
        [frozen[:, pl.ds(pl.multiple_of(ring(z + r) * keys, keys), keys)] for r in offsets],
        axis=1,
    )

    def store(b):
        return pltpu.make_async_copy(
            tiles.at[lax.rem(b, 2)], out.at[pl.ds(b * block, block)], sems.at[lax.rem(b, 2)]
        )

    parts = (
        (beside, 0), (beside, 1), (beside, 2), (beside, 3), (beyond, 0), (beyond, 1), (beyond, 2)
    )

    @pl.loop(0, steps)
    def _(b):
        @pl.when(b >= 2)
        def _():
            store(b - 2).wait()

        here = pl.ds(pl.multiple_of(b * block, block), block)
        left = jnp.concatenate(
            [cotangent[here, :]] + [ref[k, here, :] for ref, k in parts], axis=1
        )
        value = lax.dot_general(
            left, weights, (((1,), (1,)), ((), ())), preferred_element_type=jnp.float32
        )
        for k in range(2):
            g = 2 * b + k
            both = pulled[b].reshape(rows, 2 * ranks)
            extra = jnp.dot(
                both[:, k * ranks : (k + 1) * ranks], maps[places[g]].reshape(ranks, width),
                preferred_element_type=jnp.float32,
            )
            total = value[k * rows : (k + 1) * rows] + ADAPTER_SCALE * extra
            tiles[lax.rem(b, 2), k * rows : (k + 1) * rows] = jnp.where(
                row < live[g], total, 0.0
            ).astype(out.dtype)
        store(b).start()

    for b in (steps - 2, steps - 1):
        store(b).wait()


def token_gradients(places, live, cotangent, beside, beyond, frozen, pulled, maps):
    segments = places.shape[0]
    rows, width = cotangent.shape[0] // segments, frozen.shape[0]
    scalars = pl.BlockSpec(memory_space=pltpu.SMEM)
    whole = pl.BlockSpec(memory_space=pltpu.VMEM)
    return pl.pallas_call(
        tokens_kernel,
        out_shape=jax.ShapeDtypeStruct((segments * rows, width), jnp.bfloat16),
        in_specs=[scalars, scalars] + [whole] * 6,
        out_specs=pl.BlockSpec(memory_space=pl.ANY),
        scratch_shapes=[
            pltpu.VMEM((2, 2 * rows, width), jnp.bfloat16),
            pltpu.SemaphoreType.DMA((2,)),
        ],
        compiler_params=pltpu.CompilerParams(vmem_limit_bytes=28 * MIB),
        name="token_gradients",
    )(places, live, cotangent, beside, beyond, frozen, pulled, maps)


def on_device(
    tokens,
    cotangent,
    frozen_key_weight,
    adapter_down_weight,
    adapter_up_weight,
    adapter_place_table,
    segment_adapter,
    segment_live_count,
):
    dp_count = lax.axis_size("dp")
    held, ranks, width = adapter_down_weight.shape
    keys = cotangent.shape[1]
    live = segment_live_count
    places = lookup(segment_adapter, adapter_place_table)
    owners = places // held
    segment = jnp.arange(places.shape[0], dtype=jnp.int32)
    same = owners[:, None] == owners[None, :]
    heads = jnp.min(jnp.where(same, segment[None, :], places.shape[0]), axis=1)
    owner_hit = owners[:, None] == jnp.arange(dp_count, dtype=jnp.int32)[None, :]
    wanted = jnp.max(jnp.where(owner_hit, (places % held)[:, None], -1), axis=0)
    index = jnp.max(jnp.where(owner_hit, heads[:, None], 0), axis=0)
    entry = jnp.broadcast_to(wanted.astype(jnp.float32)[:, None], (dp_count, 128))
    far = lambda array: pltpu.with_memory_space_constraint(array, pltpu.HBM)
    maps, pulled, tokens_here, cotangent_here, beside = gather_maps(
        places, live,
        far(adapter_down_weight.reshape(held, 2, HALF, width)),
        far(adapter_up_weight.reshape(held, 2, HALF, keys)),
        far(tokens), far(cotangent),
    )
    part, packed = between(places, live, heads, tokens_here, maps, pulled)
    down_grad, up_grad, beyond = scatter_gradients(
        index, owners, packed, entry, part, cotangent_here, beside
    )
    token_gradient = token_gradients(
        places, live, cotangent_here, beside, beyond, frozen_key_weight, pulled, maps
    )
    return (
        token_gradient,
        down_grad.reshape(held, ranks, width),
        up_grad.reshape(held, ranks, keys),
    )


def solution(mesh):
    placed = (
        P("dp", "tsp"),
        P("dp", "tsp"),
        P("tsp", None),
        P("dp", None, "tsp"),
        P("dp", None, "tsp"),
        P(),
        P("dp"),
        P("dp"),
    )
    return jax.shard_map(
        on_device,
        mesh=mesh,
        in_specs=placed,
        out_specs=(P("dp", "tsp"), P("dp", None, "tsp"), P("dp", None, "tsp")),
        check_vma=False,
    )
```

```python
import jax
import jax.numpy as jnp
from jax import lax
from jax.experimental import pallas as pl
from jax.experimental.pallas import tpu as pltpu
from jax.sharding import PartitionSpec as P

ADAPTER_SCALE = 2.0
MESH = pl.DeviceIdType.MESH
SIDE = 4
RING = 8
HALF = 32
MIB = 1024 * 1024
NEAR = (0, -1, 1, 2)
CHIPS = sorted(
    ((dy, dx) for dy in NEAR for dx in NEAR if dy or dx), key=lambda at: -abs(at[0]) - abs(at[1])
)


def lookup(idents, mapping):
    matches = idents[:, None] == jnp.arange(mapping.shape[0], dtype=jnp.int32)[None, :]
    return jnp.sum(jnp.where(matches, mapping[None, :], 0), axis=1)


def place_in_plane():
    me = lax.axis_index("dp")
    core = lax.rem(me, 2)
    chip = lax.div(me, 2)
    return me, core, lax.div(chip, SIDE), lax.rem(chip, SIDE)


def side(v):
    return lax.rem(v + 2 * SIDE, SIDE)


def ring(v):
    return lax.rem(v + 2 * RING, RING)


def device_of(y, x, core):
    return (side(y) * SIDE + side(x)) * 2 + core


def greet_neighbours():
    me, core, y, x = place_in_plane()
    z = lax.axis_index("tsp")
    devices = [(me + 1 - 2 * core, z)] + [(me, ring(z + k)) for k in range(1, RING)]
    devices += [(device_of(y + dy, x + dx, core), z) for dy, dx in CHIPS]
    barrier = pltpu.get_barrier_semaphore()
    for device in devices:
        pl.semaphore_signal(barrier, inc=1, device_id=device, device_id_type=MESH)
    pl.semaphore_wait(barrier, len(devices))


def remote(src, dst, send, recv, device):
    return pltpu.make_async_remote_copy(src, dst, send, recv, device, MESH)


class PlaneGather:
    copies = 71

    def __init__(self, mine, out, local_sem, send_sem, recv_sem):
        self.me, self.core, self.y, self.x = place_in_plane()
        self.z = lax.axis_index("tsp")
        self.peer = self.me + 1 - 2 * self.core
        self.mine, self.out = mine, out
        self.local_sem, self.send_sem, self.recv_sem = local_sem, send_sem, recv_sem
        self.ids, self.sends = {}, []

    def make(self, src, dst, device, key):
        k = self.ids.setdefault(key, len(self.ids))
        return remote(src, dst, self.send_sem.at[k], self.recv_sem.at[k], (device, self.z))

    def send(self, ref, device, key):
        copy = self.make(ref, ref, device, key)
        copy.start()
        self.sends.append(copy)

    def arrived(self, ref, key):
        self.make(ref, ref, self.peer, key).wait_recv()

    def spot(self, tau, di, dj, core):
        if tau == 0:
            return device_of(self.y + dj, self.x + di, core)
        return device_of(self.y + di, self.x + dj, core)

    def near(self, tau, di, dj):
        return self.spot(tau, di, dj, self.core)

    def block(self, tau, di, dj, half):
        return self.out.at[pl.ds(2 * self.spot(tau, di, dj, tau), 2), half]

    def unit(self, tau, di, dj, e):
        return self.out.at[2 * self.spot(tau, di, dj, tau) + e, self.core]

    def swap(self, tau, di, dj):
        self.send(self.block(tau, di, dj, self.core), self.peer, ("swap", tau, di, dj))

    def own(self):
        here = self.out.at[pl.ds(2 * self.me, 2)]
        self.local = pltpu.make_async_copy(self.mine, here, self.local_sem)
        self.local.start()
        copy = self.make(self.mine, here, self.peer, "own")
        copy.start()
        self.sends.append(copy)

    def own_arrived(self):
        self.local.wait()
        self.make(self.mine, self.out.at[pl.ds(2 * self.peer, 2)], self.peer, "own").wait_recv()

    def one(self):
        for tau in (0, 1):
            for s in (1, -1):
                self.send(self.block(tau, 0, 0, self.core), self.near(tau, s, 0), ("one", tau, s))

    def two(self, *offsets):
        for di in offsets:
            for tau in (0, 1):
                for t in (1, -1):
                    self.send(
                        self.block(tau, di, 0, self.core), self.near(tau, 0, t), ("two", tau, di, t)
                    )

    def one_arrived(self):
        for tau in (0, 1):
            for s in (1, -1):
                self.arrived(self.block(tau, -s, 0, self.core), ("one", tau, s))
                e = 0 if s == 1 else 1
                self.send(self.unit(tau, -s, 0, e), self.near(tau, s, 0), ("onward", tau, s))
        self.two(-1, 1)
        for tau in (0, 1):
            for s in (1, -1):
                self.swap(tau, -s, 0)

    def onward_arrived(self):
        for tau in (0, 1):
            self.arrived(self.unit(tau, 2, 0, 0), ("onward", tau, 1))
            self.arrived(self.unit(tau, 2, 0, 1), ("onward", tau, -1))
        self.two(2)
        for tau in (0, 1):
            self.swap(tau, 2, 0)

    def two_arrived(self, di):
        for tau in (0, 1):
            for t in (1, -1):
                self.arrived(self.block(tau, di, -t, self.core), ("two", tau, di, t))
                e = 0 if t == 1 else 1
                self.send(
                    self.unit(tau, di, -t, e), self.near(tau, 0, t), ("last", tau, di, t)
                )
                self.swap(tau, di, -t)

    def last_arrived(self, di):
        for tau in (0, 1):
            self.arrived(self.unit(tau, di, 2, 0), ("last", tau, di, 1))
            self.arrived(self.unit(tau, di, 2, 1), ("last", tau, di, -1))
            self.swap(tau, di, 2)

    def swaps_arrived(self):
        for tau in (0, 1):
            for di in NEAR:
                for dj in NEAR:
                    if di or dj:
                        self.arrived(self.block(tau, di, dj, 1 - self.core), ("swap", tau, di, dj))

    def sent(self):
        for copy in self.sends:
            copy.wait_send()


class DirectGather:
    copies = 2 * len(CHIPS) + 1

    def __init__(self, mine, out, local_sem, send_sem, recv_sem):
        self.me, self.core, self.y, self.x = place_in_plane()
        self.z = lax.axis_index("tsp")
        self.peer = self.me + 1 - 2 * self.core
        self.mine, self.out = mine, out
        self.local_sem, self.send_sem, self.recv_sem = local_sem, send_sem, recv_sem
        self.sends = []

    def block(self, device):
        return self.out.at[pl.ds(2 * device, 2)]

    def copy(self, src, dst, device, k):
        return remote(src, dst, self.send_sem.at[k], self.recv_sem.at[k], (device, self.z))

    def send(self, src, dst, device, k):
        copy = self.copy(src, dst, device, k)
        copy.start()
        self.sends.append(copy)

    def own(self):
        here = self.block(self.me)
        for k, (dy, dx) in enumerate(CHIPS):
            self.send(self.mine, here, device_of(self.y + dy, self.x + dx, self.core), k)
        self.send(self.mine, here, self.peer, 2 * len(CHIPS))
        self.local = pltpu.make_async_copy(self.mine, here, self.local_sem)
        self.local.start()

    def pass_across(self):
        for k, (dy, dx) in reversed(list(enumerate(CHIPS))):
            block = self.block(device_of(self.y - dy, self.x - dx, self.core))
            self.copy(block, block, self.peer, k).wait_recv()
            self.send(block, block, self.peer, len(CHIPS) + k)

    def arrived(self):
        self.local.wait()
        block = self.block(self.peer)
        self.copy(block, block, self.peer, 2 * len(CHIPS)).wait_recv()
        for k, (dy, dx) in reversed(list(enumerate(CHIPS))):
            block = self.block(device_of(self.y - dy, self.x - dx, 1 - self.core))
            self.copy(block, block, self.peer, len(CHIPS) + k).wait_recv()

    def sent(self):
        for copy in self.sends:
            copy.wait_send()


class RingSum:
    def __init__(self, part, out, held, passed, send_sem, recv_sem, out_send, out_recv):
        self.me, self.i = lax.axis_index("dp"), lax.axis_index("tsp")
        self.part, self.out, self.held, self.passed = part, out, held, passed
        self.send_sem, self.recv_sem = send_sem, recv_sem
        self.out_send, self.out_recv = out_send, out_recv
        self.copies = []

    def copy(self, src, d, step, u):
        return remote(
            src, self.held.at[d, step, u], self.send_sem.at[d, step, u],
            self.recv_sem.at[d, step, u], (self.me, ring(self.i + 1 - 2 * d)),
        )

    def send(self, src, d, step, u):
        copy = self.copy(src, d, step, u)
        copy.start()
        self.copies.append(copy)

    def begin(self):
        for d in (0, 1):
            self.send(self.part.at[ring(self.i + 4), d], d, 0, d)
        for d in (0, 1):
            s = 1 - 2 * d
            self.send(self.part.at[ring(self.i + 3 * s), 1 - d], d, 1, 1 - d)

    def step(self, step):
        for v in (0, 1):
            for d in (0, 1):
                u = v if d == 0 else 1 - v
                if step == 1 and v == 1:
                    continue
                s = 1 - 2 * d
                self.copy(self.held.at[d, step - 1, u], d, step - 1, u).wait_recv()
                self.passed[d, step, u] = (
                    self.held[d, step - 1, u] + self.part[ring(self.i + s * (4 - step)), u]
                )
                self.send(self.passed.at[d, step, u], d, step, u)

    def total(self):
        for u in (0, 1):
            for d in (0, 1):
                self.copy(self.held.at[d, 3, u], d, 3, u).wait_recv()
            self.out[self.i, u] = (
                self.part[self.i, u] + self.held[0, 3, u] + self.held[1, 3, u]
            ).astype(self.out.dtype)
        for k in (4, 3, 5, 2, 6, 1, 7):
            copy = self.across(self.i, k)
            copy.start()
            self.copies.append(copy)

    def across(self, chunk, k):
        ref = self.out.at[ring(chunk)]
        return remote(
            ref, ref, self.out_send.at[k], self.out_recv.at[k], (self.me, ring(self.i + k))
        )

    def end(self):
        for k in range(1, RING):
            self.across(self.i - k, k).wait_recv()

    def sent(self):
        for copy in self.copies:
            copy.wait_send()


def ring_sum_scratch(part):
    dma = pltpu.SemaphoreType.DMA
    shape = (2, 4, 2) + part[2:]
    return [
        pltpu.VMEM(shape, jnp.float32), pltpu.VMEM(shape, jnp.float32),
        dma((2, 4, 2)), dma((2, 4, 2)), dma((RING,)), dma((RING,)),
    ]


class CotangentRing:
    eighths = 8

    def __init__(self, source, target, send_sem, recv_sem, rows, steps):
        self.me, self.z = lax.axis_index("dp"), lax.axis_index("tsp")
        self.source, self.target = source, target
        self.send_sem, self.recv_sem = send_sem, recv_sem
        self.size = rows // self.eighths
        self.copies = []
        self.origin = steps[0]
        self.queue, self.waited = [], set()
        for step in steps:
            for k in range(self.eighths if step < 3 else self.eighths // 2):
                pieces = [(step, 0, k), (step, 1, k if step < 3 else k + self.eighths // 2)]
                self.queue.append(pieces)

    def copy(self, step, d, q):
        here = pl.ds(q * self.size, self.size)
        src, dst = self.source(step, d), self.target(step, d)
        at = (step - self.origin, d, q)
        return remote(
            src.at[here], dst.at[here], self.send_sem.at[at], self.recv_sem.at[at],
            (self.me, ring(self.z + 1 - 2 * d)),
        )

    def wait(self, step, d, q):
        if step >= self.origin and (step, d, q) not in self.waited:
            self.waited.add((step, d, q))
            self.copy(step, d, q).wait_recv()

    def launch(self, count=1):
        for pieces in self.queue[:count]:
            for step, d, q in pieces:
                self.wait(step - 1, d, q)
                copy = self.copy(step, d, q)
                copy.start()
                self.copies.append((copy, (step, d, q)))
        self.queue = self.queue[count:]

    def arrived(self):
        for _, piece in self.copies:
            self.wait(*piece)

    def sent(self):
        for copy, _ in self.copies:
            copy.wait_send()


def gather_kernel(
    places, live, down, up, tokens, cotangent,
    down_maps, pulled, tokens_here, cotangent_here, beside,
    up_maps, part, held, passed, send_sem, recv_sem, out_send, out_recv,
    local_sem, down_send, down_recv, up_send, up_recv, cot_send, cot_recv,
):
    greet_neighbours()
    downs = PlaneGather(down, down_maps, local_sem.at[0], down_send, down_recv)
    ups = DirectGather(up, up_maps, local_sem.at[1], up_send, up_recv)
    sums = RingSum(part, pulled, held, passed, send_sem, recv_sem, out_send, out_recv)
    cots = CotangentRing(
        lambda step, d: cotangent if step == 0 else beside.at[d],
        lambda step, d: beside.at[2 * step + d],
        cot_send, cot_recv, cotangent.shape[0], (0, 1),
    )
    ups.own()
    downs.own()
    cotangent_copy = pltpu.make_async_copy(cotangent, cotangent_here, local_sem.at[2])
    cotangent_copy.start()
    tokens_copy = pltpu.make_async_copy(tokens, tokens_here, local_sem.at[3])
    tokens_copy.start()
    cots.launch(6)
    downs.own_arrived()
    downs.one()
    downs.two(0)
    ups.pass_across()
    ups.arrived()
    cotangent_copy.wait()

    segments = places.shape[0]
    rows = cotangent.shape[0] // segments
    ranks, keys = 2 * HALF, cotangent.shape[1]
    row = lax.broadcasted_iota(jnp.int32, (rows, ranks), 0)
    for j in range(segments // 2):
        pair = []
        for g in (2 * j, 2 * j + 1):
            term = lax.dot_general(
                cotangent_here[g * rows : (g + 1) * rows, :],
                up_maps[places[g]].reshape(ranks, keys),
                (((1,), (1,)), ((), ())),
                preferred_element_type=jnp.float32,
            )
            pair.append(jnp.where(row < live[g], term, 0.0))
        part[j] = jnp.concatenate(pair, axis=1).reshape(part.shape[1:])
    sums.begin()
    cots.launch()
    downs.one_arrived()
    sums.step(1)
    cots.launch()
    downs.two_arrived(0)
    sums.step(2)
    cots.launch()
    downs.onward_arrived()
    sums.step(3)
    cots.launch()
    downs.two_arrived(-1)
    sums.total()
    cots.launch(2)
    downs.two_arrived(1)
    cots.launch(2)
    downs.two_arrived(2)
    downs.last_arrived(0)
    cots.launch(2)
    downs.last_arrived(-1)
    downs.last_arrived(1)
    downs.last_arrived(2)
    sums.end()
    downs.swaps_arrived()
    tokens_copy.wait()
    cots.arrived()
    for each in (ups, downs, sums, cots):
        each.sent()


def gather_maps(places, live, down, up, tokens, cotangent):
    count = 2 * lax.axis_size("dp")
    rows = cotangent.shape[0] // places.shape[0]
    ranks = 2 * HALF
    part = (places.shape[0] // 2, 2, rows // 2, 2 * ranks)
    bf16 = jnp.bfloat16
    dma = pltpu.SemaphoreType.DMA
    scalars = pl.BlockSpec(memory_space=pltpu.SMEM)
    whole = pl.BlockSpec(memory_space=pltpu.VMEM)
    anywhere = pl.BlockSpec(memory_space=pl.ANY)
    far = pl.BlockSpec(memory_space=pltpu.HBM)
    return pl.pallas_call(
        gather_kernel,
        out_shape=(
            jax.ShapeDtypeStruct((count,) + down.shape[1:], bf16),
            jax.ShapeDtypeStruct(part, bf16),
            jax.ShapeDtypeStruct(tokens.shape, bf16),
            jax.ShapeDtypeStruct(cotangent.shape, bf16),
            jax.ShapeDtypeStruct((4,) + cotangent.shape, bf16),
        ),
        in_specs=[scalars, scalars, far, far, far, far],
        out_specs=(anywhere, whole, whole, whole, anywhere),
        scratch_shapes=[pltpu.VMEM((count,) + up.shape[1:], bf16), pltpu.VMEM(part, jnp.float32)]
        + ring_sum_scratch(part)
        + [dma((4,))]
        + [dma((PlaneGather.copies,)) for _ in range(2)]
        + [dma((DirectGather.copies,)) for _ in range(2)]
        + [dma((2, 2, CotangentRing.eighths)), dma((2, 2, CotangentRing.eighths))],
        compiler_params=pltpu.CompilerParams(
            collective_id=0, has_side_effects=True, vmem_limit_bytes=12 * MIB
        ),
        name="gather_maps",
    )(places, live, down, up, tokens, cotangent)


def between_kernel(places, live, heads, tokens, maps, pulled, part, packed, total):
    segments = places.shape[0]
    rows, width = tokens.shape[0] // segments, tokens.shape[1]
    ranks = 2 * HALF
    row = lax.broadcasted_iota(jnp.int32, (rows, ranks), 0)
    for j in range(segments // 2):
        both = pulled[j].reshape(rows, 2 * ranks)
        pair = []
        for k in (0, 1):
            g = 2 * j + k
            here = slice(g * rows, (g + 1) * rows)
            term = lax.dot_general(
                tokens[here, :], maps[places[g]].reshape(ranks, width),
                (((1,), (1,)), ((), ())), preferred_element_type=jnp.float32,
            )
            pair.append(jnp.where(row < live[g], term, 0.0))
            value = lax.dot_general(
                both[:, k * ranks : (k + 1) * ranks], tokens[here, :],
                (((0,), (0,)), ((), ())), preferred_element_type=jnp.float32,
            )
            h = heads[g]
            total[h] = jnp.where(h == g, value, total[h] + value)
        part[j] = jnp.concatenate(pair, axis=1).reshape(part.shape[1:])

    @pl.loop(0, segments)
    def _(g):
        scaled = (total[g] * (ADAPTER_SCALE / rows)).astype(packed.dtype)
        packed[g] = scaled.reshape(packed.shape[1:])


def between(places, live, heads, tokens, maps, pulled):
    segments, width = places.shape[0], tokens.shape[1]
    scalars = pl.BlockSpec(memory_space=pltpu.SMEM)
    whole = pl.BlockSpec(memory_space=pltpu.VMEM)
    return pl.pallas_call(
        between_kernel,
        out_shape=(
            jax.ShapeDtypeStruct(pulled.shape, jnp.float32),
            jax.ShapeDtypeStruct((segments, 2, HALF, width), jnp.bfloat16),
        ),
        in_specs=[scalars] * 3 + [whole] * 3,
        out_specs=(whole, whole),
        scratch_shapes=[pltpu.VMEM((segments, 2 * HALF, width), jnp.float32)],
        compiler_params=pltpu.CompilerParams(vmem_limit_bytes=24 * MIB),
        name="between",
    )(places, live, heads, tokens, maps, pulled)


class PlaneReduce:
    def __init__(self, index, packed, entry, peer_entry, out, bufs, sems):
        self.me, self.core, self.y, self.x = place_in_plane()
        self.z = lax.axis_index("tsp")
        self.peer = self.me + 1 - 2 * self.core
        self.index, self.packed, self.entry, self.peer_entry = index, packed, entry, peer_entry
        self.out = out
        (
            self.slots, self.peer_slots, self.s1, self.r1, self.s2, self.r2,
            self.acc, self.s3, self.r3, self.s4, self.r4, self.res,
        ) = bufs
        self.sems = sems
        self.waits = []

    @staticmethod
    def scratch(unit):
        bf16, f32 = jnp.bfloat16, jnp.float32
        dma = pltpu.SemaphoreType.DMA
        bufs = [
            pltpu.VMEM((SIDE, SIDE, 2) + unit, bf16),
            pltpu.VMEM((SIDE, SIDE, 2) + unit, bf16),
            pltpu.VMEM((2, 2, SIDE) + unit, bf16),
            pltpu.VMEM((2, 2, SIDE) + unit, bf16),
            pltpu.VMEM((2, 2, SIDE, 2) + unit, bf16),
            pltpu.VMEM((2, 2, SIDE, 2) + unit, bf16),
            pltpu.VMEM((2, SIDE, 2) + unit, f32),
            pltpu.VMEM((2, 2) + unit, bf16),
            pltpu.VMEM((2, 2) + unit, bf16),
            pltpu.VMEM((2, 2, 2) + unit, bf16),
            pltpu.VMEM((2, 2, 2) + unit, bf16),
            pltpu.VMEM((2, 2) + unit, f32),
        ]
        sems = []
        for dims in ((2, 4), (2, 2, SIDE), (2, 2, SIDE, 2), (2, 2), (2, 2, 2), (1,)):
            sems += [dma(dims), dma(dims)]
        return bufs, sems

    def copy(self, src, dst, stage, at, device):
        send, recv = self.sems[2 * stage], self.sems[2 * stage + 1]
        return remote(src, dst, send.at[at], recv.at[at], (device, self.z))

    def go(self, copy):
        copy.start()
        self.waits.append(copy)

    def spot(self, tau, di, j):
        if tau == 0:
            return side(self.y + di), j
        return j, side(self.x + di)

    def near(self, tau, axis, d):
        s = 1 - 2 * d
        if (tau == 0) == (axis == 0):
            return device_of(self.y + s, self.x, self.core)
        return device_of(self.y, self.x + s, self.core)

    def from_peer(self, tau, di):
        if tau == 0:
            at = (side(self.y + di), slice(None), 0)
        else:
            at = (slice(None), side(self.x + di), 1)
        return self.copy(
            self.slots.at[at], self.peer_slots.at[at], 0, (tau, di + 1), self.peer
        )

    def share(self):
        for di in (2, 1, -1, 0):
            for tau in (0, 1):

                @pl.loop(0, SIDE)
                def _(j):
                    yy, xx = self.spot(tau, di, j)
                    o = (yy * SIDE + xx) * 2 + tau
                    self.slots[yy, xx, tau] = self.packed[self.index[o], 1 - self.core]

                self.go(self.from_peer(tau, di))

    def term(self, tau, di, j, e):
        yy, xx = self.spot(tau, di, j)
        o = (yy * SIDE + xx) * 2 + tau
        times = self.packed.shape[-1] // self.entry.shape[1]
        mine = jnp.concatenate([self.entry[pl.ds(o, 1), :]] * times, axis=1)
        theirs = jnp.concatenate([self.peer_entry[pl.ds(o, 1), :]] * times, axis=1)
        a = self.packed[self.index[o], self.core].astype(jnp.float32)
        b = self.peer_slots[yy, xx, tau].astype(jnp.float32)
        return jnp.where(mine == e, a, 0.0) + jnp.where(theirs == e, b, 0.0)

    def first(self, tau, d, j):
        at = (tau, d, j)
        return self.copy(self.s1.at[at], self.r1.at[at], 1, at, self.near(tau, 0, d))

    def second(self, tau, d, j, e):
        at = (tau, d, j, e)
        return self.copy(self.s2.at[at], self.r2.at[at], 2, at, self.near(tau, 0, d))

    def third(self, tau, d):
        at = (tau, d)
        return self.copy(self.s3.at[at], self.r3.at[at], 3, at, self.near(tau, 1, d))

    def fourth(self, tau, d, e):
        at = (tau, d, e)
        return self.copy(self.s4.at[at], self.r4.at[at], 4, at, self.near(tau, 1, d))

    def send_first(self):
        for tau in (0, 1):
            self.from_peer(tau, 2).wait_recv()

            @pl.loop(0, SIDE)
            def _(j):
                for d in (0, 1):
                    self.s1[tau, d, j] = self.term(tau, 2, j, d).astype(self.s1.dtype)
                    self.first(tau, d, j).start()

    def send_second_free(self):
        for tau in (0, 1):
            for d in (0, 1):
                self.from_peer(tau, 1 - 2 * d).wait_recv()

            @pl.loop(0, SIDE)
            def _(j):
                for d in (0, 1):
                    value = self.term(tau, 1 - 2 * d, j, 1 - d)
                    self.s2[tau, d, j, 1 - d] = value.astype(self.s2.dtype)
                    self.second(tau, d, j, 1 - d).start()

    def send_second(self, tau):
        @pl.loop(0, SIDE)
        def _(j):
            for d in (0, 1):
                self.first(tau, d, j).wait_recv()
                value = self.term(tau, 1 - 2 * d, j, d) + self.r1[tau, d, j].astype(jnp.float32)
                self.s2[tau, d, j, d] = value.astype(self.s2.dtype)
                self.second(tau, d, j, d).start()

    def keep(self):
        for tau in (0, 1):
            self.from_peer(tau, 0).wait_recv()

            @pl.loop(0, SIDE)
            def _(j):
                for e in (0, 1):
                    self.acc[tau, j, e] = self.term(tau, 0, j, e)

    def total(self, tau, dj, e):
        j = side((self.x if tau == 0 else self.y) + dj)
        for d in (0, 1):
            self.second(tau, d, j, e).wait_recv()
        return (
            self.acc[tau, j, e]
            + self.r2[tau, 0, j, e].astype(jnp.float32)
            + self.r2[tau, 1, j, e].astype(jnp.float32)
        )

    def send_third(self):
        for tau in (0, 1):
            for d in (0, 1):
                self.s3[tau, d] = self.total(tau, 2, d).astype(self.s3.dtype)
                self.go(self.third(tau, d))

    def send_fourth_free(self):
        for tau in (0, 1):
            for d in (0, 1):
                value = self.total(tau, 1 - 2 * d, 1 - d)
                self.s4[tau, d, 1 - d] = value.astype(self.s4.dtype)
                self.go(self.fourth(tau, d, 1 - d))

    def send_fourth(self):
        for tau in (0, 1):
            for d in (0, 1):
                value = self.total(tau, 1 - 2 * d, d)
                self.third(tau, d).wait_recv()
                value += self.r3[tau, d].astype(jnp.float32)
                self.s4[tau, d, d] = value.astype(self.s4.dtype)
                self.go(self.fourth(tau, d, d))

    def finish(self):
        for tau in (0, 1):
            for e in (0, 1):
                value = self.total(tau, 0, e)
                for d in (0, 1):
                    self.fourth(tau, d, e).wait_recv()
                    value += self.r4[tau, d, e].astype(jnp.float32)
                self.res[tau, e] = value
        self.go(self.copy(
            self.res.at[1 - self.core], self.out.at[:, self.core], 5, 0, self.peer
        ))
        self.out[:, self.core] = self.res[self.core]

    def finished(self):
        self.copy(
            self.res.at[1 - self.core], self.out.at[:, 1 - self.core], 5, 0, self.peer
        ).wait_recv()

    def sent(self):
        for copy in self.waits:
            copy.wait_send()
        for tau in (0, 1):
            for d in (0, 1):

                @pl.loop(0, SIDE)
                def _(j):
                    self.first(tau, d, j).wait_send()
                    for e in (0, 1):
                        self.second(tau, d, j, e).wait_send()


class DirectReduce:
    def __init__(self, index, packed, entry, peer_entry, out, bufs, sems):
        self.me, self.core, self.y, self.x = place_in_plane()
        self.z = lax.axis_index("tsp")
        self.peer = self.me + 1 - 2 * self.core
        self.index, self.packed, self.entry, self.peer_entry = index, packed, entry, peer_entry
        self.out = out
        self.slots, self.peer_slots, self.terms, self.landed, self.res = bufs
        self.send_sem, self.recv_sem = sems
        self.waits = []

    @staticmethod
    def scratch(unit):
        bf16 = jnp.bfloat16
        dma = pltpu.SemaphoreType.DMA
        chips = SIDE * SIDE
        bufs = [
            pltpu.VMEM((chips, 2) + unit, bf16),
            pltpu.VMEM((chips, 2) + unit, bf16),
            pltpu.VMEM((chips, 2, 2) + unit, bf16),
            pltpu.VMEM((len(CHIPS), 2, 2) + unit, bf16),
            pltpu.VMEM((2, 2) + unit, jnp.float32),
        ]
        return bufs, [dma((len(CHIPS) + 2,)), dma((len(CHIPS) + 2,))]

    def copy(self, src, dst, device, k):
        return remote(src, dst, self.send_sem.at[k], self.recv_sem.at[k], (device, self.z))

    def go(self, copy):
        copy.start()
        self.waits.append(copy)

    def share(self):
        @pl.loop(0, SIDE * SIDE)
        def _(q):
            for tau in (0, 1):
                self.slots[q, tau] = self.packed[self.index[2 * q + tau], 1 - self.core]

        self.go(self.copy(self.slots, self.peer_slots, self.peer, len(CHIPS)))

    def term(self, q, tau, e):
        o = 2 * q + tau
        a = self.packed[self.index[o], self.core].astype(jnp.float32)
        b = self.peer_slots[q, tau].astype(jnp.float32)
        return jnp.where(self.entry[pl.ds(o, 1), :] == e, a, 0.0) + jnp.where(
            self.peer_entry[pl.ds(o, 1), :] == e, b, 0.0
        )

    def send_all(self):
        self.copy(self.slots, self.peer_slots, self.peer, len(CHIPS)).wait_recv()

        @pl.loop(0, SIDE * SIDE)
        def _(q):
            for tau in (0, 1):
                for e in (0, 1):
                    self.terms[q, tau, e] = self.term(q, tau, e).astype(self.terms.dtype)

        for k, (dy, dx) in enumerate(CHIPS):
            device = device_of(self.y + dy, self.x + dx, self.core)
            self.go(self.copy(
                self.terms.at[lax.div(device, 2)], self.landed.at[k], device, k
            ))

    def finish(self):
        for k in range(len(CHIPS)):
            self.copy(self.landed.at[k], self.landed.at[k], self.peer, k).wait_recv()
        for tau in (0, 1):
            for e in (0, 1):
                value = self.term(lax.div(self.me, 2), tau, e)
                for k in range(len(CHIPS)):
                    value += self.landed[k, tau, e].astype(jnp.float32)
                self.res[tau, e] = value
        self.go(self.copy(
            self.res.at[1 - self.core], self.out.at[:, self.core], self.peer, len(CHIPS) + 1
        ))
        self.out[:, self.core] = self.res[self.core]

    def finished(self):
        self.copy(
            self.res.at[1 - self.core], self.out.at[:, 1 - self.core], self.peer, len(CHIPS) + 1
        ).wait_recv()

    def sent(self):
        for copy in self.waits:
            copy.wait_send()


REDUCE_BUFS, REDUCE_SEMS, SUM_REFS = 12, 12, 6


def scatter_kernel(
    index, owners, places, live, packed, entry, part, cotangent, beside, frozen, pulled, maps,
    out_down, out_up, out_tokens, *rest
):
    rest = list(rest)

    def take(n):
        taken = rest[:n]
        del rest[:n]
        return taken

    peer_entry, lowered, packed_up, beyond, weights = take(5)
    sum_refs = take(SUM_REFS)
    down_bufs, down_sems = take(REDUCE_BUFS), take(REDUCE_SEMS)
    up_bufs, up_sems = take(5), take(2)
    entry_send, entry_recv, cot_send, cot_recv = rest
    greet_neighbours()
    downs = PlaneReduce(index, packed, entry, peer_entry, out_down, down_bufs, down_sems)
    ups = DirectReduce(index, packed_up, entry, peer_entry, out_up, up_bufs, up_sems)
    sums = RingSum(part, lowered, *sum_refs)
    rows = cotangent.shape[0]
    cots = CotangentRing(
        lambda step, d: beside.at[2 + d] if step == 2 else beyond.at[d],
        lambda step, d: beyond.at[d if step == 2 else 2],
        cot_send, cot_recv, rows, (2, 3),
    )
    sums.begin()
    entries = remote(entry, peer_entry, entry_send, entry_recv, (downs.peer, downs.z))
    entries.start()
    cots.launch()
    downs.share()
    sums.step(1)
    cots.launch()
    entries.wait_recv()
    downs.send_first()
    sums.step(2)
    cots.launch()
    downs.send_second_free()
    sums.step(3)
    cots.launch()
    sums.total()
    cots.launch(2)
    downs.send_second(0)
    cots.launch(2)
    downs.send_second(1)
    z, keys = lax.axis_index("tsp"), cotangent.shape[1]
    for k, r in enumerate((0, -1, 1, -2, 2, -3, 3, 4)):
        first = pl.multiple_of(ring(z + r) * keys, keys)
        weights[:, k * keys : (k + 1) * keys] = frozen[:, pl.ds(first, keys)]
    downs.keep()
    sums.end()

    segments = owners.shape[0]
    seg_rows, keys = rows // segments, cotangent.shape[1]
    ranks = 2 * HALF
    values = []
    for g in range(segments):
        both = lowered[g // 2].reshape(seg_rows, 2 * ranks)
        values.append(lax.dot_general(
            both[:, (g % 2) * ranks : (g % 2 + 1) * ranks],
            cotangent[g * seg_rows : (g + 1) * seg_rows, :],
            (((0,), (0,)), ((), ())),
            preferred_element_type=jnp.float32,
        ))
    for g in range(segments):
        value = values[g]
        for h in range(segments):
            if h != g:
                value = value + jnp.where(owners[h] == owners[g], values[h], 0.0)
        scaled = (value * (ADAPTER_SCALE / seg_rows)).astype(packed_up.dtype)
        packed_up[g] = scaled.reshape(packed_up.shape[1:])

    ups.share()
    downs.send_third()
    ups.send_all()
    cots.launch(4)
    downs.send_fourth_free()
    downs.send_fourth()
    cots.arrived()

    block, width = 2 * seg_rows, out_tokens.shape[1]
    row = lax.broadcasted_iota(jnp.int32, (seg_rows, width), 0)
    parts = [(beside, k) for k in range(4)] + [(beyond, k) for k in range(3)]

    def token_block(b):
        here = pl.ds(pl.multiple_of(b * block, block), block)
        left = jnp.concatenate(
            [cotangent[here, :]] + [ref[k, here, :] for ref, k in parts], axis=1
        )
        value = lax.dot_general(
            left, weights[...], (((1,), (1,)), ((), ())), preferred_element_type=jnp.float32
        )
        both = pulled[b].reshape(seg_rows, 2 * ranks)
        for k in (0, 1):
            g = 2 * b + k
            extra = jnp.dot(
                both[:, k * ranks : (k + 1) * ranks], maps[places[g]].reshape(ranks, width),
                preferred_element_type=jnp.float32,
            )
            total = value[k * seg_rows : (k + 1) * seg_rows] + ADAPTER_SCALE * extra
            rows_here = pl.ds(pl.multiple_of(g * seg_rows, seg_rows), seg_rows)
            out_tokens[rows_here, :] = jnp.where(row < live[g], total, 0.0).astype(
                out_tokens.dtype
            )

    pl.loop(0, 5)(token_block)
    downs.finish()
    ups.finish()
    pl.loop(5, segments // 2)(token_block)
    downs.finished()
    ups.finished()
    entries.wait_send()
    for each in (downs, ups, sums, cots):
        each.sent()


def scatter_gradients(
    index, owners, places, live, packed, entry, part, cotangent, beside, frozen, pulled, maps
):
    down_unit = packed.shape[2:]
    up_unit = (HALF, cotangent.shape[1])
    bf16, f32 = jnp.bfloat16, jnp.float32
    dma = pltpu.SemaphoreType.DMA
    scalars = pl.BlockSpec(memory_space=pltpu.SMEM)
    whole = pl.BlockSpec(memory_space=pltpu.VMEM)
    anywhere = pl.BlockSpec(memory_space=pl.ANY)
    down_bufs, down_sems = PlaneReduce.scratch(down_unit)
    up_bufs, up_sems = DirectReduce.scratch(up_unit)
    return pl.pallas_call(
        scatter_kernel,
        out_shape=(
            jax.ShapeDtypeStruct((2, 2) + down_unit, f32),
            jax.ShapeDtypeStruct((2, 2) + up_unit, f32),
            jax.ShapeDtypeStruct((cotangent.shape[0], frozen.shape[0]), bf16),
        ),
        in_specs=[scalars] * 4 + [whole] * 8,
        out_specs=(whole, whole, whole),
        scratch_shapes=[
            pltpu.VMEM(entry.shape, f32),
            pltpu.VMEM(part.shape, bf16),
            pltpu.VMEM((packed.shape[0], 2) + up_unit, bf16),
            pltpu.VMEM((3,) + beside.shape[1:], bf16),
            pltpu.VMEM(frozen.shape, bf16),
        ]
        + ring_sum_scratch(part.shape)
        + down_bufs + down_sems + up_bufs + up_sems
        + [dma(()), dma(()), dma((2, 2, CotangentRing.eighths)), dma((2, 2, CotangentRing.eighths))],
        compiler_params=pltpu.CompilerParams(
            collective_id=1, has_side_effects=True, vmem_limit_bytes=30 * MIB
        ),
        name="scatter_gradients",
    )(index, owners, places, live, packed, entry, part, cotangent, beside, frozen, pulled, maps)


def store_kernel(a, b, c, out_a, out_b, out_c, sems):
    pieces = 8
    copies = [
        pltpu.make_async_copy(b, out_b, sems.at[pieces]),
        pltpu.make_async_copy(c, out_c, sems.at[pieces + 1]),
    ]
    rows = a.shape[0] // pieces
    for k in range(pieces):
        here = pl.ds(k * rows, rows)
        copies.append(pltpu.make_async_copy(a.at[here], out_a.at[here], sems.at[k]))
    for copy in copies:
        copy.start()
    for copy in copies:
        copy.wait()


def store(*arrays):
    return pl.pallas_call(
        store_kernel,
        out_shape=tuple(jax.ShapeDtypeStruct(array.shape, array.dtype) for array in arrays),
        in_specs=[pl.BlockSpec(memory_space=pltpu.VMEM)] * 3,
        out_specs=(pl.BlockSpec(memory_space=pltpu.HBM),) * 3,
        scratch_shapes=[pltpu.SemaphoreType.DMA((10,))],
        compiler_params=pltpu.CompilerParams(vmem_limit_bytes=8 * MIB),
        name="store",
    )(*arrays)


def on_device(
    tokens,
    cotangent,
    frozen_key_weight,
    adapter_down_weight,
    adapter_up_weight,
    adapter_place_table,
    segment_adapter,
    segment_live_count,
):
    dp_count = lax.axis_size("dp")
    held, ranks, width = adapter_down_weight.shape
    keys = cotangent.shape[1]
    live = segment_live_count
    places = lookup(segment_adapter, adapter_place_table)
    owners = places // held
    segment = jnp.arange(places.shape[0], dtype=jnp.int32)
    same = owners[:, None] == owners[None, :]
    heads = jnp.min(jnp.where(same, segment[None, :], places.shape[0]), axis=1)
    owner_hit = owners[:, None] == jnp.arange(dp_count, dtype=jnp.int32)[None, :]
    wanted = jnp.max(jnp.where(owner_hit, (places % held)[:, None], -1), axis=0)
    index = jnp.max(jnp.where(owner_hit, heads[:, None], 0), axis=0)
    entry = jnp.broadcast_to(wanted.astype(jnp.float32)[:, None], (dp_count, 128))
    far = lambda array: pltpu.with_memory_space_constraint(array, pltpu.HBM)
    maps, pulled, tokens_here, cotangent_here, beside = gather_maps(
        places, live,
        far(adapter_down_weight.reshape(held, 2, HALF, width)),
        far(adapter_up_weight.reshape(held, 2, HALF, keys)),
        far(tokens), far(cotangent),
    )
    part, packed = between(places, live, heads, tokens_here, maps, pulled)
    down_grad, up_grad, token_gradient = scatter_gradients(
        index, owners, places, live, packed, entry, part, cotangent_here, beside,
        frozen_key_weight, pulled, maps,
    )
    token_gradient, down_grad, up_grad = store(
        token_gradient,
        down_grad.reshape(held, ranks, width),
        up_grad.reshape(held, ranks, keys),
    )
    return token_gradient, down_grad, up_grad


def solution(mesh):
    placed = (
        P("dp", "tsp"),
        P("dp", "tsp"),
        P("tsp", None),
        P("dp", None, "tsp"),
        P("dp", None, "tsp"),
        P(),
        P("dp"),
        P("dp"),
    )
    return jax.shard_map(
        on_device,
        mesh=mesh,
        in_specs=placed,
        out_specs=(P("dp", "tsp"), P("dp", None, "tsp"), P("dp", None, "tsp")),
        check_vma=False,
    )
```

```python
import jax
import jax.numpy as jnp
from jax import lax
from jax.experimental import pallas as pl
from jax.experimental.pallas import tpu as pltpu
from jax.sharding import PartitionSpec as P

ADAPTER_SCALE = 2.0
MESH = pl.DeviceIdType.MESH
SIDE = 4
RING = 8
HALF = 32
MIB = 1024 * 1024
NEAR = (0, -1, 1, 2)
CHIPS = sorted(
    ((dy, dx) for dy in NEAR for dx in NEAR if dy or dx), key=lambda at: -abs(at[0]) - abs(at[1])
)


def place_in_plane():
    me = lax.axis_index("dp")
    core = lax.rem(me, 2)
    chip = lax.div(me, 2)
    return me, core, lax.div(chip, SIDE), lax.rem(chip, SIDE)


def side(v):
    return lax.rem(v + 2 * SIDE, SIDE)


def ring(v):
    return lax.rem(v + 2 * RING, RING)


def device_of(y, x, core):
    return (side(y) * SIDE + side(x)) * 2 + core


def greet_neighbours():
    me, core, y, x = place_in_plane()
    z = lax.axis_index("tsp")
    devices = [(me + 1 - 2 * core, z)] + [(me, ring(z + k)) for k in range(1, RING)]
    devices += [(device_of(y + dy, x + dx, core), z) for dy, dx in CHIPS]
    barrier = pltpu.get_barrier_semaphore()
    for device in devices:
        pl.semaphore_signal(barrier, inc=1, device_id=device, device_id_type=MESH)
    pl.semaphore_wait(barrier, len(devices))


def remote(src, dst, send, recv, device):
    return pltpu.make_async_remote_copy(src, dst, send, recv, device, MESH)


class PlaneGather:
    copies = 71

    def __init__(self, mine, out, local_sem, send_sem, recv_sem):
        self.me, self.core, self.y, self.x = place_in_plane()
        self.z = lax.axis_index("tsp")
        self.peer = self.me + 1 - 2 * self.core
        self.mine, self.out = mine, out
        self.local_sem, self.send_sem, self.recv_sem = local_sem, send_sem, recv_sem
        self.ids, self.sends = {}, []

    def make(self, src, dst, device, key):
        k = self.ids.setdefault(key, len(self.ids))
        return remote(src, dst, self.send_sem.at[k], self.recv_sem.at[k], (device, self.z))

    def send(self, ref, device, key):
        copy = self.make(ref, ref, device, key)
        copy.start()
        self.sends.append(copy)

    def arrived(self, ref, key):
        self.make(ref, ref, self.peer, key).wait_recv()

    def spot(self, tau, di, dj, core):
        if tau == 0:
            return device_of(self.y + dj, self.x + di, core)
        return device_of(self.y + di, self.x + dj, core)

    def near(self, tau, di, dj):
        return self.spot(tau, di, dj, self.core)

    def block(self, tau, di, dj, half):
        return self.out.at[pl.ds(2 * self.spot(tau, di, dj, tau), 2), half]

    def unit(self, tau, di, dj, e):
        return self.out.at[2 * self.spot(tau, di, dj, tau) + e, self.core]

    def swap(self, tau, di, dj):
        self.send(self.block(tau, di, dj, self.core), self.peer, ("swap", tau, di, dj))

    def own(self):
        here = self.out.at[pl.ds(2 * self.me, 2)]
        self.local = pltpu.make_async_copy(self.mine, here, self.local_sem)
        self.local.start()
        copy = self.make(self.mine, here, self.peer, "own")
        copy.start()
        self.sends.append(copy)

    def own_arrived(self):
        self.local.wait()
        self.make(self.mine, self.out.at[pl.ds(2 * self.peer, 2)], self.peer, "own").wait_recv()

    def one(self):
        for tau in (0, 1):
            for s in (1, -1):
                self.send(self.block(tau, 0, 0, self.core), self.near(tau, s, 0), ("one", tau, s))

    def two(self, *offsets):
        for di in offsets:
            for tau in (0, 1):
                for t in (1, -1):
                    self.send(
                        self.block(tau, di, 0, self.core), self.near(tau, 0, t), ("two", tau, di, t)
                    )

    def one_arrived(self):
        for tau in (0, 1):
            for s in (1, -1):
                self.arrived(self.block(tau, -s, 0, self.core), ("one", tau, s))
                e = 0 if s == 1 else 1
                self.send(self.unit(tau, -s, 0, e), self.near(tau, s, 0), ("onward", tau, s))
        self.two(-1, 1)
        for tau in (0, 1):
            for s in (1, -1):
                self.swap(tau, -s, 0)

    def onward_arrived(self):
        for tau in (0, 1):
            self.arrived(self.unit(tau, 2, 0, 0), ("onward", tau, 1))
            self.arrived(self.unit(tau, 2, 0, 1), ("onward", tau, -1))
        self.two(2)
        for tau in (0, 1):
            self.swap(tau, 2, 0)

    def two_arrived(self, di):
        for tau in (0, 1):
            for t in (1, -1):
                self.arrived(self.block(tau, di, -t, self.core), ("two", tau, di, t))
                e = 0 if t == 1 else 1
                self.send(
                    self.unit(tau, di, -t, e), self.near(tau, 0, t), ("last", tau, di, t)
                )
                self.swap(tau, di, -t)

    def last_arrived(self, di):
        for tau in (0, 1):
            self.arrived(self.unit(tau, di, 2, 0), ("last", tau, di, 1))
            self.arrived(self.unit(tau, di, 2, 1), ("last", tau, di, -1))
            self.swap(tau, di, 2)

    def swaps_arrived(self):
        for tau in (0, 1):
            for di in NEAR:
                for dj in NEAR:
                    if di or dj:
                        self.arrived(self.block(tau, di, dj, 1 - self.core), ("swap", tau, di, dj))

    def sent(self):
        for copy in self.sends:
            copy.wait_send()


class DirectGather:
    copies = 2 * len(CHIPS) + 1

    def __init__(self, mine, out, local_sem, send_sem, recv_sem):
        self.me, self.core, self.y, self.x = place_in_plane()
        self.z = lax.axis_index("tsp")
        self.peer = self.me + 1 - 2 * self.core
        self.mine, self.out = mine, out
        self.local_sem, self.send_sem, self.recv_sem = local_sem, send_sem, recv_sem
        self.sends = []

    def block(self, device):
        return self.out.at[pl.ds(2 * device, 2)]

    def copy(self, src, dst, device, k):
        return remote(src, dst, self.send_sem.at[k], self.recv_sem.at[k], (device, self.z))

    def send(self, src, dst, device, k):
        copy = self.copy(src, dst, device, k)
        copy.start()
        self.sends.append(copy)

    def own(self):
        here = self.block(self.me)
        for k, (dy, dx) in enumerate(CHIPS):
            self.send(self.mine, here, device_of(self.y + dy, self.x + dx, self.core), k)
        self.send(self.mine, here, self.peer, 2 * len(CHIPS))
        self.local = pltpu.make_async_copy(self.mine, here, self.local_sem)
        self.local.start()

    def pass_across(self):
        for k, (dy, dx) in reversed(list(enumerate(CHIPS))):
            block = self.block(device_of(self.y - dy, self.x - dx, self.core))
            self.copy(block, block, self.peer, k).wait_recv()
            self.send(block, block, self.peer, len(CHIPS) + k)

    def arrived(self):
        self.local.wait()
        block = self.block(self.peer)
        self.copy(block, block, self.peer, 2 * len(CHIPS)).wait_recv()
        for k, (dy, dx) in reversed(list(enumerate(CHIPS))):
            block = self.block(device_of(self.y - dy, self.x - dx, 1 - self.core))
            self.copy(block, block, self.peer, len(CHIPS) + k).wait_recv()

    def sent(self):
        for copy in self.sends:
            copy.wait_send()


class RingSum:
    def __init__(self, part, out, held, passed, send_sem, recv_sem, out_send, out_recv):
        self.me, self.i = lax.axis_index("dp"), lax.axis_index("tsp")
        self.part, self.out, self.held, self.passed = part, out, held, passed
        self.send_sem, self.recv_sem = send_sem, recv_sem
        self.out_send, self.out_recv = out_send, out_recv
        self.copies = []

    def copy(self, src, d, step, u):
        return remote(
            src, self.held.at[d, step, u], self.send_sem.at[d, step, u],
            self.recv_sem.at[d, step, u], (self.me, ring(self.i + 1 - 2 * d)),
        )

    def send(self, src, d, step, u):
        copy = self.copy(src, d, step, u)
        copy.start()
        self.copies.append(copy)

    def halves(self, d):
        return ((0, 1), (2, 3)) if d == 0 else ((2, 3), (0, 1))

    def begin(self):
        for k in (0, 1):
            for d in (0, 1):
                u = self.halves(d)[0][k]
                self.send(self.part.at[ring(self.i + 4), u], d, 0, u)
        for k in (0, 1):
            for d in (0, 1):
                u = self.halves(d)[1][k]
                self.send(self.part.at[ring(self.i + 3 * (1 - 2 * d)), u], d, 1, u)

    def step(self, step):
        for k in range(4):
            for d in (0, 1):
                own, other = self.halves(d)
                if step == 1 and k >= 2:
                    continue
                u = own[k] if step == 1 else (other + own)[k]
                s = 1 - 2 * d
                self.copy(self.held.at[d, step - 1, u], d, step - 1, u).wait_recv()
                self.passed[d, step, u] = (
                    self.held[d, step - 1, u] + self.part[ring(self.i + s * (4 - step)), u]
                )
                self.send(self.passed.at[d, step, u], d, step, u)

    def total(self):
        for u in range(4):
            for d in (0, 1):
                self.copy(self.held.at[d, 3, u], d, 3, u).wait_recv()
            self.out[self.i, u] = (
                self.part[self.i, u] + self.held[0, 3, u] + self.held[1, 3, u]
            ).astype(self.out.dtype)
        for k in (4, 3, 5, 2, 6, 1, 7):
            copy = self.across(self.i, k)
            copy.start()
            self.copies.append(copy)

    def across(self, chunk, k):
        ref = self.out.at[ring(chunk)]
        return remote(
            ref, ref, self.out_send.at[k], self.out_recv.at[k], (self.me, ring(self.i + k))
        )

    def end(self):
        for k in range(1, RING):
            self.across(self.i - k, k).wait_recv()

    def sent(self):
        for copy in self.copies:
            copy.wait_send()


def ring_sum_scratch(part):
    dma = pltpu.SemaphoreType.DMA
    shape = (2, 4, 4) + part[2:]
    return [
        pltpu.VMEM(shape, jnp.float32), pltpu.VMEM(shape, jnp.float32),
        dma((2, 4, 4)), dma((2, 4, 4)), dma((RING,)), dma((RING,)),
    ]


class CotangentRing:
    eighths = 8

    def __init__(self, source, target, send_sem, recv_sem, rows, steps):
        self.me, self.z = lax.axis_index("dp"), lax.axis_index("tsp")
        self.source, self.target = source, target
        self.send_sem, self.recv_sem = send_sem, recv_sem
        self.size = rows // self.eighths
        self.copies = []
        self.origin = steps[0]
        self.queue, self.waited = [], set()
        for step in steps:
            for k in range(self.eighths if step < 3 else self.eighths // 2):
                pieces = [(step, 0, k), (step, 1, k if step < 3 else k + self.eighths // 2)]
                self.queue.append(pieces)

    def copy(self, step, d, q):
        here = pl.ds(q * self.size, self.size)
        src, dst = self.source(step, d), self.target(step, d)
        at = (step - self.origin, d, q)
        return remote(
            src.at[here], dst.at[here], self.send_sem.at[at], self.recv_sem.at[at],
            (self.me, ring(self.z + 1 - 2 * d)),
        )

    def wait(self, step, d, q):
        if step >= self.origin and (step, d, q) not in self.waited:
            self.waited.add((step, d, q))
            self.copy(step, d, q).wait_recv()

    def launch(self, count=1):
        for pieces in self.queue[:count]:
            for step, d, q in pieces:
                self.wait(step - 1, d, q)
                copy = self.copy(step, d, q)
                copy.start()
                self.copies.append((copy, (step, d, q)))
        self.queue = self.queue[count:]

    def arrived(self):
        for _, piece in self.copies:
            self.wait(*piece)

    def sent(self):
        for copy, _ in self.copies:
            copy.wait_send()


def gather_kernel(
    table, idents, live, down, up, tokens, cotangent,
    down_maps, pulled, tokens_here, cotangent_here, beside,
    up_maps, part, held, passed, send_sem, recv_sem, out_send, out_recv,
    local_sem, down_send, down_recv, up_send, up_recv, cot_send, cot_recv,
):
    greet_neighbours()
    downs = PlaneGather(down, down_maps, local_sem.at[0], down_send, down_recv)
    ups = DirectGather(up, up_maps, local_sem.at[1], up_send, up_recv)
    sums = RingSum(part, pulled, held, passed, send_sem, recv_sem, out_send, out_recv)
    cots = CotangentRing(
        lambda step, d: cotangent if step == 0 else beside.at[d],
        lambda step, d: beside.at[2 * step + d],
        cot_send, cot_recv, cotangent.shape[0], (0, 1),
    )
    ups.own()
    downs.own()
    cotangent_copy = pltpu.make_async_copy(cotangent, cotangent_here, local_sem.at[2])
    cotangent_copy.start()
    tokens_copy = pltpu.make_async_copy(tokens, tokens_here, local_sem.at[3])
    tokens_copy.start()
    cots.launch(6)
    downs.own_arrived()
    downs.one()
    downs.two(0)
    ups.pass_across()
    ups.arrived()
    cotangent_copy.wait()

    segments = idents.shape[0]
    rows = cotangent.shape[0] // segments
    ranks, keys = 2 * HALF, cotangent.shape[1]
    row = lax.broadcasted_iota(jnp.int32, (rows, ranks), 0)
    for j in range(segments // 2):
        pair = []
        for g in (2 * j, 2 * j + 1):
            term = lax.dot_general(
                cotangent_here[g * rows : (g + 1) * rows, :],
                up_maps[table[idents[g]]].reshape(ranks, keys),
                (((1,), (1,)), ((), ())),
                preferred_element_type=jnp.float32,
            )
            pair.append(jnp.where(row < live[g], term, 0.0))
        part[j] = jnp.concatenate(pair, axis=1).reshape(part.shape[1:])
    sums.begin()
    cots.launch()
    downs.one_arrived()
    sums.step(1)
    cots.launch()
    downs.two_arrived(0)
    sums.step(2)
    cots.launch()
    downs.onward_arrived()
    sums.step(3)
    cots.launch()
    downs.two_arrived(-1)
    sums.total()
    cots.launch(2)
    downs.two_arrived(1)
    cots.launch(2)
    downs.two_arrived(2)
    downs.last_arrived(0)
    cots.launch(2)
    downs.last_arrived(-1)
    downs.last_arrived(1)
    downs.last_arrived(2)
    sums.end()
    downs.swaps_arrived()
    tokens_copy.wait()
    cots.arrived()
    for each in (ups, downs, sums, cots):
        each.sent()


def gather_maps(table, idents, live, down, up, tokens, cotangent):
    count = 2 * lax.axis_size("dp")
    rows = cotangent.shape[0] // idents.shape[0]
    ranks = 2 * HALF
    part = (idents.shape[0] // 2, 4, rows // 4, 2 * ranks)
    bf16 = jnp.bfloat16
    dma = pltpu.SemaphoreType.DMA
    scalars = pl.BlockSpec(memory_space=pltpu.SMEM)
    whole = pl.BlockSpec(memory_space=pltpu.VMEM)
    anywhere = pl.BlockSpec(memory_space=pl.ANY)
    far = pl.BlockSpec(memory_space=pltpu.HBM)
    return pl.pallas_call(
        gather_kernel,
        out_shape=(
            jax.ShapeDtypeStruct((count,) + down.shape[1:], bf16),
            jax.ShapeDtypeStruct(part, bf16),
            jax.ShapeDtypeStruct(tokens.shape, bf16),
            jax.ShapeDtypeStruct(cotangent.shape, bf16),
            jax.ShapeDtypeStruct((4,) + cotangent.shape, bf16),
        ),
        in_specs=[scalars, scalars, scalars, far, far, far, far],
        out_specs=(anywhere, whole, whole, whole, anywhere),
        scratch_shapes=[pltpu.VMEM((count,) + up.shape[1:], bf16), pltpu.VMEM(part, jnp.float32)]
        + ring_sum_scratch(part)
        + [dma((4,))]
        + [dma((PlaneGather.copies,)) for _ in range(2)]
        + [dma((DirectGather.copies,)) for _ in range(2)]
        + [dma((2, 2, CotangentRing.eighths)), dma((2, 2, CotangentRing.eighths))],
        compiler_params=pltpu.CompilerParams(
            collective_id=0, has_side_effects=True, vmem_limit_bytes=12 * MIB
        ),
        name="gather_maps",
    )(table, idents, live, down, up, tokens, cotangent)


def between_kernel(
    table, idents, live, tokens, maps, pulled, part, packed, places, before, index, entry, total
):
    segments = idents.shape[0]
    rows, width = tokens.shape[0] // segments, tokens.shape[1]
    ranks = 2 * HALF
    @pl.loop(0, index.shape[0])
    def _(o):
        index[o] = -1

    entry[...] = jnp.full_like(entry, -1.0)

    @pl.loop(0, segments)
    def _(g):
        place = table[idents[g]]
        owner = lax.div(place, 2)
        places[g] = place
        before[g] = index[owner]
        index[owner] = g
        held = lax.rem(place, 2).astype(jnp.float32)
        entry[pl.ds(owner, 1), :] = jnp.full((1, entry.shape[1]), held, jnp.float32)

    @pl.loop(0, index.shape[0])
    def _(o):
        index[o] = jnp.maximum(index[o], 0)

    row = lax.broadcasted_iota(jnp.int32, (rows, ranks), 0)
    for j in range(segments // 2):
        both = pulled[j].reshape(rows, 2 * ranks)
        pair = []
        for k in (0, 1):
            g = 2 * j + k
            here = slice(g * rows, (g + 1) * rows)
            term = lax.dot_general(
                tokens[here, :], maps[places[g]].reshape(ranks, width),
                (((1,), (1,)), ((), ())), preferred_element_type=jnp.float32,
            )
            pair.append(jnp.where(row < live[g], term, 0.0))
            value = lax.dot_general(
                both[:, k * ranks : (k + 1) * ranks], tokens[here, :],
                (((0,), (0,)), ((), ())), preferred_element_type=jnp.float32,
            )
            if g:
                earlier = total[jnp.maximum(before[g], 0)]
                value = value + jnp.where(before[g] >= 0, earlier, 0.0)
            total[g] = value
        part[j] = jnp.concatenate(pair, axis=1).reshape(part.shape[1:])

    @pl.loop(0, segments)
    def _(g):
        scaled = (total[g] * (ADAPTER_SCALE / rows)).astype(packed.dtype)
        packed[g] = scaled.reshape(packed.shape[1:])


def between(table, idents, live, tokens, maps, pulled):
    segments, width = idents.shape[0], tokens.shape[1]
    owners = lax.axis_size("dp")
    scalars = pl.BlockSpec(memory_space=pltpu.SMEM)
    whole = pl.BlockSpec(memory_space=pltpu.VMEM)
    return pl.pallas_call(
        between_kernel,
        out_shape=(
            jax.ShapeDtypeStruct(pulled.shape, jnp.float32),
            jax.ShapeDtypeStruct((segments, 2, HALF, width), jnp.bfloat16),
            jax.ShapeDtypeStruct((segments,), jnp.int32),
            jax.ShapeDtypeStruct((segments,), jnp.int32),
            jax.ShapeDtypeStruct((owners,), jnp.int32),
            jax.ShapeDtypeStruct((owners, 128), jnp.float32),
        ),
        in_specs=[scalars] * 3 + [whole] * 3,
        out_specs=(whole, whole, scalars, scalars, scalars, whole),
        scratch_shapes=[pltpu.VMEM((segments, 2 * HALF, width), jnp.float32)],
        compiler_params=pltpu.CompilerParams(vmem_limit_bytes=24 * MIB),
        name="between",
    )(table, idents, live, tokens, maps, pulled)


class PlaneReduce:
    def __init__(self, index, packed, entry, peer_entry, out, bufs, sems):
        self.me, self.core, self.y, self.x = place_in_plane()
        self.z = lax.axis_index("tsp")
        self.peer = self.me + 1 - 2 * self.core
        self.index, self.packed, self.entry, self.peer_entry = index, packed, entry, peer_entry
        self.out = out
        (
            self.slots, self.peer_slots, self.s1, self.r1, self.s2, self.r2,
            self.acc, self.s3, self.r3, self.s4, self.r4, self.res,
        ) = bufs
        self.sems = sems
        self.waits = []

    @staticmethod
    def scratch(unit):
        bf16, f32 = jnp.bfloat16, jnp.float32
        dma = pltpu.SemaphoreType.DMA
        bufs = [
            pltpu.VMEM((SIDE, SIDE, 2) + unit, bf16),
            pltpu.VMEM((SIDE, SIDE, 2) + unit, bf16),
            pltpu.VMEM((2, 2, SIDE) + unit, bf16),
            pltpu.VMEM((2, 2, SIDE) + unit, bf16),
            pltpu.VMEM((2, 2, SIDE, 2) + unit, bf16),
            pltpu.VMEM((2, 2, SIDE, 2) + unit, bf16),
            pltpu.VMEM((2, SIDE, 2) + unit, f32),
            pltpu.VMEM((2, 2) + unit, bf16),
            pltpu.VMEM((2, 2) + unit, bf16),
            pltpu.VMEM((2, 2, 2) + unit, bf16),
            pltpu.VMEM((2, 2, 2) + unit, bf16),
            pltpu.VMEM((2, 2) + unit, f32),
        ]
        sems = []
        for dims in ((2, 4), (2, 2, SIDE), (2, 2, SIDE, 2), (2, 2), (2, 2, 2), (1,)):
            sems += [dma(dims), dma(dims)]
        return bufs, sems

    def copy(self, src, dst, stage, at, device):
        send, recv = self.sems[2 * stage], self.sems[2 * stage + 1]
        return remote(src, dst, send.at[at], recv.at[at], (device, self.z))

    def go(self, copy):
        copy.start()
        self.waits.append(copy)

    def spot(self, tau, di, j):
        if tau == 0:
            return side(self.y + di), j
        return j, side(self.x + di)

    def near(self, tau, axis, d):
        s = 1 - 2 * d
        if (tau == 0) == (axis == 0):
            return device_of(self.y + s, self.x, self.core)
        return device_of(self.y, self.x + s, self.core)

    def from_peer(self, tau, di):
        if tau == 0:
            at = (side(self.y + di), slice(None), 0)
        else:
            at = (slice(None), side(self.x + di), 1)
        return self.copy(
            self.slots.at[at], self.peer_slots.at[at], 0, (tau, di + 1), self.peer
        )

    def share(self):
        for di in (2, 1, -1, 0):
            for tau in (0, 1):

                @pl.loop(0, SIDE)
                def _(j):
                    yy, xx = self.spot(tau, di, j)
                    o = (yy * SIDE + xx) * 2 + tau
                    self.slots[yy, xx, tau] = self.packed[self.index[o], 1 - self.core]

                self.go(self.from_peer(tau, di))

    def term(self, tau, di, j, e):
        yy, xx = self.spot(tau, di, j)
        o = (yy * SIDE + xx) * 2 + tau
        times = self.packed.shape[-1] // self.entry.shape[1]
        mine = jnp.concatenate([self.entry[pl.ds(o, 1), :]] * times, axis=1)
        theirs = jnp.concatenate([self.peer_entry[pl.ds(o, 1), :]] * times, axis=1)
        a = self.packed[self.index[o], self.core].astype(jnp.float32)
        b = self.peer_slots[yy, xx, tau].astype(jnp.float32)
        return jnp.where(mine == e, a, 0.0) + jnp.where(theirs == e, b, 0.0)

    def first(self, tau, d, j):
        at = (tau, d, j)
        return self.copy(self.s1.at[at], self.r1.at[at], 1, at, self.near(tau, 0, d))

    def second(self, tau, d, j, e):
        at = (tau, d, j, e)
        return self.copy(self.s2.at[at], self.r2.at[at], 2, at, self.near(tau, 0, d))

    def third(self, tau, d):
        at = (tau, d)
        return self.copy(self.s3.at[at], self.r3.at[at], 3, at, self.near(tau, 1, d))

    def fourth(self, tau, d, e):
        at = (tau, d, e)
        return self.copy(self.s4.at[at], self.r4.at[at], 4, at, self.near(tau, 1, d))

    def send_first(self):
        for tau in (0, 1):
            self.from_peer(tau, 2).wait_recv()

            @pl.loop(0, SIDE)
            def _(j):
                for d in (0, 1):
                    self.s1[tau, d, j] = self.term(tau, 2, j, d).astype(self.s1.dtype)
                    self.first(tau, d, j).start()

    def send_second_free(self):
        for tau in (0, 1):
            for d in (0, 1):
                self.from_peer(tau, 1 - 2 * d).wait_recv()

            @pl.loop(0, SIDE)
            def _(j):
                for d in (0, 1):
                    value = self.term(tau, 1 - 2 * d, j, 1 - d)
                    self.s2[tau, d, j, 1 - d] = value.astype(self.s2.dtype)
                    self.second(tau, d, j, 1 - d).start()

    def send_second(self, tau):
        @pl.loop(0, SIDE)
        def _(j):
            for d in (0, 1):
                self.first(tau, d, j).wait_recv()
                value = self.term(tau, 1 - 2 * d, j, d) + self.r1[tau, d, j].astype(jnp.float32)
                self.s2[tau, d, j, d] = value.astype(self.s2.dtype)
                self.second(tau, d, j, d).start()

    def keep(self):
        for tau in (0, 1):
            self.from_peer(tau, 0).wait_recv()

            @pl.loop(0, SIDE)
            def _(j):
                for e in (0, 1):
                    self.acc[tau, j, e] = self.term(tau, 0, j, e)

    def total(self, tau, dj, e):
        j = side((self.x if tau == 0 else self.y) + dj)
        for d in (0, 1):
            self.second(tau, d, j, e).wait_recv()
        return (
            self.acc[tau, j, e]
            + self.r2[tau, 0, j, e].astype(jnp.float32)
            + self.r2[tau, 1, j, e].astype(jnp.float32)
        )

    def send_third(self):
        for tau in (0, 1):
            for d in (0, 1):
                self.s3[tau, d] = self.total(tau, 2, d).astype(self.s3.dtype)
                self.go(self.third(tau, d))

    def send_fourth_free(self):
        for tau in (0, 1):
            for d in (0, 1):
                value = self.total(tau, 1 - 2 * d, 1 - d)
                self.s4[tau, d, 1 - d] = value.astype(self.s4.dtype)
                self.go(self.fourth(tau, d, 1 - d))

    def send_fourth(self):
        for tau in (0, 1):
            for d in (0, 1):
                value = self.total(tau, 1 - 2 * d, d)
                self.third(tau, d).wait_recv()
                value += self.r3[tau, d].astype(jnp.float32)
                self.s4[tau, d, d] = value.astype(self.s4.dtype)
                self.go(self.fourth(tau, d, d))

    def finish(self):
        for tau in (0, 1):
            for e in (0, 1):
                value = self.total(tau, 0, e)
                for d in (0, 1):
                    self.fourth(tau, d, e).wait_recv()
                    value += self.r4[tau, d, e].astype(jnp.float32)
                self.res[tau, e] = value
        self.go(self.copy(
            self.res.at[1 - self.core], self.out.at[:, self.core], 5, 0, self.peer
        ))
        self.out[:, self.core] = self.res[self.core]

    def finished(self):
        self.copy(
            self.res.at[1 - self.core], self.out.at[:, 1 - self.core], 5, 0, self.peer
        ).wait_recv()

    def sent(self):
        for copy in self.waits:
            copy.wait_send()
        for tau in (0, 1):
            for d in (0, 1):

                @pl.loop(0, SIDE)
                def _(j):
                    self.first(tau, d, j).wait_send()
                    for e in (0, 1):
                        self.second(tau, d, j, e).wait_send()


class DirectReduce:
    def __init__(self, index, packed, entry, peer_entry, out, bufs, sems):
        self.me, self.core, self.y, self.x = place_in_plane()
        self.z = lax.axis_index("tsp")
        self.peer = self.me + 1 - 2 * self.core
        self.index, self.packed, self.entry, self.peer_entry = index, packed, entry, peer_entry
        self.out = out
        self.slots, self.peer_slots, self.terms, self.landed, self.res = bufs
        self.send_sem, self.recv_sem = sems
        self.waits = []

    @staticmethod
    def scratch(unit):
        bf16 = jnp.bfloat16
        dma = pltpu.SemaphoreType.DMA
        chips = SIDE * SIDE
        bufs = [
            pltpu.VMEM((chips, 2) + unit, bf16),
            pltpu.VMEM((chips, 2) + unit, bf16),
            pltpu.VMEM((chips, 2, 2) + unit, bf16),
            pltpu.VMEM((len(CHIPS), 2, 2) + unit, bf16),
            pltpu.VMEM((2, 2) + unit, jnp.float32),
        ]
        return bufs, [dma((len(CHIPS) + 2,)), dma((len(CHIPS) + 2,))]

    def copy(self, src, dst, device, k):
        return remote(src, dst, self.send_sem.at[k], self.recv_sem.at[k], (device, self.z))

    def go(self, copy):
        copy.start()
        self.waits.append(copy)

    def share(self):
        @pl.loop(0, SIDE * SIDE)
        def _(q):
            for tau in (0, 1):
                self.slots[q, tau] = self.packed[self.index[2 * q + tau], 1 - self.core]

        self.go(self.copy(self.slots, self.peer_slots, self.peer, len(CHIPS)))

    def term(self, q, tau, e):
        o = 2 * q + tau
        a = self.packed[self.index[o], self.core].astype(jnp.float32)
        b = self.peer_slots[q, tau].astype(jnp.float32)
        return jnp.where(self.entry[pl.ds(o, 1), :] == e, a, 0.0) + jnp.where(
            self.peer_entry[pl.ds(o, 1), :] == e, b, 0.0
        )

    def send_all(self):
        self.copy(self.slots, self.peer_slots, self.peer, len(CHIPS)).wait_recv()

        @pl.loop(0, SIDE * SIDE)
        def _(q):
            for tau in (0, 1):
                for e in (0, 1):
                    self.terms[q, tau, e] = self.term(q, tau, e).astype(self.terms.dtype)

        for k, (dy, dx) in enumerate(CHIPS):
            device = device_of(self.y + dy, self.x + dx, self.core)
            self.go(self.copy(
                self.terms.at[lax.div(device, 2)], self.landed.at[k], device, k
            ))

    def finish(self):
        for k in range(len(CHIPS)):
            self.copy(self.landed.at[k], self.landed.at[k], self.peer, k).wait_recv()
        for tau in (0, 1):
            for e in (0, 1):
                value = self.term(lax.div(self.me, 2), tau, e)
                for k in range(len(CHIPS)):
                    value += self.landed[k, tau, e].astype(jnp.float32)
                self.res[tau, e] = value
        self.go(self.copy(
            self.res.at[1 - self.core], self.out.at[:, self.core], self.peer, len(CHIPS) + 1
        ))
        self.out[:, self.core] = self.res[self.core]

    def finished(self):
        self.copy(
            self.res.at[1 - self.core], self.out.at[:, 1 - self.core], self.peer, len(CHIPS) + 1
        ).wait_recv()

    def sent(self):
        for copy in self.waits:
            copy.wait_send()


REDUCE_BUFS, REDUCE_SEMS, SUM_REFS = 12, 12, 6


def scatter_kernel(
    index, before, places, live, packed, entry, part, cotangent, beside, frozen, pulled, maps,
    out_down, out_up, out_tokens, *rest
):
    rest = list(rest)

    def take(n):
        taken = rest[:n]
        del rest[:n]
        return taken

    peer_entry, lowered, packed_up, beyond, weights, up_total = take(6)
    sum_refs = take(SUM_REFS)
    down_bufs, down_sems = take(REDUCE_BUFS), take(REDUCE_SEMS)
    up_bufs, up_sems = take(5), take(2)
    entry_send, entry_recv, cot_send, cot_recv = rest
    greet_neighbours()
    downs = PlaneReduce(index, packed, entry, peer_entry, out_down, down_bufs, down_sems)
    ups = DirectReduce(index, packed_up, entry, peer_entry, out_up, up_bufs, up_sems)
    sums = RingSum(part, lowered, *sum_refs)
    rows = cotangent.shape[0]
    cots = CotangentRing(
        lambda step, d: beside.at[2 + d] if step == 2 else beyond.at[d],
        lambda step, d: beyond.at[d if step == 2 else 2],
        cot_send, cot_recv, rows, (2, 3),
    )
    sums.begin()
    entries = remote(entry, peer_entry, entry_send, entry_recv, (downs.peer, downs.z))
    entries.start()
    cots.launch()
    downs.share()
    sums.step(1)
    cots.launch()
    entries.wait_recv()
    downs.send_first()
    sums.step(2)
    cots.launch()
    downs.send_second_free()
    sums.step(3)
    cots.launch()
    sums.total()
    cots.launch(2)
    downs.send_second(0)
    cots.launch(2)
    downs.send_second(1)
    z, keys = lax.axis_index("tsp"), cotangent.shape[1]
    for k, r in enumerate((0, -1, 1, -2, 2, -3, 3, 4)):
        first = pl.multiple_of(ring(z + r) * keys, keys)
        weights[:, k * keys : (k + 1) * keys] = frozen[:, pl.ds(first, keys)]
    downs.keep()
    sums.end()

    segments = before.shape[0]
    seg_rows, keys = rows // segments, cotangent.shape[1]
    ranks = 2 * HALF
    for g in range(segments):
        both = lowered[g // 2].reshape(seg_rows, 2 * ranks)
        value = lax.dot_general(
            both[:, (g % 2) * ranks : (g % 2 + 1) * ranks],
            cotangent[g * seg_rows : (g + 1) * seg_rows, :],
            (((0,), (0,)), ((), ())),
            preferred_element_type=jnp.float32,
        )
        up_total[g] = value

    @pl.loop(1, segments)
    def _(g):
        earlier = up_total[jnp.maximum(before[g], 0)]
        up_total[g] = up_total[g] + jnp.where(before[g] >= 0, earlier, 0.0)

    @pl.loop(0, segments)
    def _(g):
        scaled = (up_total[g] * (ADAPTER_SCALE / seg_rows)).astype(packed_up.dtype)
        packed_up[g] = scaled.reshape(packed_up.shape[1:])

    ups.share()
    downs.send_third()
    ups.send_all()
    cots.launch(4)
    downs.send_fourth_free()
    downs.send_fourth()
    cots.arrived()

    block, width = 2 * seg_rows, out_tokens.shape[1]
    row = lax.broadcasted_iota(jnp.int32, (seg_rows, width), 0)
    parts = [(beside, k) for k in range(4)] + [(beyond, k) for k in range(3)]

    def token_block(b):
        here = pl.ds(pl.multiple_of(b * block, block), block)
        left = jnp.concatenate(
            [cotangent[here, :]] + [ref[k, here, :] for ref, k in parts], axis=1
        )
        value = lax.dot_general(
            left, weights[...], (((1,), (1,)), ((), ())), preferred_element_type=jnp.float32
        )
        both = pulled[b].reshape(seg_rows, 2 * ranks)
        for k in (0, 1):
            g = 2 * b + k
            extra = jnp.dot(
                both[:, k * ranks : (k + 1) * ranks], maps[places[g]].reshape(ranks, width),
                preferred_element_type=jnp.float32,
            )
            total = value[k * seg_rows : (k + 1) * seg_rows] + ADAPTER_SCALE * extra
            rows_here = pl.ds(pl.multiple_of(g * seg_rows, seg_rows), seg_rows)
            out_tokens[rows_here, :] = jnp.where(row < live[g], total, 0.0).astype(
                out_tokens.dtype
            )

    pl.loop(0, 5)(token_block)
    downs.finish()
    ups.finish()
    pl.loop(5, segments // 2)(token_block)
    downs.finished()
    ups.finished()
    entries.wait_send()
    for each in (downs, ups, sums, cots):
        each.sent()


def scatter_gradients(
    index, before, places, live, packed, entry, part, cotangent, beside, frozen, pulled, maps
):
    down_unit = packed.shape[2:]
    up_unit = (HALF, cotangent.shape[1])
    bf16, f32 = jnp.bfloat16, jnp.float32
    dma = pltpu.SemaphoreType.DMA
    scalars = pl.BlockSpec(memory_space=pltpu.SMEM)
    whole = pl.BlockSpec(memory_space=pltpu.VMEM)
    anywhere = pl.BlockSpec(memory_space=pl.ANY)
    down_bufs, down_sems = PlaneReduce.scratch(down_unit)
    up_bufs, up_sems = DirectReduce.scratch(up_unit)
    return pl.pallas_call(
        scatter_kernel,
        out_shape=(
            jax.ShapeDtypeStruct((2, 2) + down_unit, f32),
            jax.ShapeDtypeStruct((2, 2) + up_unit, f32),
            jax.ShapeDtypeStruct((cotangent.shape[0], frozen.shape[0]), bf16),
        ),
        in_specs=[scalars] * 4 + [whole] * 8,
        out_specs=(whole, whole, whole),
        scratch_shapes=[
            pltpu.VMEM(entry.shape, f32),
            pltpu.VMEM(part.shape, bf16),
            pltpu.VMEM((packed.shape[0], 2) + up_unit, bf16),
            pltpu.VMEM((3,) + beside.shape[1:], bf16),
            pltpu.VMEM(frozen.shape, bf16),
            pltpu.VMEM((packed.shape[0], 2 * HALF, cotangent.shape[1]), f32),
        ]
        + ring_sum_scratch(part.shape)
        + down_bufs + down_sems + up_bufs + up_sems
        + [dma(()), dma(()), dma((2, 2, CotangentRing.eighths)), dma((2, 2, CotangentRing.eighths))],
        compiler_params=pltpu.CompilerParams(
            collective_id=1, has_side_effects=True, vmem_limit_bytes=30 * MIB
        ),
        name="scatter_gradients",
    )(index, before, places, live, packed, entry, part, cotangent, beside, frozen, pulled, maps)


def store_kernel(a, b, c, out_a, out_b, out_c, sems):
    pieces = 8
    copies = [
        pltpu.make_async_copy(b, out_b, sems.at[pieces]),
        pltpu.make_async_copy(c, out_c, sems.at[pieces + 1]),
    ]
    rows = a.shape[0] // pieces
    for k in range(pieces):
        here = pl.ds(k * rows, rows)
        copies.append(pltpu.make_async_copy(a.at[here], out_a.at[here], sems.at[k]))
    for copy in copies:
        copy.start()
    for copy in copies:
        copy.wait()


def store(*arrays):
    return pl.pallas_call(
        store_kernel,
        out_shape=tuple(jax.ShapeDtypeStruct(array.shape, array.dtype) for array in arrays),
        in_specs=[pl.BlockSpec(memory_space=pltpu.VMEM)] * 3,
        out_specs=(pl.BlockSpec(memory_space=pltpu.HBM),) * 3,
        scratch_shapes=[pltpu.SemaphoreType.DMA((10,))],
        compiler_params=pltpu.CompilerParams(vmem_limit_bytes=8 * MIB),
        name="store",
    )(*arrays)


def on_device(
    tokens,
    cotangent,
    frozen_key_weight,
    adapter_down_weight,
    adapter_up_weight,
    adapter_place_table,
    segment_adapter,
    segment_live_count,
):
    held, ranks, width = adapter_down_weight.shape
    keys = cotangent.shape[1]
    live = segment_live_count
    far = lambda array: pltpu.with_memory_space_constraint(array, pltpu.HBM)
    small = [far(adapter_place_table), far(segment_adapter), far(live)]
    maps, pulled, tokens_here, cotangent_here, beside = gather_maps(
        *small,
        far(adapter_down_weight.reshape(held, 2, HALF, width)),
        far(adapter_up_weight.reshape(held, 2, HALF, keys)),
        far(tokens), far(cotangent),
    )
    part, packed, places, before, index, entry = between(
        adapter_place_table, segment_adapter, live, tokens_here, maps, pulled
    )
    down_grad, up_grad, token_gradient = scatter_gradients(
        index, before, places, live, packed, entry, part, cotangent_here, beside,
        frozen_key_weight, pulled, maps,
    )
    token_gradient, down_grad, up_grad = store(
        token_gradient,
        down_grad.reshape(held, ranks, width),
        up_grad.reshape(held, ranks, keys),
    )
    return token_gradient, down_grad, up_grad


def solution(mesh):
    placed = (
        P("dp", "tsp"),
        P("dp", "tsp"),
        P("tsp", None),
        P("dp", None, "tsp"),
        P("dp", None, "tsp"),
        P(),
        P("dp"),
        P("dp"),
    )
    return jax.shard_map(
        on_device,
        mesh=mesh,
        in_specs=placed,
        out_specs=(P("dp", "tsp"), P("dp", None, "tsp"), P("dp", None, "tsp")),
        check_vma=False,
    )
```
